32 devices in a mesh: row: 16 (over z, y, x), tok: 2 (over core).
Axes of the slice: x: 2, y: 2, z: 4, core: 2. Of those that a mesh axis runs over, the one named last changes fastest.
Arguments:
- tokens: bfloat16 [16, 512, 768], P('row', 'tok'), may hold values from -6 to 6
- cotangent: bfloat16 [16, 512, 768], P('row', 'tok'), may hold values from -6 to 6
- segment_ids: int32 [16, 512], P('row', 'tok'), may hold values from 0 to 5, never falling along the last dimension, each value on 1 to 256 neighbouring positions
- valid: int32 [16, 512], P('row', 'tok'), may hold values from 0 to 1, as said below
- first_gain: float32 [2, 768], replicated, may hold values from 0.5 to 1.5
- first_shift: float32 [2, 768], replicated, may hold values from -2 to 2
- joint_weight: bfloat16 [2, 768, 2304], replicated, may hold values from -0.21875 to 0.21875
- joint_bias: float32 [2, 2, 768], replicated, may hold values from -2 to 2
- output_weight: bfloat16 [2, 768, 768], replicated, may hold values from -1.25 to 1.25
- output_bias: float32 [2, 768], replicated, may hold values from -2 to 2
- second_gain: float32 [2, 768], replicated, may hold values from 0.5 to 1.5
- second_shift: float32 [2, 768], replicated, may hold values from -2 to 2
- up_weight: bfloat16 [2, 768, 3072], replicated, may hold values from -0.21875 to 0.21875
- up_bias: float32 [2, 3072], replicated, may hold values from -2 to 2
- down_weight: bfloat16 [2, 3072, 768], replicated, may hold values from -0.109375 to 0.109375
- down_bias: float32 [2, 768], replicated, may hold values from -2 to 2
Outputs:
- output: bfloat16 [16, 512, 768], P('row', 'tok')
- input_gradient: float32 [16, 512, 768], P('row', 'tok')
- first_gain_gradient: float32 [2, 768], P(None, ('row', 'tok'))
- first_shift_gradient: float32 [2, 768], P(None, ('row', 'tok'))
- joint_weight_gradient: float32 [2, 768, 2304], P(None, ('row', 'tok'))
- joint_bias_gradient: float32 [2, 2, 768], P(None, None, ('row', 'tok'))
- output_weight_gradient: float32 [2, 768, 768], P(None, ('row', 'tok'))
- output_bias_gradient: float32 [2, 768], P(None, ('row', 'tok'))
- second_gain_gradient: float32 [2, 768], P(None, ('row', 'tok'))
- second_shift_gradient: float32 [2, 768], P(None, ('row', 'tok'))
- up_weight_gradient: float32 [2, 768, 3072], P(None, ('row', 'tok'))
- up_bias_gradient: float32 [2, 3072], P(None, ('row', 'tok'))
- down_weight_gradient: float32 [2, 3072, 768], P(None, ('row', 'tok'))
- down_bias_gradient: float32 [2, 768], P(None, ('row', 'tok'))
The draws below stay inside these ranges and needn't reach their ends.
Inputs may be any that keep to these rules, and one draw needn't show every extreme that they name: `valid`: in every row the ones come first and the zeros, at most 64 of them, fill its end.
All inputs are finite; a program needn't handle non-finite values.
Results may differ from the reference program's by a relative error of at most 0.014.
Values may be sent and summed in bfloat16 or wider, within the bound.
No kernel may reach another device: no remote copies, remote signals or barrier semaphores. Data moves between devices by JAX's collectives and lax.ppermute only.
A program may use at most 320 MiB of HBM per device.

```python
import math
import jax
import jax.numpy as jnp
import numpy as np
from jax import lax

D = 768
HEADS = 12
HDIM = 64
FF = 3072
LAYERS = 2
SEGS = 6
ROW_LEN = 512
ROWS = 16


def draw_valid(key, part):
    padding = jax.random.randint(key, (ROWS, 1), 0, ROW_LEN // 8 + 1)
    position = lax.broadcasted_iota(jnp.int32, (ROWS, ROW_LEN), 1)
    return (position < ROW_LEN - padding).astype(jnp.int32)


def with_spikes(values, stream_key, source, target, parts, factor):
    def block_of(dim):
        return (jnp.arange(values.shape[dim]) // (values.shape[dim] // parts)).reshape((-1,) + (1,) * (values.ndim - 1 - dim))

    near = jax.random.permutation(stream_key, parts)[block_of(target)]
    second = (block_of(target) + parts // 2) % parts
    return jnp.where((block_of(source) == near) | (block_of(source) == second), factor * values, values)


def level_of(stream_key, extent, split, low, high):
    loudness = 1.0
    for axis_at, parts in split:
        heights = jax.random.uniform(jax.random.fold_in(jax.random.fold_in(stream_key, 6), axis_at), (parts,), jnp.float32, low / len(split), high / len(split))
        loudness = loudness * jnp.repeat(jnp.exp(heights), extent[axis_at] // parts).reshape((-1,) + (1,) * (len(extent) - 1 - axis_at))
    return loudness


def length_profile(count, total, limit, lean):
    portions = [(1 << 20) // math.isqrt(grade ** lean) + 1 for grade in range(2, count + 1)]
    surplus, holding = total - limit - (count - 1), [1] * (count - 1)
    while surplus > 0:
        candidates = [i for i in range(count - 1) if holding[i] < limit]
        whole, remaining = sum([portions[i] for i in candidates]), surplus
        for i in candidates:
            more = min(limit - holding[i], max(1, remaining * portions[i] // whole), surplus)
            holding[i] = holding[i] + more
            surplus = surplus - more
    return np.array([limit] + holding)


def ragged(rng, count, total, reach, slope):
    if count == 2:
        one = jax.random.randint(rng, (), max(1, total - reach), min(reach, total - 1) + 1)
        return jnp.stack([one, total - one])
    sizes = jnp.asarray(length_profile(count, total, reach, slope), jnp.int32)
    pairs = (count - 1) // 2
    source_of, taker = sizes[1:1 + 2 * pairs:2], sizes[2:2 + 2 * pairs:2]
    slack = jnp.minimum(source_of - 1, reach - taker)
    shifted = jax.random.randint(jax.random.fold_in(rng, 1), (pairs,), 0, 1 << 20) % (slack + 1)
    sizes = sizes.at[1:1 + 2 * pairs:2].set(source_of - shifted).at[2:2 + 2 * pairs:2].set(taker + shifted)
    return sizes[jax.random.permutation(jax.random.fold_in(rng, 2), count)]


def centred(stream_key, extent, deviation, most, shards=(), kind=jnp.bfloat16):
    level = level_of(stream_key, extent, shards, -0.22, 0.18) if shards else 1.0
    entries = jax.random.normal(stream_key, extent, jnp.float32) * deviation * level
    return jnp.minimum(jnp.maximum(entries, -most), most).astype(kind)


def bell_draw_with(stream_key, shape, deviation, reach, cuts, heavy, dtype=jnp.bfloat16):
    entries = deviation * jax.random.normal(stream_key, shape, jnp.float32)
    if cuts:
        entries = entries * level_of(stream_key, shape, cuts, -0.22, 0.18)
    return jnp.clip(with_spikes(entries, jax.random.fold_in(stream_key, 3), *heavy), -reach, reach).astype(dtype)


def setup_inputs(seed: int = 0) -> dict:
    splits = jax.random.split(jax.random.key(seed), 17)
    tokens = centred(splits[0], (ROWS, ROW_LEN, D), 1.0, 6.0, ((0, 16), (1, 2)))
    cotangent = bell_draw_with(splits[1], (ROWS, ROW_LEN, D), 1.0, 6.0, ((0, 16), (1, 2)), (0, 2, 16, 2.0))
    segment_ids = jax.vmap(lambda own: jnp.searchsorted(jnp.cumsum(ragged(own, SEGS, ROW_LEN, ROW_LEN // 2, 0)), jnp.arange(ROW_LEN), side="right"))(jax.random.split(splits[2], ROWS)).reshape((ROWS, ROW_LEN)).astype(jnp.int32)
    valid = draw_valid(jax.random.fold_in(splits[16], 71), 0)
    first_gain = jnp.clip(1.0 + 0.1 * jax.random.normal(splits[4], (LAYERS, D), jnp.float32), 0.5, 1.5)
    first_shift = centred(splits[5], (LAYERS, D), 0.3, 2.0, (), jnp.float32)
    joint_weight = centred(splits[6], (LAYERS, D, 3 * D), D ** -0.5, 0.21875)
    joint_bias = centred(splits[7], (LAYERS, 2, D), 0.3, 2.0, (), jnp.float32)
    output_weight = centred(splits[8], (LAYERS, D, D), (D // 32) ** -0.5, 1.25)
    output_bias = centred(splits[9], (LAYERS, D), 0.3, 2.0, (), jnp.float32)
    second_gain = jnp.clip(1.0 + 0.1 * jax.random.normal(splits[10], (LAYERS, D), jnp.float32), 0.5, 1.5)
    second_shift = centred(splits[11], (LAYERS, D), 0.3, 2.0, (), jnp.float32)
    up_weight = centred(splits[12], (LAYERS, D, FF), D ** -0.5, 0.21875)
    up_bias = centred(splits[13], (LAYERS, FF), 0.3, 2.0, (), jnp.float32)
    down_weight = centred(splits[14], (LAYERS, FF, D), FF ** -0.5, 0.109375)
    down_bias = centred(splits[15], (LAYERS, D), 0.3, 2.0, (), jnp.float32)
    return dict(tokens=tokens, cotangent=cotangent, segment_ids=segment_ids, valid=valid, first_gain=first_gain, first_shift=first_shift, joint_weight=joint_weight, joint_bias=joint_bias, output_weight=output_weight, output_bias=output_bias, second_gain=second_gain, second_shift=second_shift, up_weight=up_weight, up_bias=up_bias, down_weight=down_weight, down_bias=down_bias)


@jax.custom_vjp
def low(v):
    return lax.optimization_barrier(v.astype(jnp.bfloat16)).astype(jnp.float32)

@jax.custom_vjp
def low_back(v):
    return v

def low_keep(v):
    return (low(v), None)

def low_pass(kept, grad):
    return (grad,)

def back_keep(v):
    return (v, None)

def back_low(kept, grad):
    return (low(grad),)
low.defvjp(low_keep, low_pass)
low_back.defvjp(back_keep, back_low)
epsilon = 1e-05
highest = lax.Precision.HIGHEST

def product(left, right):
    return jnp.dot(left, right, precision=highest, preferred_element_type=jnp.float32)

def normalize(stream, gain, shift):
    centre = stream - lax.optimization_barrier(jnp.mean(stream, axis=-1, keepdims=True))
    return centre * lax.rsqrt(lax.optimization_barrier(jnp.mean(centre * centre, axis=-1, keepdims=True)) + epsilon) * gain + shift

def block_layer(stream, allowed, weight_set):
    first_gain, first_shift, joint_weight, joint_bias, output_weight, output_bias, second_gain, second_shift, up_weight, up_bias, down_weight, down_bias = weight_set
    length = stream.shape[0]
    normed_one = low(normalize(stream, first_gain, first_shift))
    mixed = low_back(product(normed_one, joint_weight))
    queries = low(mixed[:, :D] + joint_bias[0]).reshape(length, HEADS, HDIM)
    key_rows = low(mixed[:, D:2 * D]).reshape(length, HEADS, HDIM)
    value_rows = low(mixed[:, 2 * D:] + joint_bias[1]).reshape(length, HEADS, HDIM)
    scores = low_back(jnp.einsum('qhd,khd->hqk', queries, key_rows, precision=highest) * 0.125)
    scores = jnp.where(allowed[None], scores, -1e+30)
    soft_low = low(jax.nn.softmax(scores, axis=-1))
    attended = jnp.einsum('hqk,khd->qhd', soft_low, value_rows, precision=highest).reshape(length, D)
    attended = low(low_back(attended))
    middle = stream + low_back(product(attended, output_weight)) + output_bias
    normed_two = low(normalize(middle, second_gain, second_shift))
    preact = low_back(product(normed_two, up_weight)) + up_bias
    hidden = low(jax.nn.gelu(preact, approximate=False))
    return middle + low_back(product(hidden, down_weight)) + down_bias

def reference(tokens, cotangent, segment_ids, valid, first_gain, first_shift, joint_weight, joint_bias, output_weight, output_bias, second_gain, second_shift, up_weight, up_bias, down_weight, down_bias):
    weight_set = tuple((member.astype(jnp.float32) for member in (first_gain, first_shift, joint_weight, joint_bias, output_weight, output_bias, second_gain, second_shift, up_weight, up_bias, down_weight, down_bias)))
    codes = segment_ids * 2 + valid

    def forward(stream_all, weights_all):

        def one_row(pieces):
            stream, code_row = pieces
            allowed = code_row[:, None] == code_row[None, :]
            for layer_index in range(LAYERS):
                stream = block_layer(stream, allowed, tuple((member[layer_index] for member in weights_all)))
            return stream
        return lax.map(jax.checkpoint(one_row), (stream_all, codes))
    result, pull = jax.vjp(forward, tokens.astype(jnp.float32), weight_set)
    input_gradient, grads = pull(cotangent.astype(jnp.float32))
    return (result.astype(jnp.bfloat16), input_gradient, grads[0], grads[1], grads[2], grads[3], grads[4], grads[5], grads[6], grads[7], grads[8], grads[9], grads[10], grads[11])
```

```python
import jax
import jax.numpy as jnp
from jax import lax
from jax.sharding import PartitionSpec as P

epsilon = 1e-05
score_scale = 0.125
masked_score = -1e30


def normalize(stream):
    centre = stream - jnp.mean(stream, axis=-1, keepdims=True)
    inverse = lax.rsqrt(jnp.mean(centre * centre, axis=-1, keepdims=True) + epsilon)
    return (centre * inverse, inverse)


def norm_back(upstream, unit, inverse, gain):
    scaled = upstream * gain
    return inverse * (
        scaled
        - jnp.mean(scaled, axis=-1, keepdims=True)
        - unit * jnp.mean(scaled * unit, axis=-1, keepdims=True)
    )


def gelu_exact(preact):
    return jax.nn.gelu(preact, approximate=False)


def left_product(left, right):
    return jnp.einsum("ti,tj->ij", left, right, preferred_element_type=jnp.float32)


def right_product(left, right):
    return jnp.einsum("tj,ij->ti", left, right, preferred_element_type=jnp.float32)


def swap_cores(array):
    return lax.ppermute(array, "tok", [(0, 1), (1, 0)])


def pair_rows(array, core):
    other = swap_cores(array)
    first = jnp.where(core == 0, array, other)
    second = jnp.where(core == 0, other, array)
    return jnp.concatenate([first, second], axis=0)


def halve(parts, bit, chips, me):
    array, bits = parts
    axis = bits.index(bit)
    mine = (me >> bit) & 1
    sent = lax.dynamic_index_in_dim(array, 1 - mine, axis, keepdims=False)
    kept = lax.dynamic_index_in_dim(array, mine, axis, keepdims=False)
    pairs = [(chip, chip ^ (1 << bit)) for chip in range(chips)]
    received = lax.ppermute(sent, "row", pairs)
    summed = kept.astype(jnp.float32) + received.astype(jnp.float32)
    return (summed, bits[:axis] + bits[axis + 1 :])


def chip_sum(array, order, chips, me):
    bits = tuple(reversed(range(chips.bit_length() - 1)))
    kind = array.dtype
    parts = (array.reshape((2,) * len(bits) + array.shape[1:]), bits)
    for bit in order:
        parts = halve((parts[0].astype(kind), parts[1]), bit, chips, me)
    return parts[0]


def body(
    tokens,
    cotangent,
    segment_ids,
    valid,
    first_gain,
    first_shift,
    joint_weight,
    joint_bias,
    output_weight,
    output_bias,
    second_gain,
    second_shift,
    up_weight,
    up_bias,
    down_weight,
    down_bias,
    chips,
):
    layers, width = joint_weight.shape[:2]
    heads = width // 64
    rows = tokens.shape[1]
    core = lax.axis_index("tok")
    me = lax.axis_index("row")
    count = chips.bit_length() - 1
    rest = tuple(range(2, count))
    by_x = (0, 1) + rest
    by_y = (1, 0) + rest
    by_z = (2, 0, 1) + tuple(range(3, count))

    code_local = segment_ids[0] * 2 + valid[0]
    code_all = pair_rows(code_local, core)
    allowed = (code_local[:, None] == code_all[None, :])[None]

    def split_heads(array):
        return array.reshape(array.shape[0], heads, -1)

    def weight_sum(left, right, order):
        half = right.shape[1] // 2
        sent = lax.dynamic_slice_in_dim(right, (1 - core) * half, half, axis=1)
        kept = lax.dynamic_slice_in_dim(right, core * half, half, axis=1)
        left_all = jnp.concatenate([left, swap_cores(left)], axis=0)
        right_all = jnp.concatenate([kept, swap_cores(sent)], axis=0)
        product = left_product(left_all, right_all).astype(jnp.bfloat16)
        product = product.reshape(chips, -1, half)
        total = chip_sum(product, order, chips, me)
        total = total.reshape(2, -1, half)
        sent = lax.dynamic_index_in_dim(total, 1 - core, 0, keepdims=False)
        kept = lax.dynamic_index_in_dim(total, core, 0, keepdims=False)
        other = swap_cores(sent)
        return jnp.where(
            core == 0,
            jnp.concatenate([kept, other], axis=1),
            jnp.concatenate([other, kept], axis=1),
        )

    stream = tokens[0].astype(jnp.float32)
    saved = []
    for layer in range(layers):
        unit_one, inverse_one = normalize(stream)
        normed_one = (unit_one * first_gain[layer] + first_shift[layer]).astype(jnp.bfloat16)
        mixed = jnp.dot(normed_one, joint_weight[layer], preferred_element_type=jnp.float32)
        queries = (mixed[:, :width] + joint_bias[layer, 0]).astype(jnp.bfloat16)
        key_rows = mixed[:, width : 2 * width].astype(jnp.bfloat16)
        value_rows = (mixed[:, 2 * width :] + joint_bias[layer, 1]).astype(jnp.bfloat16)
        both = pair_rows(jnp.concatenate([key_rows, value_rows], axis=1), core)
        queries = split_heads(queries)
        key_all = split_heads(both[:, :width])
        value_all = split_heads(both[:, width:])
        scores = (
            jnp.einsum("qhd,khd->hqk", queries, key_all, preferred_element_type=jnp.float32)
            * score_scale
        )
        scores = jnp.where(allowed, scores, masked_score)
        exponent = jnp.exp(scores - jnp.max(scores, axis=-1, keepdims=True))
        soft = exponent / jnp.sum(exponent, axis=-1, keepdims=True)
        soft_low = soft.astype(jnp.bfloat16)
        attended = jnp.einsum(
            "hqk,khd->qhd", soft_low, value_all, preferred_element_type=jnp.float32
        )
        attended = attended.reshape(rows, width).astype(jnp.bfloat16)
        middle = (
            stream
            + jnp.dot(attended, output_weight[layer], preferred_element_type=jnp.float32)
            + output_bias[layer]
        )
        unit_two, inverse_two = normalize(middle)
        normed_two = (unit_two * second_gain[layer] + second_shift[layer]).astype(jnp.bfloat16)
        preact = (
            jnp.dot(normed_two, up_weight[layer], preferred_element_type=jnp.float32)
            + up_bias[layer]
        )
        hidden = gelu_exact(preact).astype(jnp.bfloat16)
        stream = (
            middle
            + jnp.dot(hidden, down_weight[layer], preferred_element_type=jnp.float32)
            + down_bias[layer]
        )
        saved.append(
            (unit_one, inverse_one, normed_one, queries, key_all, value_all, soft, attended)
            + (unit_two, inverse_two, normed_two, preact, hidden)
        )
    output = stream.astype(jnp.bfloat16)[None]
    upstream = cotangent[0].astype(jnp.float32)
    small = [None] * layers
    large = [None] * layers
    for layer in reversed(range(layers)):
        (unit_one, inverse_one, normed_one, queries, key_all, value_all, soft, attended) = saved[
            layer
        ][:8]
        unit_two, inverse_two, normed_two, preact, hidden = saved[layer][8:]
        turn = (layers - 1 - layer) % 2
        up_low = upstream.astype(jnp.bfloat16)
        down_bias_grad = jnp.sum(upstream, axis=0)
        down_weight_grad = weight_sum(hidden, up_low, by_y if turn else by_x)
        hidden_grad = right_product(up_low, down_weight[layer])
        preact_grad = jax.vjp(gelu_exact, preact)[1](hidden_grad)[0]
        up_bias_grad = jnp.sum(preact_grad, axis=0)
        preact_low = preact_grad.astype(jnp.bfloat16)
        up_weight_grad = weight_sum(normed_two, preact_low, by_x if turn else by_y)
        normed_two_grad = right_product(preact_low, up_weight[layer])
        second_gain_grad = jnp.sum(normed_two_grad * unit_two, axis=0)
        second_shift_grad = jnp.sum(normed_two_grad, axis=0)
        middle_grad = upstream + norm_back(
            normed_two_grad, unit_two, inverse_two, second_gain[layer]
        )
        middle_low = middle_grad.astype(jnp.bfloat16)
        output_bias_grad = jnp.sum(middle_grad, axis=0)
        output_weight_grad = weight_sum(attended, middle_low, by_z)
        attended_grad = split_heads(
            right_product(middle_low, output_weight[layer]).astype(jnp.bfloat16)
        )
        soft_low = soft.astype(jnp.bfloat16)
        soft_grad = jnp.einsum(
            "qhd,khd->hqk", attended_grad, value_all, preferred_element_type=jnp.float32
        )
        delta = jnp.sum(soft_grad * soft, axis=-1, keepdims=True)
        score_grad = (soft * (soft_grad - delta)).astype(jnp.bfloat16)
        query_grad = (
            jnp.einsum("hqk,khd->qhd", score_grad, key_all, preferred_element_type=jnp.float32)
            * score_scale
        ).reshape(rows, width)
        key_grad = (
            jnp.einsum("hqk,qhd->khd", score_grad, queries, preferred_element_type=jnp.float32)
            * score_scale
        )
        value_grad = jnp.einsum(
            "hqk,qhd->khd", soft_low, attended_grad, preferred_element_type=jnp.float32
        )
        both = jnp.concatenate(
            [key_grad.reshape(2 * rows, width), value_grad.reshape(2 * rows, width)], axis=1
        )
        both = both.reshape(2, rows, 2 * width)
        sent = lax.dynamic_index_in_dim(both, 1 - core, 0, keepdims=False)
        kept = lax.dynamic_index_in_dim(both, core, 0, keepdims=False)
        both = kept + swap_cores(sent.astype(jnp.bfloat16)).astype(jnp.float32)
        joint_bias_grad = jnp.stack(
            [jnp.sum(query_grad, axis=0), jnp.sum(both[:, width:], axis=0)]
        )
        mixed_low = jnp.concatenate([query_grad, both], axis=1).astype(jnp.bfloat16)
        joint_weight_grad = weight_sum(normed_one, mixed_low, by_z)
        normed_one_grad = right_product(mixed_low, joint_weight[layer])
        first_gain_grad = jnp.sum(normed_one_grad * unit_one, axis=0)
        first_shift_grad = jnp.sum(normed_one_grad, axis=0)
        upstream = middle_grad + norm_back(
            normed_one_grad, unit_one, inverse_one, first_gain[layer]
        )
        small[layer] = (
            first_gain_grad,
            first_shift_grad,
            joint_bias_grad[0],
            joint_bias_grad[1],
            output_bias_grad,
            second_gain_grad,
            second_shift_grad,
            down_bias_grad,
            up_bias_grad,
        )
        large[layer] = (joint_weight_grad, output_weight_grad, up_weight_grad, down_weight_grad)

    pieces = [vector.reshape(chips, 2, -1) for layer in range(layers) for vector in small[layer]]
    packed = jnp.concatenate(pieces, axis=2)
    sent = lax.dynamic_index_in_dim(packed, 1 - core, 1, keepdims=False)
    kept = lax.dynamic_index_in_dim(packed, core, 1, keepdims=False)
    packed = chip_sum(kept + swap_cores(sent), by_x, chips, me)
    vectors, at = [], 0
    for piece in pieces:
        vectors.append(packed[at : at + piece.shape[2]])
        at += piece.shape[2]
    per = len(small[0])

    def stacked(position):
        return jnp.stack([vectors[layer * per + position] for layer in range(layers)])

    def matrix(position):
        return jnp.stack([large[layer][position] for layer in range(layers)])

    return (
        output,
        upstream[None],
        stacked(0),
        stacked(1),
        matrix(0),
        jnp.stack([stacked(2), stacked(3)], axis=1),
        matrix(1),
        stacked(4),
        stacked(5),
        stacked(6),
        matrix(2),
        stacked(8),
        matrix(3),
        stacked(7),
    )


def solution(mesh):
    chips = mesh.shape["row"]
    split = P("row", "tok", None)
    in_specs = (split, split, P("row", "tok"), P("row", "tok")) + (P(),) * 12
    vector = P(None, ("row", "tok"))
    table = P(None, ("row", "tok"), None)
    out_specs = (
        split,
        split,
        vector,
        vector,
        table,
        P(None, None, ("row", "tok")),
        table,
        vector,
        vector,
        vector,
        table,
        vector,
        table,
        vector,
    )

    def run(*arrays):
        return body(*arrays, chips=chips)

    return jax.shard_map(run, mesh=mesh, in_specs=in_specs, out_specs=out_specs, check_vma=False)
```

```python
import functools
import math

import jax
import jax.numpy as jnp
from jax import lax
from jax.experimental import pallas as pl
from jax.experimental.pallas import tpu as pltpu
from jax.sharding import PartitionSpec as P

epsilon = 1e-05
score_scale = 0.125
masked_score = -1e30
head_size = 64
lanes = 128
f32 = jnp.float32
bf16 = jnp.bfloat16
VMEM = pl.BlockSpec(memory_space=pltpu.VMEM)
SMEM = pl.BlockSpec(memory_space=pltpu.SMEM)
HBM = pl.BlockSpec(memory_space=pltpu.HBM)


def shape(dims, kind):
    return jax.ShapeDtypeStruct(dims, kind)


def dot(left, right):
    return jnp.dot(left, right, preferred_element_type=f32)


def dot_nt(left, right):
    return lax.dot_general(left, right, (((1,), (1,)), ((), ())), preferred_element_type=f32)


def dot_tn(left, right):
    return lax.dot_general(left, right, (((0,), (0,)), ((), ())), preferred_element_type=f32)


def normalize(stream):
    centre = stream - jnp.mean(stream, axis=-1, keepdims=True)
    inverse = lax.rsqrt(jnp.mean(centre * centre, axis=-1, keepdims=True) + epsilon)
    return centre * inverse, inverse


def norm_back(upstream, unit, inverse, gain):
    scaled = upstream * gain
    return inverse * (
        scaled
        - jnp.mean(scaled, axis=-1, keepdims=True)
        - unit * jnp.mean(scaled * unit, axis=-1, keepdims=True)
    )


def column_sum(array):
    return jnp.sum(array, axis=0, keepdims=True)


def gelu_and_slope(x):
    size = jnp.abs(x)
    t = 1.0 / (1.0 + (0.3275911 * 0.7071067811865476) * size)
    bell = jnp.exp(-0.5 * (x * x))
    series = t * (
        0.5 * 0.254829592
        + t
        * (
            0.5 * -0.284496736
            + t * (0.5 * 1.421413741 + t * (0.5 * -1.453152027 + t * (0.5 * 1.061405429)))
        )
    )
    tail = series * bell
    share = jnp.where(x >= 0, 1.0 - tail, tail)
    return x * share, share + x * (bell * 0.3989422804014327)


class Copies:
    def __init__(self, sems):
        self.sems = sems
        self.used = 0
        self.out = []

    def bring(self, source, target):
        copy = pltpu.make_async_copy(source, target, self.sems.at[self.used])
        self.used += 1
        copy.start()
        return copy

    def send(self, source, target):
        self.out.append(self.bring(source, target))

    def finish(self):
        for copy in self.out:
            copy.wait()


def emit_project(stream, layer, gain, shift, bias, weight, normed_ref, query_ref, kv_ref):
    width = stream.shape[1]
    unit, _ = normalize(stream)
    normed_ref[...] = (unit * gain[layer : layer + 1] + shift[layer : layer + 1]).astype(bf16)
    normed = normed_ref[...]
    kv_ref[:, :width] = dot(normed, weight[:, width : 2 * width]).astype(bf16)
    kv_ref[:, width:] = (
        dot(normed, weight[:, 2 * width :]) + bias[2 * layer + 1 : 2 * layer + 2]
    ).astype(bf16)
    queries = (dot(normed, weight[:, :width]) + bias[2 * layer : 2 * layer + 1]).astype(bf16)
    query_ref[...] = queries * jnp.asarray(score_scale, bf16)


def head_masks():
    lane = lax.broadcasted_iota(jnp.int32, (1, lanes), 1)
    return (lane < head_size, lane >= head_size)


def emit_mask(rows, code_ref, far_ref, mask_ref):
    own = code_ref[...].astype(f32)
    diagonal = lax.broadcasted_iota(jnp.int32, (rows, rows), 0) == lax.broadcasted_iota(
        jnp.int32, (rows, rows), 1
    )
    column = jnp.sum(jnp.where(diagonal, own, 0.0), axis=1, keepdims=True)
    mask_ref[:, :rows] = jnp.where(column == own, 0.0, masked_score)
    mask_ref[:, rows:] = jnp.where(column == far_ref[...].astype(f32), 0.0, masked_score)


def emit_attention(width, query_ref, kv_ref, mask_ref, attended_ref, soft_ref):
    rows = query_ref.shape[0]
    masks = head_masks()
    zero = jnp.zeros((), bf16)

    def one_pair(pair, carry):
        at = pl.multiple_of(pair * lanes, lanes)
        columns = pl.ds(at, lanes)
        queries = query_ref[:, columns]
        keys = kv_ref[:, columns]
        values = kv_ref[:, pl.ds(pl.multiple_of(at + width, lanes), lanes)]
        total = jnp.zeros((rows, lanes), f32)
        for side in range(2):
            own = jnp.where(masks[side], queries, zero)
            scores = dot_nt(own, keys) + mask_ref[...]
            exponent = jnp.exp(scores - jnp.max(scores, axis=-1, keepdims=True))
            soft = exponent * (1.0 / jnp.sum(exponent, axis=-1, keepdims=True))
            soft_low = soft.astype(bf16)
            soft_ref[pair * 2 + side] = soft_low
            total += dot(soft_low, jnp.where(masks[side], values, zero))
        attended_ref[:, columns] = total.astype(bf16)
        return carry

    lax.fori_loop(0, width // lanes, one_pair, 0, unroll=2)


def emit_attention_back(
    width, query_ref, kv_ref, soft_ref, wait_soft, grad_ref, dq_ref, dq_sum, own_ref, sent_ref
):
    rows = query_ref.shape[0]
    masks = head_masks()
    zero = jnp.zeros((), bf16)

    def one_pair(pair, carry):
        wait_soft(pair)
        at = pl.multiple_of(pair * lanes, lanes)
        columns = pl.ds(at, lanes)
        value_columns = pl.ds(pl.multiple_of(at + width, lanes), lanes)
        queries = query_ref[:, columns]
        grads = grad_ref[:, columns]
        keys = kv_ref[:, columns]
        values = kv_ref[:, value_columns]
        dq = jnp.zeros((rows, lanes), f32)
        dk = jnp.zeros((2 * rows, lanes), f32)
        dv = jnp.zeros((2 * rows, lanes), f32)
        for side in range(2):
            soft_low = soft_ref[pair * 2 + side]
            soft = soft_low.astype(f32)
            own = jnp.where(masks[side], grads, zero)
            soft_grad = dot_nt(own, values)
            delta = jnp.sum(soft_grad * soft, axis=-1, keepdims=True)
            score_grad = (soft * (soft_grad - delta)).astype(bf16)
            dq += dot(score_grad, jnp.where(masks[side], keys, zero))
            dk += dot_tn(score_grad, jnp.where(masks[side], queries, zero))
            dv += dot_tn(soft_low, own)
        dq = dq * score_scale
        dq_ref[:, columns] = dq.astype(bf16)
        dq_sum[0:1, columns] = column_sum(dq)
        own_ref[:, columns] = dk[:rows]
        own_ref[:, value_columns] = dv[:rows]
        sent_ref[:, columns] = dk[rows:].astype(bf16)
        sent_ref[:, value_columns] = dv[rows:].astype(bf16)
        return carry

    lax.fori_loop(0, width // lanes, one_pair, 0, unroll=2)


def project_kernel(
    meta, gain, shift, bias, tokens_hbm, weight_hbm, grad_hbm,
    normed_hbm, query_hbm, kv_hbm, kept_hbm, sent_hbm,
    tokens, weight, grad, normed, query, kv, sems,
):
    copies = Copies(sems)
    width = tokens.shape[1]
    half = width // 2
    first = copies.bring(tokens_hbm, tokens)
    second = copies.bring(weight_hbm.at[0], weight)
    third = copies.bring(grad_hbm, grad)
    first.wait()
    second.wait()
    emit_project(tokens[...].astype(f32), 0, gain, shift, bias, weight, normed, query, kv)
    copies.send(kv, kv_hbm)
    copies.send(query, query_hbm)
    copies.send(normed, normed_hbm)
    third.wait()
    core = meta[0]
    copies.send(grad.at[:, pl.ds(pl.multiple_of(core * half, half), half)], kept_hbm)
    copies.send(grad.at[:, pl.ds(pl.multiple_of((1 - core) * half, half), half)], sent_hbm)
    copies.finish()


def middle_kernel(layer, last, *refs):
    code, code_far, output_bias, gain, shift, up_bias = refs[:6]
    if last:
        stream_hbm, query_hbm, kv_hbm, far_hbm, output_hbm, up_hbm = refs[6:12]
        acts_hbm, soft_hbm, middle_hbm, slope_hbm = refs[12:16]
        refs = refs[16:]
    else:
        down_bias, next_gain, next_shift, joint_bias = refs[6:10]
        stream_hbm, query_hbm, kv_hbm, far_hbm, output_hbm, up_hbm, down_hbm, joint_hbm = refs[10:18]
        acts_hbm, soft_hbm, middle_hbm, slope_hbm, stream_next_hbm = refs[18:23]
        normed_next_hbm, query_next_hbm, kv_next_hbm = refs[23:26]
        refs = refs[26:]
    stream_ref, query, kv, mask, acts, soft, middle_ref, slope, output_weight, up_weight = refs[:10]
    copies = Copies(refs[-1])
    rows, width = query.shape
    inner = up_weight.shape[1]
    wait = [
        copies.bring(query_hbm, query),
        copies.bring(kv_hbm, kv.at[pl.ds(0, rows)]),
        copies.bring(far_hbm, kv.at[pl.ds(rows, rows)]),
        copies.bring(stream_hbm, stream_ref),
    ]
    emit_mask(rows, code, code_far, mask)
    for copy in wait[:3]:
        copy.wait()
    output_copy = copies.bring(output_hbm.at[layer], output_weight)
    up_copy = copies.bring(up_hbm.at[layer], up_weight)
    if not last:
        down_weight, joint_weight, total, normed, query_next, kv_next = refs[10:16]
        down_copy = copies.bring(down_hbm.at[layer], down_weight)
        joint_copy = copies.bring(joint_hbm.at[layer + 1], joint_weight)
    emit_attention(width, query, kv, mask, acts, soft)
    copies.send(soft, soft_hbm)
    wait[3].wait()
    output_copy.wait()
    middle = (
        stream_ref[...].astype(f32)
        + dot(acts[:, :width], output_weight[...])
        + output_bias[layer : layer + 1]
    )
    middle_ref[...] = middle
    copies.send(middle_ref, middle_hbm)
    unit, _ = normalize(middle)
    acts[:, width : 2 * width] = (
        unit * gain[layer : layer + 1] + shift[layer : layer + 1]
    ).astype(bf16)
    up_copy.wait()
    if not last:
        down_copy.wait()
        total[...] = middle + down_bias[layer : layer + 1]
    chunk = width

    def one_chunk(index, carry):
        at = pl.multiple_of(index * chunk, chunk)
        columns = pl.ds(at, chunk)
        preact = dot(acts[:, width : 2 * width], up_weight[:, columns])
        hidden, rate = gelu_and_slope(preact + up_bias[layer : layer + 1, columns])
        hidden = hidden.astype(bf16)
        slope[:, columns] = rate.astype(bf16)
        acts[:, pl.ds(pl.multiple_of(2 * width + at, lanes), chunk)] = hidden
        if not last:
            total[...] += dot(hidden, down_weight[columns, :])
        return carry

    lax.fori_loop(0, inner // chunk, one_chunk, 0)
    copies.send(acts, acts_hbm)
    copies.send(slope, slope_hbm)
    if not last:
        copies.send(total, stream_next_hbm)
        joint_copy.wait()
        emit_project(
            total[...],
            layer + 1,
            next_gain,
            next_shift,
            joint_bias,
            joint_weight,
            normed,
            query_next,
            kv_next,
        )
        copies.send(kv_next, kv_next_hbm)
        copies.send(query_next, query_next_hbm)
        copies.send(normed, normed_next_hbm)
    copies.finish()


def mlp_back_kernel(layer, first, *refs):
    meta, gain = refs[:2]
    if first:
        down_bias, acts_hbm = refs[2:4]
        refs = refs[4:]
    else:
        refs = refs[2:]
    upstream_hbm, slope_hbm, middle_hbm, down_hbm, up_hbm = refs[:5]
    kept_hbm, sent_hbm, low_hbm, grad_hbm, vectors, up_sum = refs[5:11]
    refs = refs[11:]
    if first:
        output_hbm, hidden, output = refs[0], refs[1], refs[2]
        refs = refs[3:]
    upstream_ref, slope, middle_ref, kept, sent, low, grad_ref, total = refs[:8]
    down_weight, up_weight, sems = refs[8:]
    copies = Copies(sems)
    rows, width = upstream_ref.shape
    inner = up_weight.shape[1]
    if first:
        hidden_copy = copies.bring(acts_hbm.at[:, pl.ds(2 * width, inner)], hidden)
    upstream_copy = copies.bring(upstream_hbm, upstream_ref)
    down_copy = copies.bring(down_hbm.at[layer], down_weight)
    middle_copy = copies.bring(middle_hbm, middle_ref)
    slope_copy = copies.bring(slope_hbm, slope)
    up_copy = copies.bring(up_hbm.at[layer], up_weight)
    core = meta[0]
    chunk = width
    half = inner // 2 // chunk
    upstream_copy.wait()
    upstream = upstream_ref[...].astype(f32)
    low[...] = upstream.astype(bf16)
    vectors[0:4] = jnp.zeros_like(vectors[0:4])
    vectors[7:8] = column_sum(upstream)
    up_sum[...] = jnp.zeros_like(up_sum)
    down_copy.wait()
    middle_copy.wait()
    if first:
        hidden_copy.wait()
        result = middle_ref[...] + down_bias[layer : layer + 1]
        output[...] = (result + dot(hidden[...], down_weight[...])).astype(bf16)
        copies.send(output, output_hbm)
    slope_copy.wait()
    up_copy.wait()
    total[...] = jnp.zeros_like(total)

    def one_chunk(index, carry, target, side):
        at = pl.multiple_of(side * (inner // 2) + index * chunk, chunk)
        columns = pl.ds(at, chunk)
        hidden_grad = dot_nt(low[...], down_weight[columns, :])
        preact_grad = hidden_grad * slope[:, columns].astype(f32)
        up_sum[0:1, columns] = column_sum(preact_grad)
        preact_low = preact_grad.astype(bf16)
        target[:, pl.ds(pl.multiple_of(index * chunk, chunk), chunk)] = preact_low
        total[...] += dot_nt(preact_low, up_weight[:, columns])
        return carry

    lax.fori_loop(0, half, functools.partial(one_chunk, target=sent, side=1 - core), 0)
    copies.send(sent, sent_hbm)
    lax.fori_loop(0, half, functools.partial(one_chunk, target=kept, side=core), 0)
    copies.send(kept, kept_hbm)
    unit, inverse = normalize(middle_ref[...])
    normed_grad = total[...]
    vectors[5:6] = column_sum(normed_grad * unit)
    vectors[6:7] = column_sum(normed_grad)
    middle_grad = upstream_ref[...].astype(f32) + norm_back(
        normed_grad, unit, inverse, gain[layer : layer + 1]
    )
    vectors[4:5] = column_sum(middle_grad)
    grad_ref[...] = middle_grad
    low[...] = middle_grad.astype(bf16)
    copies.send(low, low_hbm)
    copies.send(grad_ref, grad_hbm)
    copies.finish()


def attention_back_kernel(
    layer, low_hbm, query_hbm, kv_hbm, far_hbm, soft_hbm, output_hbm,
    dq_hbm, own_hbm, sent_hbm, dq_sum,
    low, query, kv, soft, attended_grad, output_weight, dq, own, sent, soft_sems, sems,
):
    copies = Copies(sems)
    rows, width = low.shape
    wait = [
        copies.bring(low_hbm, low),
        copies.bring(output_hbm.at[layer], output_weight),
        copies.bring(query_hbm, query),
        copies.bring(kv_hbm, kv.at[pl.ds(0, rows)]),
        copies.bring(far_hbm, kv.at[pl.ds(rows, rows)]),
    ]

    def soft_copy(pair):
        two = pl.ds(pair * 2, 2)
        return pltpu.make_async_copy(soft_hbm.at[two], soft.at[two], soft_sems.at[pair])

    for pair in range(width // lanes):
        soft_copy(pair).start()
    dq_sum[...] = jnp.zeros_like(dq_sum)
    wait[0].wait()
    wait[1].wait()
    attended_grad[...] = dot_nt(low[...], output_weight[...]).astype(bf16)
    for copy in wait[2:]:
        copy.wait()
    emit_attention_back(
        width,
        query,
        kv,
        soft,
        lambda pair: soft_copy(pair).wait(),
        attended_grad,
        dq,
        dq_sum,
        own,
        sent,
    )
    copies.send(sent, sent_hbm)
    copies.send(dq, dq_hbm)
    copies.send(own, own_hbm)
    copies.finish()


def project_back_kernel(layer, split, *refs):
    meta, gain, dq_sum, vectors_two = refs[:4]
    dq_hbm, own_hbm, received_hbm, stream_hbm, low_hbm, grad_hbm, joint_hbm = refs[4:11]
    kept_hbm, sent_hbm, upstream_hbm, vectors = refs[11:15]
    refs = refs[15:]
    if split:
        up_kept_hbm, up_sent_hbm = refs[:2]
        refs = refs[2:]
    own, received, stream_ref, low, below_low, grad_ref, mixed, upstream, joint_weight, sems = refs
    copies = Copies(sems)
    rows, width = low.shape
    core = meta[0]
    wide = 3 * width // 2
    half = width // 2
    wait = [
        copies.bring(dq_hbm, mixed.at[:, pl.ds(0, width)]),
        copies.bring(own_hbm, own),
        copies.bring(received_hbm, received),
        copies.bring(low_hbm, low),
        copies.bring(joint_hbm.at[layer], joint_weight),
        copies.bring(stream_hbm, stream_ref),
        copies.bring(grad_hbm, grad_ref),
    ]
    vectors[4:8] = vectors_two[4:8]
    vectors[2:3] = dq_sum[0:1]
    for copy in wait[:4]:
        copy.wait()
    kv_grad = own[...] + received[...].astype(f32)
    mixed[:, width:] = kv_grad.astype(bf16)
    vectors[3:4] = column_sum(kv_grad[:, width:])
    for side, target in ((1 - core, sent_hbm), (core, kept_hbm)):
        copies.send(
            mixed.at[:, pl.ds(pl.multiple_of(side * wide, lanes), wide)],
            target.at[:, pl.ds(0, wide)],
        )
        copies.send(
            low.at[:, pl.ds(pl.multiple_of(side * half, lanes), half)],
            target.at[:, pl.ds(wide, half)],
        )
    wait[4].wait()
    wait[5].wait()
    normed_grad = dot_nt(mixed[...], joint_weight[...])
    unit, inverse = normalize(stream_ref[...].astype(f32))
    vectors[0:1] = column_sum(normed_grad * unit)
    vectors[1:2] = column_sum(normed_grad)
    wait[6].wait()
    below = grad_ref[...] + norm_back(normed_grad, unit, inverse, gain[layer : layer + 1])
    upstream[...] = below
    copies.send(upstream, upstream_hbm)
    if split:
        below_low[...] = below.astype(bf16)
        for side, target in ((1 - core, up_sent_hbm), (core, up_kept_hbm)):
            copies.send(
                below_low.at[:, pl.ds(pl.multiple_of(side * half, lanes), half)], target
            )
    copies.finish()


def weight_kernel(chips, plan, with_vectors, *refs):
    meta = refs[0]
    refs = refs[1:]
    if with_vectors:
        vectors, up_sum = refs[:2]
        refs = refs[2:]
    count = 1 + max(max(item[0], item[1], item[4], item[5]) for item in plan)
    arrays = refs[:count]
    kept_hbm, sent_hbm = refs[count : count + 2]
    refs = refs[count + 2 :]
    lefts, rights = refs[: len(plan)], refs[len(plan) : 2 * len(plan)]
    total, block, slot_sems, sems = refs[2 * len(plan) :]
    copies = Copies(sems)
    columns = total.shape[1]
    waits = []
    for item, left, right in zip(plan, lefts, rights):
        own, far, at, size, right_own, right_far, right_at, strips, row = item
        rows = left.shape[0] // 2
        window, right_window = pl.ds(at, size), pl.ds(right_at, strips * columns)
        waits.append(
            [
                copies.bring(arrays[own].at[:, window], left.at[pl.ds(0, rows)]),
                copies.bring(arrays[right_own].at[:, right_window], right.at[pl.ds(0, rows)]),
                copies.bring(arrays[far].at[:, window], left.at[pl.ds(rows, rows)]),
                copies.bring(arrays[right_far].at[:, right_window], right.at[pl.ds(rows, rows)]),
            ]
        )
    half = chips // 2
    cuts = []

    def cut(source, first, part, row):
        def slot_copy(slot, index):
            chip = meta[1 + slot]
            start = pl.multiple_of(first + chip * part, 16)
            target = kept_hbm if slot < half else sent_hbm
            return pltpu.make_async_copy(
                source.at[pl.ds(start, part)],
                target.at[slot % half, pl.ds(row, part)],
                slot_sems.at[index],
            )

        for slot in reversed(range(chips)):
            copy = slot_copy(slot, len(cuts))
            copy.start()
            cuts.append(copy)

    if with_vectors:
        depth = block.shape[0] // chips

        def one_chip(chip, carry):
            width = vectors.shape[1]
            inner = up_sum.shape[1]
            short = pltpu.roll(vectors[...], width - chip * (width // chips), axis=1)
            wide = pltpu.roll(up_sum[...], inner - chip * (inner // chips), axis=1)
            rows = pl.ds(pl.multiple_of(chip * depth, 16), depth)
            block[rows, :] = jnp.concatenate(
                [short[:, :columns], wide[:, :columns]], axis=0
            ).astype(bf16)
            return carry

        lax.fori_loop(0, chips, one_chip, 0)
        last = plan[-1]
        cut(block, 0, depth, last[8] + last[7] * last[3] // chips)
    base = 0
    for item, left, right, wait in zip(plan, lefts, rights, waits):
        size, strips, row = item[3], item[7], item[8]
        part = size // chips
        for copy in wait:
            copy.wait()
        for strip in range(strips):
            strip_columns = slice(strip * columns, (strip + 1) * columns)
            for at in range(0, size, 768):
                window = slice(at, min(size, at + 768))
                total[base + at : base + min(size, at + 768), :] = dot_tn(
                    left[:, window], right[:, strip_columns]
                ).astype(bf16)
            cut(total, base, part, row + strip * part)
            base += size
    for copy in cuts:
        copy.wait()


def sum_kernel(groups, *refs):
    meta = refs[0]
    count = len(groups)
    steps = (len(refs) - 1 - 2 - count - 4) // count
    inputs = refs[1 : 1 + count * steps]
    kept_hbm, sent_hbm = refs[1 + count * steps : 3 + count * steps]
    buffers = refs[3 + count * steps : 3 + count * steps + count]
    total, kept, sent, sems = refs[3 + count * steps + count :]
    copies = Copies(sems)
    core = meta[0]
    waits = [
        [
            copies.bring(inputs[g * steps + step].at[0], buffers[g].at[step])
            for step in range(steps)
        ]
        for g in range(count)
    ]
    out = 0
    for g, pieces in enumerate(groups):
        for copy in waits[g]:
            copy.wait()
        rows = buffers[g].shape[1]
        value = buffers[g][0].astype(f32)
        for step in range(1, steps):
            value += buffers[g][step].astype(f32)
        total[:rows] = value
        for row, part, repeats in pieces:
            if not repeats:
                kept[out : out + part] = total[row : row + part]
                sent[out : out + part] = total[row : row + part]
                out += part
            for repeat in range(repeats):
                first = row + repeat * 2 * part
                kept[out : out + part] = total[pl.ds(pl.multiple_of(first + core * part, 8), part)]
                sent[out : out + part] = total[
                    pl.ds(pl.multiple_of(first + (1 - core) * part, 8), part)
                ]
                out += part
    copies.send(sent, sent_hbm)
    copies.send(kept, kept_hbm)
    copies.finish()


def place_kernel(places, meta, kept_hbm, far_hbm, *refs):
    outputs, (kept, far, sems) = refs[:-3], refs[-3:]
    copies = Copies(sems)
    wait = [copies.bring(kept_hbm, kept), copies.bring(far_hbm, far)]
    core = meta[0]
    columns = kept.shape[1]
    for copy in wait:
        copy.wait()
    for place in places:
        if len(place) == 5:
            first, part, index, layer, strips = place
            for strip in range(strips):
                rows = slice(first + strip * part, first + (strip + 1) * part)
                for side, source in ((core, kept), (1 - core, far)):
                    at = pl.multiple_of(side * (strips * columns) + strip * columns, lanes)
                    outputs[index][layer, :, pl.ds(at, columns)] = source[rows, :]
        else:
            first, half, layer = place
            short = kept[first : first + half] + far[first : first + half]
            wide = kept[first + half : first + 2 * half] + far[first + half : first + 2 * half]
            size, wide_size = outputs[4].shape[1], outputs[11].shape[1]
            short = pltpu.roll(short, columns - core * size, axis=1)
            wide = pltpu.roll(wide, columns - core * wide_size, axis=1)
            outputs[4][layer : layer + 1] = short[0:1, :size]
            outputs[5][layer : layer + 1] = short[1:2, :size]
            outputs[6][layer] = short[2:4, :size]
            for row, index in ((4, 7), (5, 8), (6, 9), (7, 10)):
                outputs[index][layer : layer + 1] = short[row : row + 1, :size]
            outputs[11][layer : layer + 1] = wide[0:1, :wide_size]


def call(kernel, outs, ins, scratch, *arrays, flops=0, out_specs=None):
    count = sum(math.prod(a.shape) * a.dtype.itemsize for a in list(arrays) + list(outs))
    return pl.pallas_call(
        kernel,
        out_shape=tuple(outs),
        in_specs=list(ins),
        out_specs=tuple(out_specs or (HBM for _ in outs)),
        scratch_shapes=scratch,
        compiler_params=pltpu.CompilerParams(vmem_limit_bytes=56 * 1024 * 1024),
        cost_estimate=pl.CostEstimate(flops=flops, bytes_accessed=count, transcendentals=0),
    )(*arrays)


def swap_cores(array):
    return lax.ppermute(array, "tok", [(0, 1), (1, 0)])


def after(array, *others):
    return lax.optimization_barrier((array,) + others)[0]


def step_bit(step, core):
    return step ^ core if step < 2 else step


def step_pairs(chips, step):
    return [
        (chip * 2 + core, (chip ^ (1 << step_bit(step, core))) * 2 + core)
        for chip in range(chips)
        for core in range(2)
    ]


class Halving:
    def __init__(self, kept, sent, chips):
        self.chips = chips
        self.slots = chips // 2
        self.step = 0
        self.parts = [kept]
        self.move(sent)

    def move(self, sent):
        pairs = step_pairs(self.chips, self.step)
        self.parts.append(lax.ppermute(sent, ("row", "tok"), pairs))
        self.step += 1

    def next(self):
        half = self.slots // 2
        sent = sum(part[half : self.slots].astype(f32) for part in self.parts)
        sent = sent.astype(self.parts[0].dtype)
        self.slots = half
        self.move(sent)
        return sent

    def rest(self):
        while self.slots > 1:
            self.next()
        return self


def slots_of_chips(chips, me, core):
    steps = chips.bit_length() - 1
    slot = jnp.arange(chips, dtype=jnp.int32)
    distance = jnp.zeros_like(slot)
    for step in range(steps):
        bit = (slot >> (steps - 1 - step)) & 1
        shift = jnp.where(core == 0, step_bit(step, 0), step_bit(step, 1))
        distance = distance | (bit << shift)
    return distance ^ me


def plain_sums(left, left_far, right, right_far, slots, chips, core):
    product = dot_tn(
        jnp.concatenate([left, left_far], axis=0), jnp.concatenate([right, right_far], axis=0)
    ).astype(bf16)
    product = product.reshape(chips, -1, product.shape[1])[slots]
    done = Halving(product[: chips // 2], product[chips // 2 :], chips).rest()
    total = sum(part[0].astype(f32) for part in done.parts)
    total = total.reshape(2, -1, total.shape[1])
    kept = lax.dynamic_index_in_dim(total, core, 0, keepdims=False)
    other = swap_cores(lax.dynamic_index_in_dim(total, 1 - core, 0, keepdims=False))
    return jnp.where(
        core == 0,
        jnp.concatenate([kept, other], axis=1),
        jnp.concatenate([other, kept], axis=1),
    )


def plain_vectors(vectors, slots, chips, core):
    pieces = [vector.reshape(chips, 2, -1) for vector in vectors]
    packed = jnp.concatenate(pieces, axis=2)
    sent = lax.dynamic_index_in_dim(packed, 1 - core, 1, keepdims=False)
    packed = lax.dynamic_index_in_dim(packed, core, 1, keepdims=False) + swap_cores(sent)
    packed = packed[slots]
    done = Halving(packed[: chips // 2], packed[chips // 2 :], chips).rest()
    packed = sum(part[0] for part in done.parts)
    cuts, at = [], 0
    for piece in pieces:
        cuts.append(packed[at : at + piece.shape[2]])
        at += piece.shape[2]
    return cuts


def body(
    tokens,
    cotangent,
    segment_ids,
    valid,
    first_gain,
    first_shift,
    joint_weight,
    joint_bias,
    output_weight,
    output_bias,
    second_gain,
    second_shift,
    up_weight,
    up_bias,
    down_weight,
    down_bias,
    chips,
):
    layers, width = joint_weight.shape[:2]
    inner = up_weight.shape[2]
    heads = width // head_size
    rows = tokens.shape[1]
    columns = width // 2
    wide = 3 * columns
    core = lax.axis_index("tok").astype(jnp.int32)
    me = lax.axis_index("row").astype(jnp.int32)
    slots = slots_of_chips(chips, me, core)
    meta = jnp.concatenate([core[None], slots])
    code = segment_ids * 2 + valid
    code_far = swap_cores(code)
    joint_bias = joint_bias.reshape(2 * layers, width)
    dma = pltpu.SemaphoreType.DMA
    vm = pltpu.VMEM

    tokens = tokens[0]
    cotangent = cotangent[0]
    normed_one, query, kv, up_kept, up_sent = call(
        project_kernel,
        (
            shape((rows, width), bf16),
            shape((rows, width), bf16),
            shape((rows, 2 * width), bf16),
            shape((rows, columns), bf16),
            shape((rows, columns), bf16),
        ),
        (SMEM,) + (VMEM,) * 3 + (HBM,) * 3,
        [
            vm((rows, width), bf16),
            vm((width, 3 * width), bf16),
            vm((rows, width), bf16),
            vm((rows, width), bf16),
            vm((rows, width), bf16),
            vm((rows, 2 * width), bf16),
            dma((8,)),
        ],
        meta,
        first_gain,
        first_shift,
        joint_bias,
        tokens,
        joint_weight,
        cotangent,
        flops=2 * rows * width * 3 * width,
    )
    saved = []
    stream = tokens
    for layer in range(layers):
        last = layer == layers - 1
        far = swap_cores(kv)
        outs = [
            shape((rows, 2 * width + inner), bf16),
            shape((heads, rows, 2 * rows), bf16),
            shape((rows, width), f32),
            shape((rows, inner), bf16),
        ]
        small = [code, code_far, output_bias, second_gain, second_shift, up_bias]
        hbm = [stream, query, kv, far, output_weight, up_weight]
        scratch = [
            vm((rows, width), stream.dtype),
            vm((rows, width), bf16),
            vm((2 * rows, 2 * width), bf16),
            vm((rows, 2 * rows), f32),
            vm((rows, 2 * width + inner), bf16),
            vm((heads, rows, 2 * rows), bf16),
            vm((rows, width), f32),
            vm((rows, inner), bf16),
            vm((width, width), bf16),
            vm((width, inner), bf16),
        ]
        if not last:
            small += [down_bias, first_gain, first_shift, joint_bias]
            hbm += [down_weight, joint_weight]
            outs += [
                shape((rows, width), f32),
                shape((rows, width), bf16),
                shape((rows, width), bf16),
                shape((rows, 2 * width), bf16),
            ]
            scratch += [
                vm((inner, width), bf16),
                vm((width, 3 * width), bf16),
                vm((rows, width), f32),
                vm((rows, width), bf16),
                vm((rows, width), bf16),
                vm((rows, 2 * width), bf16),
            ]
        results = call(
            functools.partial(middle_kernel, layer, last),
            outs,
            [VMEM] * len(small) + [HBM] * len(hbm),
            scratch + [dma((16,))],
            *small,
            *hbm,
            flops=2 * rows * width * (2 * inner + 4 * width),
        )
        acts, soft, middle, slope = results[:4]
        saved.append(
            (stream, normed_one, query, kv, far, acts, soft, middle, slope)
            + (swap_cores(normed_one), swap_cores(acts))
        )
        if not last:
            stream, normed_one, query, kv = results[4:]

    part = width // chips
    native = part % 48 == 0
    strips_up = inner // 2 // columns
    strips_joint = wide // columns
    vector_rows = 8

    def weight_sums(plan, total_rows, gate, arrays, vectors=()):
        slot_rows = 16
        depth = max(item[7] * item[3] for item in plan) if len(plan) == 1 else sum(
            item[7] * item[3] for item in plan
        )
        cuts = chips * (sum(item[7] for item in plan) + (1 if vectors else 0))
        kept, sent = call(
            functools.partial(weight_kernel, chips, plan, bool(vectors)),
            (shape((chips // 2, total_rows, columns), bf16),) * 2,
            (SMEM,) + (VMEM,) * len(vectors) + (HBM,) * len(arrays),
            [vm((2 * rows, item[3]), bf16) for item in plan]
            + [vm((2 * rows, item[7] * columns), bf16) for item in plan]
            + [
                vm((depth, columns), bf16),
                vm((chips * slot_rows, columns), bf16),
                dma((cuts,)),
                dma((4 * len(plan),)),
            ],
            after(meta, *gate),
            *vectors,
            *arrays,
            flops=4 * rows * columns * depth,
        )
        return (kept, sent)

    def start(sums):
        return Halving(*sums, chips)

    def mlp_back(layer, upstream, gate):
        stream, normed_one, query, kv, far, acts, soft, middle, slope = saved[layer][:9]
        first = layer == layers - 1
        small = [after(meta, *gate), second_gain]
        hbm = []
        outs = [
            shape((rows, inner // 2), bf16),
            shape((rows, inner // 2), bf16),
            shape((rows, width), bf16),
            shape((rows, width), f32),
            shape((8, width), f32),
            shape((8, inner), f32),
        ]
        specs = [HBM] * 4 + [VMEM] * 2
        scratch = []
        if first:
            small += [down_bias]
            hbm += [acts]
            outs += [shape((rows, width), bf16)]
            specs += [HBM]
            scratch += [vm((rows, inner), bf16), vm((rows, width), bf16)]
        hbm += [upstream, slope, middle, down_weight, up_weight]
        return call(
            functools.partial(mlp_back_kernel, layer, first),
            outs,
            [SMEM] + [VMEM] * (len(small) - 1) + [HBM] * len(hbm),
            scratch
            + [
                vm((rows, width), upstream.dtype),
                vm((rows, inner), bf16),
                vm((rows, width), f32),
                vm((rows, inner // 2), bf16),
                vm((rows, inner // 2), bf16),
                vm((rows, width), bf16),
                vm((rows, width), f32),
                vm((rows, width), f32),
                vm((inner, width), bf16),
                vm((width, inner), bf16),
                dma((12,)),
            ],
            *small,
            *hbm,
            flops=4 * rows * width * inner,
            out_specs=specs,
        )

    def attention_back(layer, low, gate):
        stream, normed_one, query, kv, far, acts, soft, middle, slope = saved[layer][:9]
        return call(
            functools.partial(attention_back_kernel, layer),
            (
                shape((rows, width), bf16),
                shape((rows, 2 * width), f32),
                shape((rows, 2 * width), bf16),
                shape((8, width), f32),
            ),
            (HBM,) * 6,
            [
                vm((rows, width), bf16),
                vm((rows, width), bf16),
                vm((2 * rows, 2 * width), bf16),
                vm((heads, rows, 2 * rows), bf16),
                vm((rows, width), bf16),
                vm((width, width), bf16),
                vm((rows, width), bf16),
                vm((rows, 2 * width), f32),
                vm((rows, 2 * width), bf16),
                dma((heads // 2,)),
                dma((8,)),
            ],
            after(low, *gate),
            query,
            kv,
            far,
            soft,
            output_weight,
            flops=2 * rows * width * (width + 6 * rows),
            out_specs=(HBM,) * 3 + (VMEM,),
        )

    def project_back(layer, dq, own, received, dq_sum, vectors_two, low, middle_grad, gate):
        stream = saved[layer][0]
        split = layer > 0
        outs = [
            shape((rows, wide + columns), bf16),
            shape((rows, wide + columns), bf16),
            shape((rows, width), f32),
            shape((8, width), f32),
        ]
        specs = [HBM] * 3 + [VMEM]
        if split:
            outs += [shape((rows, columns), bf16)] * 2
            specs += [HBM] * 2
        return call(
            functools.partial(project_back_kernel, layer, split),
            outs,
            (SMEM,) + (VMEM,) * 3 + (HBM,) * 7,
            [
                vm((rows, 2 * width), f32),
                vm((rows, 2 * width), bf16),
                vm((rows, width), stream.dtype),
                vm((rows, width), bf16),
                vm((rows, width), bf16),
                vm((rows, width), f32),
                vm((rows, 3 * width), bf16),
                vm((rows, width), f32),
                vm((width, 3 * width), bf16),
                dma((16,)),
            ],
            after(meta, *gate),
            first_gain,
            dq_sum,
            vectors_two,
            dq,
            own,
            received,
            stream,
            low,
            middle_grad,
            joint_weight,
            flops=2 * rows * width * 3 * width,
            out_specs=specs,
        )

    plan_down = ((0, 1, 2 * width, inner, 2, 3, 0, 1, 0),)
    plan_up = ((0, 1, width, width, 2, 3, 0, strips_up, 0),)
    plan_joint = (
        (0, 1, 0, width, 4, 5, 0, strips_joint, 0),
        (2, 3, 0, width, 4, 5, wide, 1, strips_joint * part),
    )
    down_rows, up_rows = inner // chips, strips_up * part
    joint_rows = (strips_joint + 1) * part + 16

    groups = [None] * layers
    upstream = cotangent
    gate = (saved[-1][8],)
    output = None
    pending = []
    mats, vecs = [None] * layers, [None] * layers
    for layer in reversed(range(layers)):
        normed_one, acts, normed_far, acts_far = (saved[layer][i] for i in (1, 5, 9, 10))
        got = mlp_back(layer, upstream, gate)
        preact_kept, preact_sent, low, middle_grad, vectors_two, up_sum = got[:6]
        if layer == layers - 1:
            output = got[6]
        preact_far = swap_cores(preact_sent)
        gate = (low,)
        if pending:
            joint = pending.pop()
            sums = joint(gate)
            gate = (sums[0],)
        up_far = swap_cores(up_sent)
        if native:
            down = weight_sums(
                plan_down, down_rows, gate, (acts, acts_far, up_kept, up_far)
            )
            down_sum = start(down)
            up = weight_sums(
                plan_up, up_rows, (down[0],), (acts, acts_far, preact_kept, preact_far)
            )
            up_group = start(up)
            gate = (up[0],)
        dq, own, sent, dq_sum = attention_back(layer, low, gate)
        received = swap_cores(sent)
        got = project_back(
            layer, dq, own, received, dq_sum, vectors_two, low, middle_grad, (dq,)
        )
        mix_kept, mix_sent, upstream, vectors = got[:4]
        mix_far = swap_cores(mix_sent)
        if native:
            groups[layer] = [down_sum, up_group, None]

            def joint(
                gate,
                layer=layer,
                arrays=(normed_one, normed_far, acts, acts_far, mix_kept, mix_far),
                vectors=(vectors, up_sum),
            ):
                sums = weight_sums(plan_joint, joint_rows, gate, arrays, vectors)
                groups[layer][2] = start(sums)
                return sums

            pending.append(joint)
        else:
            split = functools.partial(plain_sums, slots=slots, chips=chips, core=core)
            mats[layer] = (
                split(normed_one, normed_far, mix_kept[:, :wide], mix_far[:, :wide]),
                split(
                    acts[:, :width], acts_far[:, :width], mix_kept[:, wide:], mix_far[:, wide:]
                ),
                split(
                    acts[:, width : 2 * width],
                    acts_far[:, width : 2 * width],
                    preact_kept,
                    preact_far,
                ),
                split(acts[:, 2 * width :], acts_far[:, 2 * width :], up_kept, up_far),
            )
            vecs[layer] = [vectors[row] for row in range(vector_rows)] + [up_sum[0]]
        gate = (upstream,)
        if layer:
            up_kept, up_sent = got[4:6]
    if native:
        pending.pop()(gate)
    input_gradient = upstream

    if not native:
        cuts = plain_vectors(
            [vector for layer in range(layers) for vector in vecs[layer]], slots, chips, core
        )

        def stacked(position):
            return jnp.stack([cuts[layer * 9 + position] for layer in range(layers)])

        def matrix(position):
            return jnp.stack([mats[layer][position] for layer in range(layers)])

        return (
            output[None],
            input_gradient[None],
            stacked(0),
            stacked(1),
            matrix(0),
            jnp.stack([stacked(2), stacked(3)], axis=1),
            matrix(1),
            stacked(4),
            stacked(5),
            stacked(6),
            matrix(2),
            stacked(8),
            matrix(3),
            stacked(7),
        )

    half = part // 2
    pieces, places, parts, base = [], [], [], 0
    for layer in range(layers):
        down_sum, up_group, joint_group = (group.rest() for group in groups[layer])
        parts += down_sum.parts + up_group.parts + joint_group.parts
        pieces += [
            ((0, inner // chips // 2, 1),),
            ((0, half, strips_up),),
            (
                (0, half, strips_joint),
                (strips_joint * part, half, 1),
                ((strips_joint + 1) * part, 16, 0),
            ),
        ]
        for size, index, strips in (
            (inner // chips // 2, 3, 1),
            (half, 2, strips_up),
            (half, 0, strips_joint),
            (half, 1, 1),
        ):
            places.append((base, size, index, layer, strips))
            base += strips * size
        places.append((base, 8, layer))
        base += 16
    group_rows = [down_rows, up_rows, joint_rows] * layers
    steps = len(parts) // len(group_rows)
    kept, sent = call(
        functools.partial(sum_kernel, pieces),
        (shape((base, columns), f32),) * 2,
        (SMEM,) + (HBM,) * len(parts),
        [vm((steps, count, columns), bf16) for count in group_rows]
        + [
            vm((max(group_rows), columns), f32),
            vm((base, columns), f32),
            vm((base, columns), f32),
            dma((len(parts) + 2,)),
        ],
        meta,
        *parts,
    )
    far = swap_cores(sent)
    outs = [
        shape((layers, half, 3 * width), f32),
        shape((layers, half, width), f32),
        shape((layers, half, inner), f32),
        shape((layers, inner // chips // 2, width), f32),
        shape((layers, half), f32),
        shape((layers, half), f32),
        shape((layers, 2, half), f32),
        shape((layers, half), f32),
        shape((layers, half), f32),
        shape((layers, half), f32),
        shape((layers, half), f32),
        shape((layers, inner // chips // 2), f32),
    ]
    final = call(
        functools.partial(place_kernel, places),
        outs,
        (SMEM, HBM, HBM),
        [vm((base, columns), f32), vm((base, columns), f32), dma((2,))],
        meta,
        kept,
        far,
        out_specs=(VMEM,) * len(outs),
    )
    joints, outputs, ups, downs, gain_one, shift_one, biases = final[:7]
    bias_out, gain_two, shift_two, bias_down, bias_up = final[7:]
    return (
        output[None],
        input_gradient[None],
        gain_one,
        shift_one,
        joints,
        biases,
        outputs,
        bias_out,
        gain_two,
        shift_two,
        ups,
        bias_up,
        downs,
        bias_down,
    )


def solution(mesh):
    chips = mesh.shape["row"]
    split = P("row", "tok", None)
    in_specs = (split, split, P("row", "tok"), P("row", "tok")) + (P(),) * 12
    vector = P(None, ("row", "tok"))
    table = P(None, ("row", "tok"), None)
    out_specs = (
        split,
        split,
        vector,
        vector,
        table,
        P(None, None, ("row", "tok")),
        table,
        vector,
        vector,
        vector,
        table,
        vector,
        table,
        vector,
    )

    def run(*arrays):
        return body(*arrays, chips=chips)

    return jax.shard_map(run, mesh=mesh, in_specs=in_specs, out_specs=out_specs, check_vma=False)
```

```python
import functools
import math

import jax
import jax.numpy as jnp
from jax import lax
from jax.experimental import pallas as pl
from jax.experimental.pallas import tpu as pltpu
from jax.sharding import PartitionSpec as P

epsilon = 1e-05
score_scale = 0.125
masked_score = -1e30
head_size = 64
lanes = 128
f32 = jnp.float32
bf16 = jnp.bfloat16
VMEM = pl.BlockSpec(memory_space=pltpu.VMEM)
SMEM = pl.BlockSpec(memory_space=pltpu.SMEM)
HBM = pl.BlockSpec(memory_space=pltpu.HBM)
ANY = pl.BlockSpec(memory_space=pl.ANY)


def shape(dims, kind):
    return jax.ShapeDtypeStruct(dims, kind)


def dot(left, right):
    return jnp.dot(left, right, preferred_element_type=f32)


def dot_nt(left, right):
    return lax.dot_general(left, right, (((1,), (1,)), ((), ())), preferred_element_type=f32)


def dot_tn(left, right):
    return lax.dot_general(left, right, (((0,), (0,)), ((), ())), preferred_element_type=f32)


def normalize(stream):
    centre = stream - jnp.mean(stream, axis=-1, keepdims=True)
    inverse = lax.rsqrt(jnp.mean(centre * centre, axis=-1, keepdims=True) + epsilon)
    return centre * inverse, inverse


def norm_back(upstream, unit, inverse, gain):
    scaled = upstream * gain
    return inverse * (
        scaled
        - jnp.mean(scaled, axis=-1, keepdims=True)
        - unit * jnp.mean(scaled * unit, axis=-1, keepdims=True)
    )


def column_sum(array):
    return jnp.sum(array, axis=0, keepdims=True)


def gelu_and_slope(x):
    size = jnp.abs(x)
    t = 1.0 / (1.0 + (0.3275911 * 0.7071067811865476) * size)
    bell = jnp.exp(-0.5 * (x * x))
    series = t * (
        0.5 * 0.254829592
        + t
        * (
            0.5 * -0.284496736
            + t * (0.5 * 1.421413741 + t * (0.5 * -1.453152027 + t * (0.5 * 1.061405429)))
        )
    )
    tail = series * bell
    share = jnp.where(x >= 0, 1.0 - tail, tail)
    return x * share, share + x * (bell * 0.3989422804014327)


class Copies:
    def __init__(self, sems):
        self.sems = sems
        self.used = 0
        self.out = []

    def bring(self, source, target):
        copy = pltpu.make_async_copy(source, target, self.sems.at[self.used])
        self.used += 1
        copy.start()
        return copy

    def send(self, source, target):
        self.out.append(self.bring(source, target))

    def thirds(self, source, target, order):
        third = target.shape[1] // 3
        windows = [pl.ds(index * third, third) for index in order]
        return [self.bring(source.at[:, window], target.at[:, window]) for window in windows]

    def finish(self):
        for copy in self.out:
            copy.wait()


def emit_project(stream, layer, gain, shift, bias, weight, waits, normed_ref, query_ref, kv_ref):
    width = stream.shape[1]
    unit, _ = normalize(stream)
    normed_ref[...] = (unit * gain[layer : layer + 1] + shift[layer : layer + 1]).astype(bf16)
    normed = normed_ref[...]
    waits[0].wait()
    kv_ref[:, :width] = dot(normed, weight[:, width : 2 * width]).astype(bf16)
    waits[1].wait()
    kv_ref[:, width:] = (
        dot(normed, weight[:, 2 * width :]) + bias[layer, 1:2]
    ).astype(bf16)
    waits[2].wait()
    queries = (dot(normed, weight[:, :width]) + bias[layer, 0:1]).astype(bf16)
    query_ref[...] = queries * jnp.asarray(score_scale, bf16)


def head_masks():
    lane = lax.broadcasted_iota(jnp.int32, (1, lanes), 1)
    return (lane < head_size, lane >= head_size)


def emit_mask(rows, code_ref, far_ref, mask_ref):
    own = code_ref[...].astype(f32)
    diagonal = lax.broadcasted_iota(jnp.int32, (rows, rows), 0) == lax.broadcasted_iota(
        jnp.int32, (rows, rows), 1
    )
    column = jnp.sum(jnp.where(diagonal, own, 0.0), axis=1, keepdims=True)
    mask_ref[:, :rows] = jnp.where(column == own, 0.0, masked_score)
    mask_ref[:, rows:] = jnp.where(column == far_ref[...].astype(f32), 0.0, masked_score)


def emit_attention(width, query_ref, kv_ref, mask_ref, attended_ref, soft_ref):
    rows = query_ref.shape[0]
    masks = head_masks()
    zero = jnp.zeros((), bf16)

    def one_pair(pair, carry):
        at = pl.multiple_of(pair * lanes, lanes)
        columns = pl.ds(at, lanes)
        queries = query_ref[:, columns]
        keys = kv_ref[:, columns]
        values = kv_ref[:, pl.ds(pl.multiple_of(at + width, lanes), lanes)]
        total = jnp.zeros((rows, lanes), f32)
        for side in range(2):
            own = jnp.where(masks[side], queries, zero)
            scores = dot_nt(own, keys) + mask_ref[...]
            exponent = jnp.exp(scores - jnp.max(scores, axis=-1, keepdims=True))
            soft = exponent * (1.0 / jnp.sum(exponent, axis=-1, keepdims=True))
            soft_low = soft.astype(bf16)
            soft_ref[pair * 2 + side] = soft_low
            total += dot(soft_low, jnp.where(masks[side], values, zero))
        attended_ref[:, columns] = total.astype(bf16)
        return carry

    lax.fori_loop(0, width // lanes, one_pair, 0, unroll=2)


def emit_attention_back(
    width, query_ref, kv_ref, soft_ref, wait_soft, grad_ref, dq_ref, dq_sum, own_ref, sent_ref
):
    rows = query_ref.shape[0]
    masks = head_masks()
    zero = jnp.zeros((), bf16)

    def one_pair(pair, carry):
        wait_soft(pair)
        at = pl.multiple_of(pair * lanes, lanes)
        columns = pl.ds(at, lanes)
        value_columns = pl.ds(pl.multiple_of(at + width, lanes), lanes)
        queries = query_ref[:, columns]
        grads = grad_ref[:, columns]
        keys = kv_ref[:, columns]
        values = kv_ref[:, value_columns]
        dq = jnp.zeros((rows, lanes), f32)
        dk = jnp.zeros((2 * rows, lanes), f32)
        dv = jnp.zeros((2 * rows, lanes), f32)
        for side in range(2):
            soft_low = soft_ref[pair * 2 + side]
            soft = soft_low.astype(f32)
            own = jnp.where(masks[side], grads, zero)
            soft_grad = dot_nt(own, values)
            delta = jnp.sum(soft_grad * soft, axis=-1, keepdims=True)
            score_grad = (soft * (soft_grad - delta)).astype(bf16)
            dq += dot(score_grad, jnp.where(masks[side], keys, zero))
            dk += dot_tn(score_grad, jnp.where(masks[side], queries, zero))
            dv += dot_tn(soft_low, own)
        dq = dq * score_scale
        dq_ref[:, columns] = dq.astype(bf16)
        dq_sum[0:1, columns] = column_sum(dq)
        own_ref[:, columns] = dk[:rows]
        own_ref[:, value_columns] = dv[:rows]
        sent_ref[:, columns] = dk[rows:].astype(bf16)
        sent_ref[:, value_columns] = dv[rows:].astype(bf16)
        return carry

    lax.fori_loop(0, width // lanes, one_pair, 0, unroll=2)


def project_kernel(
    gain, shift, bias, tokens_hbm, weight_hbm, grad_hbm,
    query_hbm, packed_hbm, kept_hbm,
    tokens, weight, grad, normed, query, kv, sems,
):
    copies = Copies(sems)
    width = tokens.shape[1]
    half = width // 2
    first = copies.bring(tokens_hbm, tokens)
    third = copies.bring(grad_hbm, grad)
    thirds = copies.thirds(weight_hbm.at[0], weight, (1, 2, 0))
    core = lax.axis_index("tok")
    first.wait()
    third.wait()
    copies.send(
        grad.at[:, pl.ds(pl.multiple_of((1 - core) * half, half), half)],
        packed_hbm.at[:, pl.ds(3 * width, half)],
    )
    copies.send(grad.at[:, pl.ds(pl.multiple_of(core * half, half), half)], kept_hbm)
    emit_project(tokens[...].astype(f32), 0, gain, shift, bias, weight, thirds, normed, query, kv)
    copies.send(kv, packed_hbm.at[:, pl.ds(0, 2 * width)])
    copies.send(normed, packed_hbm.at[:, pl.ds(2 * width, width)])
    copies.send(query, query_hbm)
    copies.finish()


def emit_upper_half(layer, stream, output_weight, bias, gain, shift, acts, middle_ref):
    width = stream.shape[1]
    middle = stream + dot(acts[:, :width], output_weight[...]) + bias[layer : layer + 1]
    middle_ref[...] = middle
    unit, _ = normalize(middle)
    acts[:, width:] = (unit * gain[layer : layer + 1] + shift[layer : layer + 1]).astype(bf16)


def middle_kernel(
    layer, code, code_far, output_bias, gain, shift, up_bias,
    down_bias, next_gain, next_shift, joint_bias,
    stream_hbm, query_hbm, packed_hbm, far_hbm, output_hbm, up_hbm, down_hbm, joint_hbm,
    acts_hbm, hidden_hbm, soft_hbm, middle_hbm, slope_hbm,
    stream_next_hbm, query_next_hbm, packed_next_hbm,
    stream_ref, query, kv, mask, acts, hidden_ref, soft, middle_ref, slope,
    output_weight, up_weight, down_weight, joint_weight, total, normed, query_next, kv_next, sems,
):
    copies = Copies(sems)
    rows, width = query.shape
    inner = up_weight.shape[1]
    kv_window = pl.ds(0, 2 * width)
    wait = [
        copies.bring(query_hbm, query),
        copies.bring(packed_hbm.at[:, kv_window], kv.at[pl.ds(0, rows)]),
        copies.bring(far_hbm.at[:, kv_window], kv.at[pl.ds(rows, rows)]),
        copies.bring(stream_hbm, stream_ref),
    ]
    emit_mask(rows, code, code_far, mask)
    for copy in wait[:3]:
        copy.wait()
    output_copy = copies.bring(output_hbm.at[layer], output_weight)
    up_copy = copies.bring(up_hbm.at[layer], up_weight)
    down_copy = copies.bring(down_hbm.at[layer], down_weight)
    thirds = copies.thirds(joint_hbm.at[layer + 1], joint_weight, (1, 2, 0))
    emit_attention(width, query, kv, mask, acts, soft)
    copies.send(soft, soft_hbm)
    wait[3].wait()
    output_copy.wait()
    emit_upper_half(
        layer,
        stream_ref[...].astype(f32),
        output_weight,
        output_bias,
        gain,
        shift,
        acts,
        middle_ref,
    )
    copies.send(acts, acts_hbm)
    copies.send(middle_ref, middle_hbm)
    up_copy.wait()
    down_copy.wait()
    total[...] = middle_ref[...] + down_bias[layer : layer + 1]
    chunk = width
    for at in range(0, inner, chunk):
        columns = slice(at, at + chunk)
        preact = dot(acts[:, width:], up_weight[:, columns])
        hidden, rate = gelu_and_slope(preact + up_bias[layer : layer + 1, columns])
        hidden_ref[:, columns] = hidden.astype(bf16)
        slope[:, columns] = rate.astype(bf16)
        total[...] += dot(hidden_ref[:, columns], down_weight[columns, :])
    copies.send(hidden_ref, hidden_hbm)
    copies.send(slope, slope_hbm)
    copies.send(total, stream_next_hbm)
    emit_project(
        total[...],
        layer + 1,
        next_gain,
        next_shift,
        joint_bias,
        joint_weight,
        thirds,
        normed,
        query_next,
        kv_next,
    )
    copies.send(kv_next, packed_next_hbm.at[:, kv_window])
    copies.send(normed, packed_next_hbm.at[:, pl.ds(2 * width, width)])
    copies.send(query_next, query_next_hbm)
    copies.finish()


def emit_middle_grad(layer, core, upstream, middle, total, gain, vectors, low, grad_ref, kept, sent):
    width = middle.shape[1]
    columns = width // 2
    unit, inverse = normalize(middle)
    normed_grad = total[...]
    vectors[5:6] = column_sum(normed_grad * unit)
    vectors[6:7] = column_sum(normed_grad)
    middle_grad = upstream + norm_back(normed_grad, unit, inverse, gain[layer : layer + 1])
    vectors[4:5] = column_sum(middle_grad)
    grad_ref[...] = middle_grad
    low[...] = middle_grad.astype(bf16)
    behind = kept.shape[1] - columns
    for side, target in ((1 - core, sent), (core, kept)):
        target[:, behind:] = low[:, pl.ds(pl.multiple_of(side * columns, lanes), columns)]


def turn_kernel(
    layer, code, code_far, output_bias, gain, shift, up_bias, down_bias,
    stream_hbm, query_hbm, packed_hbm, far_hbm, upstream_hbm, output_hbm, up_hbm, down_hbm,
    acts_hbm, hidden_hbm, soft_hbm, result_hbm, kept_hbm, sent_hbm, low_hbm, grad_hbm,
    vectors, up_sum,
    stream_ref, query, kv, mask, acts, hidden_ref, soft, middle_ref, upstream_ref,
    kept, sent, low, grad_ref, result, result_low, total,
    output_weight, up_weight, down_weight, sems,
):
    copies = Copies(sems)
    rows, width = query.shape
    inner = up_weight.shape[1]
    core = lax.axis_index("tok")
    kv_window = pl.ds(0, 2 * width)
    wait = [
        copies.bring(query_hbm, query),
        copies.bring(packed_hbm.at[:, kv_window], kv.at[pl.ds(0, rows)]),
        copies.bring(far_hbm.at[:, kv_window], kv.at[pl.ds(rows, rows)]),
        copies.bring(stream_hbm, stream_ref),
    ]
    emit_mask(rows, code, code_far, mask)
    for copy in wait[:3]:
        copy.wait()
    output_copy = copies.bring(output_hbm.at[layer], output_weight)
    upstream_copy = copies.bring(upstream_hbm, upstream_ref)
    up_copy = copies.bring(up_hbm.at[layer], up_weight)
    down_copy = copies.bring(down_hbm.at[layer], down_weight)
    emit_attention(width, query, kv, mask, acts, soft)
    copies.send(soft, soft_hbm)
    wait[3].wait()
    output_copy.wait()
    emit_upper_half(
        layer,
        stream_ref[...].astype(f32),
        output_weight,
        output_bias,
        gain,
        shift,
        acts,
        middle_ref,
    )
    copies.send(acts, acts_hbm)
    upstream_copy.wait()
    upstream = upstream_ref[...].astype(f32)
    low[...] = upstream.astype(bf16)
    vectors[0:4] = jnp.zeros_like(vectors[0:4])
    vectors[7:8] = column_sum(upstream)
    up_sum[...] = jnp.zeros_like(up_sum)
    result[...] = middle_ref[...] + down_bias[layer : layer + 1]
    total[...] = jnp.zeros_like(total)
    up_copy.wait()
    down_copy.wait()
    chunk = width
    half = inner // 2
    for side, target in ((1 - core, sent), (core, kept)):
        for at in range(0, half, chunk):
            columns = pl.ds(pl.multiple_of(side * half + at, chunk), chunk)
            preact = dot(acts[:, width:], up_weight[:, columns])
            hidden, rate = gelu_and_slope(preact + up_bias[layer : layer + 1, columns])
            hidden_ref[:, columns] = hidden.astype(bf16)
            result[...] += dot(hidden_ref[:, columns], down_weight[columns, :])
            preact_grad = dot_nt(low[...], down_weight[columns, :]) * rate
            up_sum[0:1, columns] = column_sum(preact_grad)
            target[:, at : at + chunk] = preact_grad.astype(bf16)
            total[...] += dot_nt(target[:, at : at + chunk], up_weight[:, columns])
    copies.send(hidden_ref, hidden_hbm)
    result_low[...] = result[...].astype(bf16)
    copies.send(result_low, result_hbm)
    emit_middle_grad(
        layer,
        core,
        upstream_ref[...].astype(f32),
        middle_ref[...],
        total,
        gain,
        vectors,
        low,
        grad_ref,
        kept,
        sent,
    )
    copies.send(low, low_hbm)
    copies.send(sent, sent_hbm)
    copies.send(kept, kept_hbm)
    copies.send(grad_ref, grad_hbm)
    copies.finish()


def attention_back_kernel(
    layer, low_hbm, query_hbm, packed_hbm, far_hbm, soft_hbm, output_hbm,
    dq_hbm, own_hbm, sent_hbm, dq_sum,
    low, query, kv, soft, attended_grad, output_weight, dq, own, sent, soft_sems, sems,
):
    copies = Copies(sems)
    rows, width = low.shape
    kv_window = pl.ds(0, 2 * width)
    wait = [
        copies.bring(low_hbm, low),
        copies.bring(output_hbm.at[layer], output_weight),
        copies.bring(query_hbm, query),
        copies.bring(packed_hbm.at[:, kv_window], kv.at[pl.ds(0, rows)]),
        copies.bring(far_hbm.at[:, kv_window], kv.at[pl.ds(rows, rows)]),
    ]

    def soft_copy(pair):
        two = pl.ds(pair * 2, 2)
        return pltpu.make_async_copy(soft_hbm.at[two], soft.at[two], soft_sems.at[pair])

    for pair in range(width // lanes):
        soft_copy(pair).start()
    dq_sum[...] = jnp.zeros_like(dq_sum)
    wait[0].wait()
    wait[1].wait()
    attended_grad[...] = dot_nt(low[...], output_weight[...]).astype(bf16)
    for copy in wait[2:]:
        copy.wait()
    emit_attention_back(
        width,
        query,
        kv,
        soft,
        lambda pair: soft_copy(pair).wait(),
        attended_grad,
        dq,
        dq_sum,
        own,
        sent,
    )
    copies.send(sent, sent_hbm)
    copies.send(dq, dq_hbm)
    copies.send(own, own_hbm)
    copies.finish()


def emit_project_back(
    layer, copies, core, wait, thirds, dq_sum, vectors_two, gain, mixed, own, received,
    stream_ref, grad_ref, joint_weight, kept_hbm, sent_hbm, vectors,
):
    rows, width = stream_ref.shape
    wide = 3 * width // 2
    vectors[4:8] = vectors_two[4:8]
    vectors[2:3] = dq_sum[0:1]
    for copy in wait[:3]:
        copy.wait()
    kv_grad = own[...] + received[...].astype(f32)
    mixed[:, width:] = kv_grad.astype(bf16)
    vectors[3:4] = column_sum(kv_grad[:, width:])
    for side, target in ((1 - core, sent_hbm), (core, kept_hbm)):
        copies.send(mixed.at[:, pl.ds(pl.multiple_of(side * wide, lanes), wide)], target)
    normed_grad = jnp.zeros((rows, width), f32)
    for index, copy in enumerate(thirds):
        copy.wait()
        window = slice(index * width, (index + 1) * width)
        normed_grad += dot_nt(mixed[:, window], joint_weight[:, window])
    wait[3].wait()
    unit, inverse = normalize(stream_ref[...].astype(f32))
    vectors[0:1] = column_sum(normed_grad * unit)
    vectors[1:2] = column_sum(normed_grad)
    wait[4].wait()
    return grad_ref[...] + norm_back(normed_grad, unit, inverse, gain[layer : layer + 1])


def project_back_kernel(
    layer, gate, gain, dq_sum, vectors_two,
    dq_hbm, own_hbm, received_hbm, stream_hbm, grad_hbm, joint_hbm,
    kept_hbm, sent_hbm, upstream_hbm, vectors,
    own, received, stream_ref, grad_ref, mixed, upstream, joint_weight, sems,
):
    copies = Copies(sems)
    width = stream_ref.shape[1]
    wait = [
        copies.bring(dq_hbm, mixed.at[:, pl.ds(0, width)]),
        copies.bring(own_hbm, own),
        copies.bring(received_hbm, received),
        copies.bring(stream_hbm, stream_ref),
        copies.bring(grad_hbm, grad_ref),
    ]
    thirds = copies.thirds(joint_hbm.at[layer], joint_weight, (0, 1, 2))
    upstream[...] = emit_project_back(
        layer, copies, lax.axis_index("tok"), wait, thirds, dq_sum, vectors_two, gain, mixed,
        own, received, stream_ref, grad_ref, joint_weight, kept_hbm, sent_hbm, vectors,
    )
    copies.send(upstream, upstream_hbm)
    copies.finish()


def between_kernel(
    above, gate, gain, second_gain, dq_sum, vectors_two,
    dq_hbm, own_hbm, received_hbm, stream_hbm, grad_hbm, slope_hbm, middle_hbm,
    joint_hbm, down_hbm, up_hbm,
    mix_kept_hbm, mix_sent_hbm, up_kept_hbm, up_sent_hbm, kept_hbm, sent_hbm, low_hbm,
    grad_next_hbm, vectors, vectors_next, up_sum,
    own, received, stream_ref, grad_ref, mixed, upstream, low, slope, middle_ref,
    kept, sent, low_next, grad_next, total, joint_weight, down_weight, up_weight, sems,
):
    copies = Copies(sems)
    rows, width = stream_ref.shape
    inner = up_weight.shape[1]
    layer = above - 1
    core = lax.axis_index("tok")
    wait = [
        copies.bring(dq_hbm, mixed.at[:, pl.ds(0, width)]),
        copies.bring(own_hbm, own),
        copies.bring(received_hbm, received),
        copies.bring(stream_hbm, stream_ref),
        copies.bring(grad_hbm, grad_ref),
    ]
    thirds = copies.thirds(joint_hbm.at[above], joint_weight, (0, 1, 2))
    chunk = width
    half = inner // 2
    windows = [
        pl.ds(pl.multiple_of(side * half + at, chunk), chunk)
        for side in (1 - core, core)
        for at in range(0, half, chunk)
    ]
    slope_copy = copies.bring(slope_hbm, slope)
    weight_copies = [
        (
            copies.bring(down_hbm.at[layer, window], down_weight.at[window]),
            copies.bring(up_hbm.at[layer, :, window], up_weight.at[:, window]),
        )
        for window in windows
    ]
    middle_copy = copies.bring(middle_hbm, middle_ref)
    below = emit_project_back(
        above, copies, core, wait, thirds, dq_sum, vectors_two, gain, mixed,
        own, received, stream_ref, grad_ref, joint_weight, mix_kept_hbm, mix_sent_hbm, vectors,
    )
    upstream[...] = below
    low[...] = below.astype(bf16)
    columns = width // 2
    for side, target in ((1 - core, up_sent_hbm), (core, up_kept_hbm)):
        copies.send(low.at[:, pl.ds(pl.multiple_of(side * columns, lanes), columns)], target)
    vectors_next[0:4] = jnp.zeros_like(vectors_next[0:4])
    vectors_next[7:8] = column_sum(below)
    up_sum[...] = jnp.zeros_like(up_sum)
    total[...] = jnp.zeros_like(total)
    slope_copy.wait()
    for index, window in enumerate(windows):
        target = kept if index >= len(windows) // 2 else sent
        at = index % (len(windows) // 2) * chunk
        for copy in weight_copies[index]:
            copy.wait()
        preact_grad = dot_nt(low[...], down_weight[window, :]) * slope[:, window].astype(f32)
        up_sum[0:1, window] = column_sum(preact_grad)
        target[:, at : at + chunk] = preact_grad.astype(bf16)
        total[...] += dot_nt(target[:, at : at + chunk], up_weight[:, window])
    middle_copy.wait()
    emit_middle_grad(
        layer,
        core,
        upstream[...],
        middle_ref[...],
        total,
        second_gain,
        vectors_next,
        low_next,
        grad_next,
        kept,
        sent,
    )
    copies.send(low_next, low_hbm)
    copies.send(sent, sent_hbm)
    copies.send(kept, kept_hbm)
    copies.send(grad_next, grad_next_hbm)
    copies.finish()


def weight_kernel(chips, order, plan, vector_row, *refs):
    core, me = lax.axis_index("tok"), lax.axis_index("row")
    refs = refs[1:]
    if vector_row:
        vectors, up_sum = refs[:2]
        refs = refs[2:]
    count = 1 + max(max(item[0], item[1], item[5], item[6]) for item in plan)
    arrays = refs[:count]
    kept_hbm, sent_hbm = refs[count : count + 2]
    refs = refs[count + 2 :]
    lefts, rights = refs[: len(plan)], refs[len(plan) : 2 * len(plan)]
    turned, kept, sent, sems = refs[2 * len(plan) :]
    copies = Copies(sems)
    columns = kept.shape[2]
    half = chips // 2
    steps = chips.bit_length() - 1
    waits = []
    for item, left, right in zip(plan, lefts, rights):
        own, far, at, at_far, size, right_own, right_far, right_at, right_at_far, strips, row = item
        piece = min(size, 768)
        wait = []
        for first in range(0, size, piece):
            for side, array, start in ((0, own, at), (1, far, at_far)):
                wait.append(
                    copies.bring(
                        arrays[array].at[:, pl.ds(start + first, piece)],
                        left.at[side, :, pl.ds(first, piece)],
                    )
                )
        for side, array, start in ((0, right_own, right_at), (1, right_far, right_at_far)):
            window = pl.ds(start, strips * columns)
            wait.append(copies.bring(arrays[array].at[:, window], right.at[side]))
        waits.append(wait)
    slots = []
    for chip in range(chips):
        apart = chip ^ me
        slot = 0
        for step in range(steps):
            bit = jnp.where(core == 0, step_bit(order, step, 0), step_bit(order, step, 1))
            slot = slot * 2 + ((apart >> bit) & 1)
        slots.append(slot)
    if vector_row:
        depth = 16
        width, inner = vectors.shape[1], up_sum.shape[1]
        for base, target in ((half, sent), (0, kept)):
            for slot in range(half):
                chip = me ^ jnp.where(
                    core == 0,
                    distance(chips, order, base + slot, 0),
                    distance(chips, order, base + slot, 1),
                )
                short = pltpu.roll(vectors[...], width - chip * (width // chips), axis=1)
                wide = pltpu.roll(up_sum[...], inner - chip * (inner // chips), axis=1)
                target[slot, vector_row : vector_row + depth, :] = jnp.concatenate(
                    [short[:, :columns], wide[:, :columns]], axis=0
                ).astype(bf16)
    for number, (item, left, right, wait) in enumerate(zip(plan, lefts, rights, waits)):
        size, strips, row = item[4], item[9], item[10]
        part = size // chips
        piece = min(size, 768)
        rows = left.shape[1]
        for first in range(0, size, piece):
            for side in range(2):
                wait[first // piece * 2 + side].wait()
                flipped = left[side, :, first : first + piece].T
                for cut in range(0, piece, part):
                    slot = slots[(first + cut) // part]
                    turned[
                        pl.ds(pl.multiple_of(slot * part, 16), part),
                        side * rows : (side + 1) * rows,
                    ] = flipped[cut : cut + part]
        wait[-2].wait()
        wait[-1].wait()
        several = min(half, max(1, 384 // part))
        for base, target, target_hbm in ((half, sent, sent_hbm), (0, kept, kept_hbm)):

            def some_slots(index, carry, base=base, target=target):
                start = (base + index * several) * part
                both = turned[pl.ds(pl.multiple_of(start, 16), several * part), :]
                for strip in range(strips):
                    window = slice(strip * columns, (strip + 1) * columns)
                    product = dot(both[:, :rows], right[0, :, window])
                    product += dot(both[:, rows:], right[1, :, window])
                    for one in range(several):
                        target[
                            index * several + one, row + strip * part : row + (strip + 1) * part, :
                        ] = product[one * part : (one + 1) * part].astype(bf16)
                return carry

            lax.fori_loop(0, half // several, some_slots, 0)
            if number == len(plan) - 1:
                copies.send(target, target_hbm)
    copies.finish()


def sum_kernel(groups, *refs):
    count = len(groups)
    steps = (len(refs) - 2 - count - 4) // count
    inputs = refs[: count * steps]
    kept_hbm, sent_hbm = refs[count * steps : 2 + count * steps]
    buffers = refs[2 + count * steps : 2 + count * steps + count]
    total, kept, sent, sems = refs[2 + count * steps + count :]
    copies = Copies(sems)
    core = lax.axis_index("tok")
    waits = [
        [
            copies.bring(inputs[g * steps + step].at[0], buffers[g].at[step])
            for step in range(steps)
        ]
        for g in range(count)
    ]
    out = 0
    for g, pieces in enumerate(groups):
        for copy in waits[g]:
            copy.wait()
        rows = buffers[g].shape[1]
        value = buffers[g][0].astype(f32)
        for step in range(1, steps):
            value += buffers[g][step].astype(f32)
        total[:rows] = value
        for row, part, repeats in pieces:
            if not repeats:
                kept[out : out + part] = total[row : row + part]
                sent[out : out + part] = total[row : row + part]
                out += part
            for repeat in range(repeats):
                first = row + repeat * 2 * part
                kept[out : out + part] = total[pl.ds(pl.multiple_of(first + core * part, 8), part)]
                sent[out : out + part] = total[
                    pl.ds(pl.multiple_of(first + (1 - core) * part, 8), part)
                ]
                out += part
    copies.send(sent, sent_hbm)
    copies.send(kept, kept_hbm)
    copies.finish()


def place_kernel(places, *refs):
    count = len(places)
    inputs, outputs = refs[: 2 * count], refs[2 * count : -2 * count - 1]
    buffers, sems = refs[-2 * count - 1 : -1], refs[-1]
    copies = Copies(sems)
    wait = [copies.bring(source, target) for source, target in zip(inputs, buffers)]
    core = lax.axis_index("tok")
    for number, group in enumerate(places):
        kept, far = buffers[2 * number : 2 * number + 2]
        columns = kept.shape[1]
        for copy in wait[2 * number : 2 * number + 2]:
            copy.wait()
        for place in group:
            if len(place) == 5:
                first, part, index, layer, strips = place
                for strip in range(strips):
                    rows = slice(first + strip * part, first + (strip + 1) * part)
                    for side, source in ((core, kept), (1 - core, far)):
                        at = pl.multiple_of(side * (strips * columns) + strip * columns, lanes)
                        outputs[index][layer, :, pl.ds(at, columns)] = source[rows, :]
            else:
                first, half, layer = place
                short = kept[first : first + half] + far[first : first + half]
                wide = kept[first + half : first + 2 * half] + far[first + half : first + 2 * half]
                size, wide_size = outputs[4].shape[1], outputs[11].shape[1]
                short = pltpu.roll(short, columns - core * size, axis=1)
                wide = pltpu.roll(wide, columns - core * wide_size, axis=1)
                outputs[4][layer : layer + 1] = short[0:1, :size]
                outputs[5][layer : layer + 1] = short[1:2, :size]
                outputs[6][layer] = short[2:4, :size]
                for row, index in ((4, 7), (5, 8), (6, 9), (7, 10)):
                    outputs[index][layer : layer + 1] = short[row : row + 1, :size]
                outputs[11][layer : layer + 1] = wide[0:1, :wide_size]


def call(kernel, outs, ins, scratch, *arrays, flops=0, out_specs=None, limit=58):
    out_specs = tuple(out_specs or (ANY for _ in outs))
    count = sum(math.prod(a.shape) * a.dtype.itemsize for a in list(arrays) + list(outs))
    held = [kept for kept in scratch if kept.memory_space == pltpu.VMEM]
    held += [a for a, spec in zip(list(arrays) + list(outs), list(ins) + list(out_specs)) if spec is VMEM]
    need = sum(math.prod(a.shape) * a.dtype.itemsize for a in held) + (8 << 20)
    return pl.pallas_call(
        kernel,
        out_shape=tuple(outs),
        in_specs=list(ins),
        out_specs=out_specs,
        scratch_shapes=scratch,
        compiler_params=pltpu.CompilerParams(vmem_limit_bytes=max(need, limit << 20)),
        cost_estimate=pl.CostEstimate(flops=flops, bytes_accessed=count, transcendentals=0),
    )(*arrays)


def swap_cores(array):
    return lax.ppermute(array, "tok", [(0, 1), (1, 0)])


def after(array, *others):
    return lax.optimization_barrier((array,) + others)[0]


def step_bit(order, step, core):
    bit = order[step] if step < len(order) else step
    return bit ^ core if bit < 2 else bit


def distance(chips, order, slot, core):
    steps = chips.bit_length() - 1
    bits = [step_bit(order, step, core) for step in range(steps) if slot >> (steps - 1 - step) & 1]
    return sum(1 << bit for bit in bits)


def step_pairs(chips, order, step):
    return [
        (chip * 2 + core, (chip ^ (1 << step_bit(order, step, core))) * 2 + core)
        for chip in range(chips)
        for core in range(2)
    ]


class Halving:
    def __init__(self, kept, sent, chips, order=(0, 1)):
        self.chips = chips
        self.order = order
        self.slots = chips // 2
        self.step = 0
        self.parts = [kept]
        self.move(sent)

    def move(self, sent):
        pairs = step_pairs(self.chips, self.order, self.step)
        self.parts.append(lax.ppermute(sent, ("row", "tok"), pairs))
        self.step += 1

    def next(self):
        half = self.slots // 2
        sent = sum(part[half : self.slots].astype(f32) for part in self.parts)
        sent = sent.astype(self.parts[0].dtype)
        self.slots = half
        self.move(sent)
        return sent

    def rest(self):
        while self.slots > 1:
            self.next()
        return self


def slots_of_chips(chips, me, core):
    sides = [[distance(chips, (0, 1), slot, side) for slot in range(chips)] for side in range(2)]
    return me ^ jnp.asarray(sides, jnp.int32)[core]


def plain_sums(left, left_far, right, right_far, slots, chips, core):
    product = dot_tn(
        jnp.concatenate([left, left_far], axis=0), jnp.concatenate([right, right_far], axis=0)
    ).astype(bf16)
    product = product.reshape(chips, -1, product.shape[1])[slots]
    done = Halving(product[: chips // 2], product[chips // 2 :], chips).rest()
    total = sum(part[0].astype(f32) for part in done.parts)
    total = total.reshape(2, -1, total.shape[1])
    kept = lax.dynamic_index_in_dim(total, core, 0, keepdims=False)
    other = swap_cores(lax.dynamic_index_in_dim(total, 1 - core, 0, keepdims=False))
    return jnp.where(
        core == 0,
        jnp.concatenate([kept, other], axis=1),
        jnp.concatenate([other, kept], axis=1),
    )


def plain_vectors(vectors, slots, chips, core):
    pieces = [vector.reshape(chips, 2, -1) for vector in vectors]
    packed = jnp.concatenate(pieces, axis=2)
    sent = lax.dynamic_index_in_dim(packed, 1 - core, 1, keepdims=False)
    packed = lax.dynamic_index_in_dim(packed, core, 1, keepdims=False) + swap_cores(sent)
    packed = packed[slots]
    done = Halving(packed[: chips // 2], packed[chips // 2 :], chips).rest()
    packed = sum(part[0] for part in done.parts)
    cuts, at = [], 0
    for piece in pieces:
        cuts.append(packed[at : at + piece.shape[2]])
        at += piece.shape[2]
    return cuts


def body(
    tokens,
    cotangent,
    segment_ids,
    valid,
    first_gain,
    first_shift,
    joint_weight,
    joint_bias,
    output_weight,
    output_bias,
    second_gain,
    second_shift,
    up_weight,
    up_bias,
    down_weight,
    down_bias,
    chips,
):
    layers, width = joint_weight.shape[:2]
    inner = up_weight.shape[2]
    heads = width // head_size
    rows = tokens.shape[1]
    columns = width // 2
    wide = 3 * columns
    part = width // chips
    native = part % 48 == 0
    strips_up = inner // 2 // columns
    strips_joint = wide // columns
    core = lax.axis_index("tok").astype(jnp.int32)
    code = segment_ids * 2 + valid
    code_far = swap_cores(code)
    dma = pltpu.SemaphoreType.DMA
    weights = (joint_weight, output_weight, up_weight, down_weight)

    def vm(*sizes, kind=bf16):
        return pltpu.VMEM(sizes, kind)

    def low_shape(*sizes):
        return shape(sizes, bf16)

    def full_shape(*sizes):
        return shape(sizes, f32)

    def places_of(arrays):
        return [HBM if any(array is weight for weight in weights) else ANY for array in arrays]

    def wired(kernel, small, large, outs, scratch, flops, vector_outs=0):
        return call(
            kernel,
            outs,
            [VMEM] * len(small) + places_of(large),
            scratch,
            *small,
            *large,
            flops=flops,
            out_specs=[ANY] * (len(outs) - vector_outs) + [VMEM] * vector_outs,
        )

    tokens = tokens[0]
    cotangent = cotangent[0]
    last = layers - 1
    query, packed, up_kept = wired(
        project_kernel,
        [first_gain, first_shift, joint_bias],
        [tokens, joint_weight, cotangent],
        [low_shape(rows, width), low_shape(rows, 3 * width + columns), low_shape(rows, columns)],
        [
            vm(rows, width),
            vm(width, 3 * width),
            vm(rows, width),
            vm(rows, width),
            vm(rows, width),
            vm(rows, 2 * width),
            dma((12,)),
        ],
        2 * rows * width * 3 * width,
    )
    saved = []
    stream = tokens
    for layer in range(last):
        far = swap_cores(packed)
        gate = [item for kept in saved for item in kept[-2:]]
        acts, hidden, soft, middle, slope, stream_next, query_next, packed_next = wired(
            functools.partial(middle_kernel, layer),
            [after(code, *gate), code_far, output_bias, second_gain, second_shift, up_bias]
            + [down_bias, first_gain, first_shift, joint_bias],
            [stream, query, packed, far, output_weight, up_weight, down_weight, joint_weight],
            [
                low_shape(rows, 2 * width),
                low_shape(rows, inner),
                low_shape(heads, rows, 2 * rows),
                full_shape(rows, width),
                low_shape(rows, inner),
                full_shape(rows, width),
                low_shape(rows, width),
                low_shape(rows, 3 * width),
            ],
            [
                vm(rows, width, kind=stream.dtype),
                vm(rows, width),
                vm(2 * rows, 2 * width),
                vm(rows, 2 * rows, kind=f32),
                vm(rows, 2 * width),
                vm(rows, inner),
                vm(heads, rows, 2 * rows),
                vm(rows, width, kind=f32),
                vm(rows, inner),
                vm(width, width),
                vm(width, inner),
                vm(inner, width),
                vm(width, 3 * width),
                vm(rows, width, kind=f32),
                vm(rows, width),
                vm(rows, width),
                vm(rows, 2 * width),
                dma((24,)),
            ],
            2 * rows * width * (2 * inner + 4 * width + 4 * rows),
        )
        saved.append(
            (stream, query, packed, far, acts, hidden, soft, middle, slope)
            + (swap_cores(acts), swap_cores(hidden))
        )
        stream, query, packed = stream_next, query_next, packed_next

    mixed_columns = inner // 2 + columns
    far = swap_cores(packed)
    gate = [item for kept in saved for item in kept[-2:]] if len(saved) > 1 else []
    got = wired(
        functools.partial(turn_kernel, last),
        [after(code, *gate), code_far, output_bias, second_gain, second_shift, up_bias, down_bias],
        [stream, query, packed, far, cotangent, output_weight, up_weight, down_weight],
        [
            low_shape(rows, 2 * width),
            low_shape(rows, inner),
            low_shape(heads, rows, 2 * rows),
            low_shape(rows, width),
            low_shape(rows, mixed_columns),
            low_shape(rows, mixed_columns),
            low_shape(rows, width),
            full_shape(rows, width),
            full_shape(8, width),
            full_shape(8, inner),
        ],
        [
            vm(rows, width, kind=stream.dtype),
            vm(rows, width),
            vm(2 * rows, 2 * width),
            vm(rows, 2 * rows, kind=f32),
            vm(rows, 2 * width),
            vm(rows, inner),
            vm(heads, rows, 2 * rows),
            vm(rows, width, kind=f32),
            vm(rows, width),
            vm(rows, mixed_columns),
            vm(rows, mixed_columns),
            vm(rows, width),
            vm(rows, width, kind=f32),
            vm(rows, width, kind=f32),
            vm(rows, width),
            vm(rows, width, kind=f32),
            vm(width, width),
            vm(width, inner),
            vm(inner, width),
            dma((24,)),
        ],
        2 * rows * width * (4 * inner + width + 4 * rows),
        vector_outs=2,
    )
    acts, hidden, soft, output, preact_kept, preact_sent, low, middle_grad = got[:8]
    vectors_two, up_sum = got[8:]
    saved.append(
        (stream, query, packed, far, acts, hidden, soft, None, None)
        + (swap_cores(acts), swap_cores(hidden))
    )

    def attention_back(layer, low, gate):
        query, packed, far, _, _, soft = saved[layer][1:7]
        return wired(
            functools.partial(attention_back_kernel, layer),
            [],
            [after(low, *gate), query, packed, far, soft, output_weight],
            [
                low_shape(rows, width),
                full_shape(rows, 2 * width),
                low_shape(rows, 2 * width),
                full_shape(8, width),
            ],
            [
                vm(rows, width),
                vm(rows, width),
                vm(2 * rows, 2 * width),
                vm(heads, rows, 2 * rows),
                vm(rows, width),
                vm(width, width),
                vm(rows, width),
                vm(rows, 2 * width, kind=f32),
                vm(rows, 2 * width),
                dma((heads // 2,)),
                dma((8,)),
            ],
            2 * rows * width * (width + 10 * rows),
            vector_outs=1,
        )

    back_scratch = [
        vm(rows, 2 * width, kind=f32),
        vm(rows, 2 * width),
        vm(rows, width, kind=f32),
        vm(rows, width, kind=f32),
        vm(rows, 3 * width),
        vm(rows, width, kind=f32),
    ]

    def project_back(layer, dq, own, received, dq_sum, vectors_two, middle_grad, gate):
        stream = saved[layer][0]
        scratch = list(back_scratch)
        scratch[2] = vm(rows, width, kind=stream.dtype)
        return wired(
            functools.partial(project_back_kernel, layer),
            [after(code, *gate), first_gain, dq_sum, vectors_two],
            [dq, own, received, stream, middle_grad, joint_weight],
            [
                low_shape(rows, wide),
                low_shape(rows, wide),
                full_shape(rows, width),
                full_shape(8, width),
            ],
            scratch + [vm(width, 3 * width), dma((16,))],
            2 * rows * width * 3 * width,
            vector_outs=1,
        )

    def between(above, dq, own, received, dq_sum, vectors_two, middle_grad, gate):
        stream = saved[above][0]
        middle, slope = saved[above - 1][7:9]
        return wired(
            functools.partial(between_kernel, above),
            [after(code, *gate), first_gain, second_gain, dq_sum, vectors_two],
            [dq, own, received, stream, middle_grad, slope, middle]
            + [joint_weight, down_weight, up_weight],
            [
                low_shape(rows, wide),
                low_shape(rows, wide),
                low_shape(rows, columns),
                low_shape(rows, columns),
                low_shape(rows, mixed_columns),
                low_shape(rows, mixed_columns),
                low_shape(rows, width),
                full_shape(rows, width),
                full_shape(8, width),
                full_shape(8, width),
                full_shape(8, inner),
            ],
            back_scratch
            + [
                vm(rows, width),
                vm(rows, inner),
                vm(rows, width, kind=f32),
                vm(rows, mixed_columns),
                vm(rows, mixed_columns),
                vm(rows, width),
                vm(rows, width, kind=f32),
                vm(rows, width, kind=f32),
                vm(width, 3 * width),
                vm(inner, width),
                vm(width, inner),
                dma((40,)),
            ],
            2 * rows * width * (3 * width + 2 * inner),
            vector_outs=3,
        )

    groups = []
    gate = []

    def start(order, items, gate_arrays, vectors=()):
        arrays, plan, pieces, places = [], [], [], []
        row, vector_row = 0, 0

        def number(array):
            for index, known in enumerate(arrays):
                if known is array:
                    return index
            arrays.append(array)
            return len(arrays) - 1

        for left, left_far, at, at_far, size, right, right_far, r_at, r_at_far, strips, kind in items:
            left, left_far, right, right_far = map(number, (left, left_far, right, right_far))
            plan.append(
                (left, left_far, at, at_far, size, right, right_far, r_at, r_at_far, strips, row)
            )
            pieces.append((row, size // chips // 2, strips))
            places.append((size // chips // 2, kind[0], kind[1], strips))
            row += strips * size // chips
        if vectors:
            vector_row = row
            pieces.append((row, 16, 0))
            places.append((16, vectors[2]))
            row += 16
        depth = sum(item[9] * item[4] for item in plan)
        kept, sent = call(
            functools.partial(weight_kernel, chips, order, tuple(plan), vector_row),
            (low_shape(chips // 2, row, columns),) * 2,
            [ANY] + [VMEM] * len(vectors[:2]) + [ANY] * len(arrays),
            [vm(2, rows, item[4]) for item in plan]
            + [vm(2, rows, item[9] * columns) for item in plan]
            + [
                vm(max(item[4] for item in plan), 2 * rows),
                vm(chips // 2, row, columns),
                vm(chips // 2, row, columns),
                dma((sum(2 * max(1, item[4] // 768) + 2 for item in plan) + 2,)),
            ],
            after(code, *gate_arrays),
            *vectors[:2],
            *arrays,
            flops=4 * rows * columns * depth,
        )
        groups.append((Halving(kept, sent, chips, order), row, pieces, places))
        return kept

    def step(*which):
        return [
            groups[index][0].next()
            for index in which
            if index < len(groups) and groups[index][0].slots > 1
        ]

    by_z = (0, 2, 1)
    by_row = (0, 1, 2)

    def down_item(layer, up_kept, up_far, at_far):
        hidden, hidden_far = saved[layer][5], saved[layer][10]
        return (hidden, hidden_far, 0, 0, inner, up_kept, up_far, 0, at_far, 1, (3, layer))

    def up_items(layer, kept, far):
        acts, acts_far = saved[layer][4], saved[layer][9]
        return [
            (acts, acts_far, width, width, width, kept, far, 0, 0, strips_up, (2, layer)),
            (acts, acts_far, 0, 0, width, kept, far, inner // 2, inner // 2, 1, (1, layer)),
        ]

    def joint_item(layer, kept, far):
        packed, packed_far = saved[layer][2], saved[layer][3]
        at = 2 * width
        return (packed, packed_far, at, at, width, kept, far, 0, 0, strips_joint, (0, layer))

    preact_far = swap_cores(preact_sent)
    dq, own, sent, dq_sum = attention_back(last, low, [])
    received = swap_cores(sent)
    joints = []
    loose = []
    if native:
        first_far = saved[0][3]
        kept = start(by_z, [down_item(last, up_kept, first_far, 3 * width)], [dq])
        kept = start(by_z, up_items(last, preact_kept, preact_far), [kept])
        gate = [kept]
    else:
        up_far = saved[0][3][:, 3 * width :]
        loose.append((last, up_kept, up_far, preact_kept, preact_far))
    for above in reversed(range(1, layers)):
        layer = above - 1
        got = between(above, dq, own, received, dq_sum, vectors_two, middle_grad, gate)
        mix_kept, mix_sent, up_kept, up_sent, preact_kept, preact_sent, low, middle_grad = got[:8]
        vectors_one, vectors_two, up_sum_next = got[8:]
        mix_far, up_far = swap_cores(mix_sent), swap_cores(up_sent)
        preact_far = swap_cores(preact_sent)
        gate = [low]
        gate += step(0)
        if native:
            kept = start(
                by_z,
                [joint_item(above, mix_kept, mix_far), down_item(layer, up_kept, up_far, 0)],
                gate,
                (vectors_one, up_sum, above),
            )
            gate = [kept] + step(1)
            kept = start(by_row, up_items(layer, preact_kept, preact_far), gate)
            gate = [kept] + step(0)
        else:
            joints.append((above, mix_kept, mix_far, vectors_one, up_sum))
            loose.append((layer, up_kept, up_far, preact_kept, preact_far))
        up_sum = up_sum_next
        dq, own, sent, dq_sum = attention_back(layer, low, gate)
        received = swap_cores(sent)
        gate = [dq]
        gate += step(1, 0)
    got = project_back(0, dq, own, received, dq_sum, vectors_two, middle_grad, gate)
    mix_kept, mix_sent, input_gradient, vectors_one = got
    mix_far = swap_cores(mix_sent)
    if native:
        gate = [input_gradient] + step(2, 1)
        kept = start(
            by_row, [joint_item(0, mix_kept, mix_far)], gate, (vectors_one, up_sum, 0)
        )
    else:
        joints.append((0, mix_kept, mix_far, vectors_one, up_sum))
        return plain_outputs(
            output, input_gradient, saved, loose, joints, chips, core, layers, width, inner
        )

    half = part // 2
    outs = [
        full_shape(layers, half, 3 * width),
        full_shape(layers, half, width),
        full_shape(layers, half, inner),
        full_shape(layers, inner // chips // 2, width),
        full_shape(layers, half),
        full_shape(layers, half),
        full_shape(layers, 2, half),
        full_shape(layers, half),
        full_shape(layers, half),
        full_shape(layers, half),
        full_shape(layers, half),
        full_shape(layers, inner // chips // 2),
    ]

    def finish(some, gate_arrays):
        parts, pieces, places, group_rows, base = [], [], [], [], 0
        for halving, count, group_pieces, group_places in some:
            parts += halving.rest().parts
            pieces.append(tuple(group_pieces))
            group_rows.append(count)
            for place in group_places:
                if len(place) == 4:
                    size, index, layer, strips = place
                    places.append((base, size, index, layer, strips))
                    base += size * strips
                else:
                    places.append((base, 8, place[1]))
                    base += 16
        steps = len(parts) // len(some)
        if gate_arrays:
            parts[0] = after(parts[0], *gate_arrays)
        kept, sent = call(
            functools.partial(sum_kernel, pieces),
            (full_shape(base, columns),) * 2,
            [ANY] * len(parts),
            [vm(steps, count, columns) for count in group_rows]
            + [
                vm(max(group_rows), columns, kind=f32),
                vm(base, columns, kind=f32),
                vm(base, columns, kind=f32),
                dma((len(parts) + 2,)),
            ],
            *parts,
        )
        return kept, swap_cores(sent), places

    done = [finish(groups[:-2], ()), finish(groups[-2:], ())]
    final = call(
        functools.partial(place_kernel, [places for _, _, places in done]),
        outs,
        [ANY] * (2 * len(done)),
        [vm(*array.shape, kind=f32) for kept, far, _ in done for array in (kept, far)]
        + [dma((2 * len(done),))],
        *[array for kept, far, _ in done for array in (kept, far)],
        out_specs=(VMEM,) * len(outs),
    )
    joints, outputs, ups, downs, gain_one, shift_one, biases = final[:7]
    bias_out, gain_two, shift_two, bias_down, bias_up = final[7:]
    return (
        output[None],
        input_gradient[None],
        gain_one,
        shift_one,
        joints,
        biases,
        outputs,
        bias_out,
        gain_two,
        shift_two,
        ups,
        bias_up,
        downs,
        bias_down,
    )


def plain_outputs(
    output, input_gradient, saved, loose, joints, chips, core, layers, width, inner
):
    slots = slots_of_chips(chips, lax.axis_index("row").astype(jnp.int32), core)
    split = functools.partial(plain_sums, slots=slots, chips=chips, core=core)
    mats, vecs = [[None] * 4 for _ in range(layers)], [None] * layers
    for layer, up_kept, up_far, preact_kept, preact_far in loose:
        acts, hidden, acts_far, hidden_far = (saved[layer][index] for index in (4, 5, 9, 10))
        cut = inner // 2
        mats[layer][1] = split(
            acts[:, :width], acts_far[:, :width], preact_kept[:, cut:], preact_far[:, cut:]
        )
        mats[layer][2] = split(
            acts[:, width:], acts_far[:, width:], preact_kept[:, :cut], preact_far[:, :cut]
        )
        mats[layer][3] = split(hidden, hidden_far, up_kept, up_far)
    for layer, mix_kept, mix_far, vectors, up_sum in joints:
        packed, packed_far = saved[layer][2:4]
        window = slice(2 * width, 3 * width)
        mats[layer][0] = split(packed[:, window], packed_far[:, window], mix_kept, mix_far)
        vecs[layer] = [vectors[row] for row in range(8)] + [up_sum[0]]
    cuts = plain_vectors(
        [vector for layer in range(layers) for vector in vecs[layer]], slots, chips, core
    )

    def stacked(position):
        return jnp.stack([cuts[layer * 9 + position] for layer in range(layers)])

    def matrix(position):
        return jnp.stack([mats[layer][position] for layer in range(layers)])

    return (
        output[None],
        input_gradient[None],
        stacked(0),
        stacked(1),
        matrix(0),
        jnp.stack([stacked(2), stacked(3)], axis=1),
        matrix(1),
        stacked(4),
        stacked(5),
        stacked(6),
        matrix(2),
        stacked(8),
        matrix(3),
        stacked(7),
    )


def solution(mesh):
    chips = mesh.shape["row"]
    split = P("row", "tok", None)
    in_specs = (split, split, P("row", "tok"), P("row", "tok")) + (P(),) * 12
    vector = P(None, ("row", "tok"))
    table = P(None, ("row", "tok"), None)
    out_specs = (
        split,
        split,
        vector,
        vector,
        table,
        P(None, None, ("row", "tok")),
        table,
        vector,
        vector,
        vector,
        table,
        vector,
        table,
        vector,
    )

    def run(*arrays):
        return body(*arrays, chips=chips)

    return jax.shard_map(run, mesh=mesh, in_specs=in_specs, out_specs=out_specs, check_vma=False)
```

```python
import functools
import math

import jax
import jax.numpy as jnp
from jax import lax
from jax.experimental import pallas as pl
from jax.experimental.pallas import tpu as pltpu
from jax.sharding import PartitionSpec as P

epsilon = 1e-05
score_scale = 0.125
masked_score = -1e30
head_size = 64
lanes = 128
plan = {"F2": (), "jd": (), "u0": (), "B1b": (0,), "B2": (1,), "j0": (0, 2), "tail": (), "first": 1, "orders": "zzzrr", "done": 2}
forward_unroll = 1
backward_unroll = 1
mlp_unroll = 1
f32 = jnp.float32
bf16 = jnp.bfloat16
VMEM = pl.BlockSpec(memory_space=pltpu.VMEM)
SMEM = pl.BlockSpec(memory_space=pltpu.SMEM)
HBM = pl.BlockSpec(memory_space=pltpu.HBM)
ANY = pl.BlockSpec(memory_space=pl.ANY)


def shape(dims, kind):
    return jax.ShapeDtypeStruct(dims, kind)


def dot(left, right):
    return jnp.dot(left, right, preferred_element_type=f32)


def dot_nt(left, right):
    return lax.dot_general(left, right, (((1,), (1,)), ((), ())), preferred_element_type=f32)


def dot_tn(left, right):
    return lax.dot_general(left, right, (((0,), (0,)), ((), ())), preferred_element_type=f32)


def normalize(stream):
    centre = stream - jnp.mean(stream, axis=-1, keepdims=True)
    inverse = lax.rsqrt(jnp.mean(centre * centre, axis=-1, keepdims=True) + epsilon)
    return centre * inverse, inverse


def norm_back(upstream, unit, inverse, gain):
    scaled = upstream * gain
    return inverse * (
        scaled
        - jnp.mean(scaled, axis=-1, keepdims=True)
        - unit * jnp.mean(scaled * unit, axis=-1, keepdims=True)
    )


def column_sum(array):
    return jnp.sum(array, axis=0, keepdims=True)


def gelu_and_slope(x):
    size = jnp.abs(x)
    t = 1.0 / (1.0 + (0.3275911 * 0.7071067811865476) * size)
    bell = jnp.exp(-0.5 * (x * x))
    series = t * (
        0.5 * 0.254829592
        + t
        * (
            0.5 * -0.284496736
            + t * (0.5 * 1.421413741 + t * (0.5 * -1.453152027 + t * (0.5 * 1.061405429)))
        )
    )
    tail = series * bell
    share = jnp.where(x >= 0, 1.0 - tail, tail)
    return x * share, share + x * (bell * 0.3989422804014327)


class Copies:
    def __init__(self, sems):
        self.sems = sems
        self.used = 0
        self.out = []

    def bring(self, source, target):
        copy = pltpu.make_async_copy(source, target, self.sems.at[self.used])
        self.used += 1
        copy.start()
        return copy

    def send(self, source, target):
        self.out.append(self.bring(source, target))

    def thirds(self, source, target, order):
        third = target.shape[1] // 3
        windows = [pl.ds(index * third, third) for index in order]
        return [self.bring(source.at[:, window], target.at[:, window]) for window in windows]

    def finish(self):
        for copy in self.out:
            copy.wait()


def emit_project(stream, layer, gain, shift, bias, weight, waits, normed_ref, query_ref, kv_ref):
    width = stream.shape[1]
    unit, _ = normalize(stream)
    normed_ref[...] = (unit * gain[layer : layer + 1] + shift[layer : layer + 1]).astype(bf16)
    normed = normed_ref[...]
    waits[0].wait()
    kv_ref[:, :width] = dot(normed, weight[:, width : 2 * width]).astype(bf16)
    waits[1].wait()
    kv_ref[:, width:] = (
        dot(normed, weight[:, 2 * width :]) + bias[layer, 1:2]
    ).astype(bf16)
    waits[2].wait()
    queries = (dot(normed, weight[:, :width]) + bias[layer, 0:1]).astype(bf16)
    query_ref[...] = queries * jnp.asarray(score_scale, bf16)


def head_masks():
    lane = lax.broadcasted_iota(jnp.int32, (1, lanes), 1)
    return (lane < head_size, lane >= head_size)


def emit_mask(rows, code_ref, far_ref, mask_ref):
    own = code_ref[...].astype(f32)
    diagonal = lax.broadcasted_iota(jnp.int32, (rows, rows), 0) == lax.broadcasted_iota(
        jnp.int32, (rows, rows), 1
    )
    column = jnp.sum(jnp.where(diagonal, own, 0.0), axis=1, keepdims=True)
    mask_ref[:, :rows] = jnp.where(column == own, 0.0, masked_score)
    mask_ref[:, rows:] = jnp.where(column == far_ref[...].astype(f32), 0.0, masked_score)


def emit_attention(width, query_ref, kv_ref, mask_ref, attended_ref, soft_ref):
    rows = query_ref.shape[0]
    masks = head_masks()
    zero = jnp.zeros((), bf16)

    def one_pair(pair, carry):
        columns = pl.ds(pl.multiple_of(pair * lanes, lanes), lanes)
        value_columns = pl.ds(pl.multiple_of(width + pair * lanes, lanes), lanes)
        queries = query_ref[:, columns]
        both = jnp.concatenate([jnp.where(mask, queries, zero) for mask in masks], axis=0)
        scores = dot_nt(both, kv_ref[:, columns])
        softs = []
        for side in range(2):
            own = scores[side * rows : (side + 1) * rows] + mask_ref[...]
            exponent = jnp.exp(own - jnp.max(own, axis=-1, keepdims=True))
            soft = exponent * (1.0 / jnp.sum(exponent, axis=-1, keepdims=True))
            softs.append(soft.astype(bf16))
            soft_ref[pair * 2 + side] = softs[-1]
        total = dot(jnp.concatenate(softs, axis=0), kv_ref[:, value_columns])
        attended_ref[:, columns] = jnp.where(masks[0], total[:rows], total[rows:]).astype(bf16)
        return carry

    lax.fori_loop(0, width // lanes, one_pair, 0, unroll=forward_unroll)


def emit_attention_back(
    width, query_ref, kv_ref, soft_ref, wait_soft, grad_ref, dq_ref, dq_sum, own_ref, sent_ref
):
    rows = query_ref.shape[0]
    masks = head_masks()
    zero = jnp.zeros((), bf16)
    def one_pair(pair, carry):
        wait_soft(pair)
        columns = pl.ds(pl.multiple_of(pair * lanes, lanes), lanes)
        value_columns = pl.ds(pl.multiple_of(width + pair * lanes, lanes), lanes)
        queries = query_ref[:, columns]
        grads = grad_ref[:, columns]
        keys = kv_ref[:, columns]
        own_grads = [jnp.where(mask, grads, zero) for mask in masks]
        soft_grads = dot_nt(jnp.concatenate(own_grads, axis=0), kv_ref[:, value_columns])
        dq = jnp.zeros((rows, lanes), f32)
        dk = jnp.zeros((2 * rows, lanes), f32)
        dv = jnp.zeros((2 * rows, lanes), f32)
        for side in range(2):
            soft_low = soft_ref[pair * 2 + side]
            soft = soft_low.astype(f32)
            soft_grad = soft_grads[side * rows : (side + 1) * rows]
            delta = jnp.sum(soft_grad * soft, axis=-1, keepdims=True)
            score_grad = (soft * (soft_grad - delta)).astype(bf16)
            dq += dot(score_grad, jnp.where(masks[side], keys, zero))
            dk += dot_tn(score_grad, jnp.where(masks[side], queries, zero))
            dv += dot_tn(soft_low, own_grads[side])
        dq = dq * score_scale
        dq_ref[:, columns] = dq.astype(bf16)
        dq_sum[0:1, columns] = column_sum(dq)
        own_ref[:, columns] = dk[:rows]
        own_ref[:, value_columns] = dv[:rows]
        sent_ref[:, columns] = dk[rows:].astype(bf16)
        sent_ref[:, value_columns] = dv[rows:].astype(bf16)
        return carry

    lax.fori_loop(0, width // lanes, one_pair, 0, unroll=backward_unroll)


def project_kernel(
    gain, shift, bias, tokens_hbm, weight_hbm, grad_hbm,
    query_hbm, packed_hbm, kept_hbm,
    tokens, weight, grad, normed, query, kv, sems,
):
    copies = Copies(sems)
    width = tokens.shape[1]
    half = width // 2
    first = copies.bring(tokens_hbm, tokens)
    third = copies.bring(grad_hbm, grad)
    thirds = copies.thirds(weight_hbm.at[0], weight, (1, 2, 0))
    core = lax.axis_index("tok")
    first.wait()
    third.wait()
    copies.send(
        grad.at[:, pl.ds(pl.multiple_of((1 - core) * half, half), half)],
        packed_hbm.at[:, pl.ds(3 * width, half)],
    )
    copies.send(grad.at[:, pl.ds(pl.multiple_of(core * half, half), half)], kept_hbm)
    emit_project(tokens[...].astype(f32), 0, gain, shift, bias, weight, thirds, normed, query, kv)
    copies.send(kv, packed_hbm.at[:, pl.ds(0, 2 * width)])
    copies.send(normed, packed_hbm.at[:, pl.ds(2 * width, width)])
    copies.send(query, query_hbm)
    copies.finish()


def emit_upper_half(layer, stream, output_weight, bias, gain, shift, acts, middle_ref):
    width = stream.shape[1]
    middle = stream + dot(acts[:, :width], output_weight[...]) + bias[layer : layer + 1]
    middle_ref[...] = middle
    unit, _ = normalize(middle)
    acts[:, width:] = (unit * gain[layer : layer + 1] + shift[layer : layer + 1]).astype(bf16)


def middle_kernel(
    layer, code, code_far, output_bias, gain, shift, up_bias,
    down_bias, next_gain, next_shift, joint_bias,
    stream_hbm, query_hbm, packed_hbm, far_hbm, output_hbm, up_hbm, down_hbm, joint_hbm,
    acts_hbm, hidden_hbm, soft_hbm, middle_hbm, slope_hbm,
    stream_next_hbm, query_next_hbm, packed_next_hbm,
    stream_ref, query, kv, mask, acts, hidden_ref, soft, middle_ref, slope,
    output_weight, up_weight, down_weight, joint_weight, total, normed, query_next, kv_next, sems,
):
    copies = Copies(sems)
    rows, width = query.shape
    inner = up_weight.shape[1]
    kv_window = pl.ds(0, 2 * width)
    wait = [
        copies.bring(query_hbm, query),
        copies.bring(packed_hbm.at[:, kv_window], kv.at[pl.ds(0, rows)]),
        copies.bring(far_hbm.at[:, kv_window], kv.at[pl.ds(rows, rows)]),
        copies.bring(stream_hbm, stream_ref),
    ]
    emit_mask(rows, code, code_far, mask)
    for copy in wait[:3]:
        copy.wait()
    output_copy = copies.bring(output_hbm.at[layer], output_weight)
    up_copy = copies.bring(up_hbm.at[layer], up_weight)
    down_copy = copies.bring(down_hbm.at[layer], down_weight)
    thirds = copies.thirds(joint_hbm.at[layer + 1], joint_weight, (1, 2, 0))
    emit_attention(width, query, kv, mask, acts, soft)
    copies.send(soft, soft_hbm)
    wait[3].wait()
    output_copy.wait()
    emit_upper_half(
        layer,
        stream_ref[...].astype(f32),
        output_weight,
        output_bias,
        gain,
        shift,
        acts,
        middle_ref,
    )
    copies.send(acts, acts_hbm)
    copies.send(middle_ref, middle_hbm)
    up_copy.wait()
    down_copy.wait()
    total[...] = middle_ref[...] + down_bias[layer : layer + 1]
    chunk = width

    def one_chunk(index, carry):
        columns = pl.ds(pl.multiple_of(index * chunk, chunk), chunk)
        preact = dot(acts[:, width:], up_weight[:, columns])
        hidden, rate = gelu_and_slope(preact + up_bias[layer : layer + 1, columns])
        hidden_ref[:, columns] = hidden.astype(bf16)
        slope[:, columns] = rate.astype(bf16)
        total[...] += dot(hidden_ref[:, columns], down_weight[columns, :])
        return carry

    lax.fori_loop(0, inner // chunk, one_chunk, 0, unroll=mlp_unroll)
    copies.send(hidden_ref, hidden_hbm)
    copies.send(slope, slope_hbm)
    copies.send(total, stream_next_hbm)
    emit_project(
        total[...],
        layer + 1,
        next_gain,
        next_shift,
        joint_bias,
        joint_weight,
        thirds,
        normed,
        query_next,
        kv_next,
    )
    copies.send(kv_next, packed_next_hbm.at[:, kv_window])
    copies.send(normed, packed_next_hbm.at[:, pl.ds(2 * width, width)])
    copies.send(query_next, query_next_hbm)
    copies.finish()


def emit_middle_grad(layer, core, upstream, middle, total, gain, vectors, low, grad_ref, grads):
    width = middle.shape[1]
    columns = width // 2
    unit, inverse = normalize(middle)
    normed_grad = total[...]
    vectors[5:6] = column_sum(normed_grad * unit)
    vectors[6:7] = column_sum(normed_grad)
    middle_grad = upstream + norm_back(normed_grad, unit, inverse, gain[layer : layer + 1])
    vectors[4:5] = column_sum(middle_grad)
    grad_ref[...] = middle_grad
    low[...] = middle_grad.astype(bf16)
    behind = grads.shape[2] - columns
    for turn, side in enumerate((1 - core, core)):
        grads[turn, :, behind:] = low[:, pl.ds(pl.multiple_of(side * columns, lanes), columns)]


def turn_kernel(
    layer, code, code_far, output_bias, gain, shift, up_bias, down_bias,
    stream_hbm, query_hbm, packed_hbm, far_hbm, upstream_hbm, output_hbm, up_hbm, down_hbm,
    acts_hbm, hidden_hbm, soft_hbm, result_hbm, kept_hbm, sent_hbm, low_hbm, grad_hbm,
    vectors, up_sum,
    stream_ref, query, kv, mask, acts, hidden_ref, soft, middle_ref, upstream_ref,
    grads, low, grad_ref, result, result_low, total,
    output_weight, up_weight, down_weight, sems,
):
    copies = Copies(sems)
    rows, width = query.shape
    inner = up_weight.shape[1]
    core = lax.axis_index("tok")
    kv_window = pl.ds(0, 2 * width)
    wait = [
        copies.bring(query_hbm, query),
        copies.bring(packed_hbm.at[:, kv_window], kv.at[pl.ds(0, rows)]),
        copies.bring(far_hbm.at[:, kv_window], kv.at[pl.ds(rows, rows)]),
        copies.bring(stream_hbm, stream_ref),
    ]
    emit_mask(rows, code, code_far, mask)
    for copy in wait[:3]:
        copy.wait()
    output_copy = copies.bring(output_hbm.at[layer], output_weight)
    upstream_copy = copies.bring(upstream_hbm, upstream_ref)
    up_copy = copies.bring(up_hbm.at[layer], up_weight)
    down_copy = copies.bring(down_hbm.at[layer], down_weight)
    emit_attention(width, query, kv, mask, acts, soft)
    copies.send(soft, soft_hbm)
    wait[3].wait()
    output_copy.wait()
    emit_upper_half(
        layer,
        stream_ref[...].astype(f32),
        output_weight,
        output_bias,
        gain,
        shift,
        acts,
        middle_ref,
    )
    copies.send(acts, acts_hbm)
    upstream_copy.wait()
    upstream = upstream_ref[...].astype(f32)
    low[...] = upstream.astype(bf16)
    vectors[0:4] = jnp.zeros_like(vectors[0:4])
    vectors[7:8] = column_sum(upstream)
    up_sum[...] = jnp.zeros_like(up_sum)
    result[...] = middle_ref[...] + down_bias[layer : layer + 1]
    total[...] = jnp.zeros_like(total)
    up_copy.wait()
    down_copy.wait()
    chunk = width
    half = inner // 2

    def one_chunk(index, carry):
        turn = index // (half // chunk)
        at = pl.multiple_of(index % (half // chunk) * chunk, chunk)
        side = jnp.where(turn == 0, 1 - core, core)
        columns = pl.ds(pl.multiple_of(side * half + at, chunk), chunk)
        preact = dot(acts[:, width:], up_weight[:, columns])
        hidden, rate = gelu_and_slope(preact + up_bias[layer : layer + 1, columns])
        hidden_ref[:, columns] = hidden.astype(bf16)
        result[...] += dot(hidden_ref[:, columns], down_weight[columns, :])
        preact_grad = dot_nt(low[...], down_weight[columns, :]) * rate
        up_sum[0:1, columns] = column_sum(preact_grad)
        grads[turn, :, pl.ds(at, chunk)] = preact_grad.astype(bf16)
        total[...] += dot_nt(preact_grad.astype(bf16), up_weight[:, columns])
        return carry

    lax.fori_loop(0, inner // chunk, one_chunk, 0, unroll=mlp_unroll)
    copies.send(hidden_ref, hidden_hbm)
    result_low[...] = result[...].astype(bf16)
    copies.send(result_low, result_hbm)
    emit_middle_grad(
        layer,
        core,
        upstream_ref[...].astype(f32),
        middle_ref[...],
        total,
        gain,
        vectors,
        low,
        grad_ref,
        grads,
    )
    copies.send(low, low_hbm)
    copies.send(grads.at[0], sent_hbm)
    copies.send(grads.at[1], kept_hbm)
    copies.send(grad_ref, grad_hbm)
    copies.finish()


def attention_back_kernel(
    layer, low_hbm, query_hbm, packed_hbm, far_hbm, soft_hbm, output_hbm,
    dq_hbm, own_hbm, sent_hbm, dq_sum,
    low, query, kv, soft, attended_grad, output_weight, dq, own, sent, soft_sems, sems,
):
    copies = Copies(sems)
    rows, width = low.shape
    kv_window = pl.ds(0, 2 * width)
    wait = [
        copies.bring(low_hbm, low),
        copies.bring(output_hbm.at[layer], output_weight),
        copies.bring(query_hbm, query),
        copies.bring(packed_hbm.at[:, kv_window], kv.at[pl.ds(0, rows)]),
        copies.bring(far_hbm.at[:, kv_window], kv.at[pl.ds(rows, rows)]),
    ]

    def soft_copy(pair):
        two = pl.ds(pair * 2, 2)
        return pltpu.make_async_copy(soft_hbm.at[two], soft.at[two], soft_sems.at[pair])

    for pair in range(width // lanes):
        soft_copy(pair).start()
    dq_sum[...] = jnp.zeros_like(dq_sum)
    wait[0].wait()
    wait[1].wait()
    attended_grad[...] = dot_nt(low[...], output_weight[...]).astype(bf16)
    for copy in wait[2:]:
        copy.wait()
    emit_attention_back(
        width,
        query,
        kv,
        soft,
        lambda pair: soft_copy(pair).wait(),
        attended_grad,
        dq,
        dq_sum,
        own,
        sent,
    )
    copies.send(sent, sent_hbm)
    copies.send(dq, dq_hbm)
    copies.send(own, own_hbm)
    copies.finish()


def emit_project_back(
    layer, copies, core, wait, thirds, dq_sum, vectors_two, gain, mixed, own, received,
    stream_ref, grad_ref, joint_weight, kept_hbm, sent_hbm, vectors,
):
    rows, width = stream_ref.shape
    wide = 3 * width // 2
    vectors[4:8] = vectors_two[4:8]
    vectors[2:3] = dq_sum[0:1]
    for copy in wait[:3]:
        copy.wait()
    kv_grad = own[...] + received[...].astype(f32)
    mixed[:, width:] = kv_grad.astype(bf16)
    vectors[3:4] = column_sum(kv_grad[:, width:])
    for side, target in ((1 - core, sent_hbm), (core, kept_hbm)):
        copies.send(mixed.at[:, pl.ds(pl.multiple_of(side * wide, lanes), wide)], target)
    normed_grad = jnp.zeros((rows, width), f32)
    for index, copy in enumerate(thirds):
        copy.wait()
        window = slice(index * width, (index + 1) * width)
        normed_grad += dot_nt(mixed[:, window], joint_weight[:, window])
    wait[3].wait()
    unit, inverse = normalize(stream_ref[...].astype(f32))
    vectors[0:1] = column_sum(normed_grad * unit)
    vectors[1:2] = column_sum(normed_grad)
    wait[4].wait()
    return grad_ref[...] + norm_back(normed_grad, unit, inverse, gain[layer : layer + 1])


def project_back_kernel(
    layer, gate, gain, dq_sum, vectors_two,
    dq_hbm, own_hbm, received_hbm, stream_hbm, grad_hbm, joint_hbm,
    kept_hbm, sent_hbm, upstream_hbm, vectors,
    own, received, stream_ref, grad_ref, mixed, upstream, joint_weight, sems,
):
    copies = Copies(sems)
    width = stream_ref.shape[1]
    wait = [
        copies.bring(dq_hbm, mixed.at[:, pl.ds(0, width)]),
        copies.bring(own_hbm, own),
        copies.bring(received_hbm, received),
        copies.bring(stream_hbm, stream_ref),
        copies.bring(grad_hbm, grad_ref),
    ]
    thirds = copies.thirds(joint_hbm.at[layer], joint_weight, (0, 1, 2))
    upstream[...] = emit_project_back(
        layer, copies, lax.axis_index("tok"), wait, thirds, dq_sum, vectors_two, gain, mixed,
        own, received, stream_ref, grad_ref, joint_weight, kept_hbm, sent_hbm, vectors,
    )
    copies.send(upstream, upstream_hbm)
    copies.finish()


def between_kernel(
    above, gate, gain, second_gain, dq_sum, vectors_two,
    dq_hbm, own_hbm, received_hbm, stream_hbm, grad_hbm, slope_hbm, middle_hbm,
    joint_hbm, down_hbm, up_hbm,
    mix_kept_hbm, mix_sent_hbm, up_kept_hbm, up_sent_hbm, kept_hbm, sent_hbm, low_hbm,
    grad_next_hbm, vectors, vectors_next, up_sum,
    own, received, stream_ref, grad_ref, mixed, upstream, low, slope, middle_ref,
    grads, low_next, grad_next, total, joint_weight, down_weight, up_weight, weight_sems, sems,
):
    copies = Copies(sems)
    rows, width = stream_ref.shape
    inner = up_weight.shape[1]
    layer = above - 1
    core = lax.axis_index("tok")
    wait = [
        copies.bring(dq_hbm, mixed.at[:, pl.ds(0, width)]),
        copies.bring(own_hbm, own),
        copies.bring(received_hbm, received),
        copies.bring(stream_hbm, stream_ref),
        copies.bring(grad_hbm, grad_ref),
    ]
    thirds = copies.thirds(joint_hbm.at[above], joint_weight, (0, 1, 2))
    chunk = width
    half = inner // 2

    def window_of(index):
        turn = index // (half // chunk)
        at = pl.multiple_of(index % (half // chunk) * chunk, chunk)
        side = jnp.where(turn == 0, 1 - core, core)
        return turn, at, pl.ds(pl.multiple_of(side * half + at, chunk), chunk)

    def weight_copies(index):
        window = window_of(index)[2]
        return (
            pltpu.make_async_copy(
                down_hbm.at[layer, window], down_weight.at[window], weight_sems.at[0, index]
            ),
            pltpu.make_async_copy(
                up_hbm.at[layer, :, window], up_weight.at[:, window], weight_sems.at[1, index]
            ),
        )

    slope_copy = copies.bring(slope_hbm, slope)
    for index in range(inner // chunk):
        for copy in weight_copies(index):
            copy.start()
    middle_copy = copies.bring(middle_hbm, middle_ref)
    below = emit_project_back(
        above, copies, core, wait, thirds, dq_sum, vectors_two, gain, mixed,
        own, received, stream_ref, grad_ref, joint_weight, mix_kept_hbm, mix_sent_hbm, vectors,
    )
    upstream[...] = below
    low[...] = below.astype(bf16)
    columns = width // 2
    for side, target in ((1 - core, up_sent_hbm), (core, up_kept_hbm)):
        copies.send(low.at[:, pl.ds(pl.multiple_of(side * columns, lanes), columns)], target)
    vectors_next[0:4] = jnp.zeros_like(vectors_next[0:4])
    vectors_next[7:8] = column_sum(below)
    up_sum[...] = jnp.zeros_like(up_sum)
    total[...] = jnp.zeros_like(total)
    slope_copy.wait()

    def one_chunk(index, carry):
        turn, at, window = window_of(index)
        for copy in weight_copies(index):
            copy.wait()
        preact_grad = dot_nt(low[...], down_weight[window, :]) * slope[:, window].astype(f32)
        up_sum[0:1, window] = column_sum(preact_grad)
        grads[turn, :, pl.ds(at, chunk)] = preact_grad.astype(bf16)
        total[...] += dot_nt(preact_grad.astype(bf16), up_weight[:, window])
        return carry

    lax.fori_loop(0, inner // chunk, one_chunk, 0, unroll=mlp_unroll)
    middle_copy.wait()
    emit_middle_grad(
        layer,
        core,
        upstream[...],
        middle_ref[...],
        total,
        second_gain,
        vectors_next,
        low_next,
        grad_next,
        grads,
    )
    copies.send(low_next, low_hbm)
    copies.send(grads.at[0], sent_hbm)
    copies.send(grads.at[1], kept_hbm)
    copies.send(grad_next, grad_next_hbm)
    copies.finish()


def weight_kernel(chips, order, plan, vector_row, *refs):
    core, me = lax.axis_index("tok"), lax.axis_index("row")
    refs = refs[1:]
    if vector_row:
        vectors, up_sum = refs[:2]
        refs = refs[2:]
    count = 1 + max(max(item[0], item[1], item[5], item[6]) for item in plan)
    arrays = refs[:count]
    kept_hbm, sent_hbm = refs[count : count + 2]
    refs = refs[count + 2 :]
    lefts, rights = refs[: len(plan)], refs[len(plan) : 2 * len(plan)]
    block, slot_sems, sems = refs[2 * len(plan) :]
    copies = Copies(sems)
    columns = block.shape[2]
    half = chips // 2
    steps = chips.bit_length() - 1
    waits = []
    for item, left, right in zip(plan, lefts, rights):
        own, far, at, at_far, size, right_own, right_far, right_at, right_at_far, strips, row = item
        piece = min(size, 768)
        wait = []
        for first in range(0, size, piece):
            for side, array, start in ((0, own, at), (1, far, at_far)):
                wait.append(
                    copies.bring(
                        arrays[array].at[:, pl.ds(start + first, piece)],
                        left.at[side, :, pl.ds(first, piece)],
                    )
                )
        for side, array, start in ((0, right_own, right_at), (1, right_far, right_at_far)):
            window = pl.ds(start, strips * columns)
            wait.append(copies.bring(arrays[array].at[:, window], right.at[side]))
        waits.append(wait)
    slots = []
    for chip in range(chips):
        apart = chip ^ me
        slot = 0
        for step in range(steps):
            bit = jnp.where(core == 0, step_bit(order, step, 0), step_bit(order, step, 1))
            slot = slot * 2 + ((apart >> bit) & 1)
        slots.append(slot)
    outgoing = []

    def send_rows(chip, row, count):
        sem = slot_sems.at[len(outgoing)]
        window = pl.ds(row, count)
        source = block.at[slots[chip], window]

        @pl.when(slots[chip] >= half)
        def _():
            target = sent_hbm.at[slots[chip] - half, window]
            pltpu.make_async_copy(source, target, sem).start()

        @pl.when(slots[chip] < half)
        def _():
            pltpu.make_async_copy(source, kept_hbm.at[slots[chip], window], sem).start()

        outgoing.append(pltpu.make_async_copy(source, kept_hbm.at[0, window], sem))

    if vector_row:
        depth = 16
        width, inner = vectors.shape[1], up_sum.shape[1]

        def one_slot(slot, carry):
            apart = sum(
                ((slot >> (steps - 1 - step)) & 1)
                << jnp.where(core == 0, step_bit(order, step, 0), step_bit(order, step, 1))
                for step in range(steps)
            )
            chip = me ^ apart
            short = pltpu.roll(vectors[...], width - chip * (width // chips), axis=1)
            wide = pltpu.roll(up_sum[...], inner - chip * (inner // chips), axis=1)
            block[slot, vector_row : vector_row + depth, :] = jnp.concatenate(
                [short[:, :columns], wide[:, :columns]], axis=0
            ).astype(bf16)
            return carry

        lax.fori_loop(0, chips, one_slot, 0)
    for item, left, right, wait in zip(plan, lefts, rights, waits):
        size, strips, row = item[4], item[9], item[10]
        part = size // chips
        piece = min(size, 768)
        for first in range(0, size, piece):
            flipped = []
            for side in range(2):
                wait[first // piece * 2 + side].wait()
                flipped.append(left[side, :, first : first + piece].T)
            if not first:
                wait[-2].wait()
                wait[-1].wait()
            for strip in range(strips):
                window = slice(strip * columns, (strip + 1) * columns)
                product = dot(flipped[0], right[0, :, window]) + dot(
                    flipped[1], right[1, :, window]
                )
                product = product.astype(bf16)
                for cut in range(0, piece, part):
                    slot = slots[(first + cut) // part]
                    block[slot, row + strip * part : row + (strip + 1) * part, :] = product[
                        cut : cut + part
                    ]
            for cut in range(0, piece, part):
                with_them = vector_row == row + strips * part
                send_rows(
                    (first + cut) // part, row, strips * part + (depth if with_them else 0)
                )
    for copy in outgoing:
        copy.wait()


def sum_kernel(groups, *refs):
    count = len(groups)
    steps = (len(refs) - 2 - count - 4) // count
    inputs = refs[: count * steps]
    kept_hbm, sent_hbm = refs[count * steps : 2 + count * steps]
    buffers = refs[2 + count * steps : 2 + count * steps + count]
    total, kept, sent, sems = refs[2 + count * steps + count :]
    copies = Copies(sems)
    core = lax.axis_index("tok")
    waits = [
        [
            copies.bring(inputs[g * steps + step].at[0], buffers[g].at[step])
            for step in range(steps)
        ]
        for g in range(count)
    ]
    out = 0
    for g, pieces in enumerate(groups):
        for copy in waits[g]:
            copy.wait()
        rows = buffers[g].shape[1]
        value = buffers[g][0].astype(f32)
        for step in range(1, steps):
            value += buffers[g][step].astype(f32)
        total[:rows] = value
        for row, part, repeats in pieces:
            if not repeats:
                kept[out : out + part] = total[row : row + part]
                sent[out : out + part] = total[row : row + part]
                out += part
            for repeat in range(repeats):
                first = row + repeat * 2 * part
                kept[out : out + part] = total[pl.ds(pl.multiple_of(first + core * part, 8), part)]
                sent[out : out + part] = total[
                    pl.ds(pl.multiple_of(first + (1 - core) * part, 8), part)
                ]
                out += part
    copies.send(sent, sent_hbm)
    copies.send(kept, kept_hbm)
    copies.finish()


def place_kernel(places, *refs):
    count = len(places)
    inputs, outputs = refs[: 2 * count], refs[2 * count : -2 * count - 1]
    buffers, sems = refs[-2 * count - 1 : -1], refs[-1]
    copies = Copies(sems)
    wait = [copies.bring(source, target) for source, target in zip(inputs, buffers)]
    core = lax.axis_index("tok")
    for number, group in enumerate(places):
        kept, far = buffers[2 * number : 2 * number + 2]
        columns = kept.shape[1]
        for copy in wait[2 * number : 2 * number + 2]:
            copy.wait()
        for place in group:
            if len(place) == 5:
                first, part, index, layer, strips = place
                for strip in range(strips):
                    rows = slice(first + strip * part, first + (strip + 1) * part)
                    for side, source in ((core, kept), (1 - core, far)):
                        at = pl.multiple_of(side * (strips * columns) + strip * columns, lanes)
                        outputs[index][layer, :, pl.ds(at, columns)] = source[rows, :]
            else:
                first, half, layer = place
                short = kept[first : first + half] + far[first : first + half]
                wide = kept[first + half : first + 2 * half] + far[first + half : first + 2 * half]
                size, wide_size = outputs[4].shape[1], outputs[11].shape[1]
                short = pltpu.roll(short, columns - core * size, axis=1)
                wide = pltpu.roll(wide, columns - core * wide_size, axis=1)
                outputs[4][layer : layer + 1] = short[0:1, :size]
                outputs[5][layer : layer + 1] = short[1:2, :size]
                outputs[6][layer] = short[2:4, :size]
                for row, index in ((4, 7), (5, 8), (6, 9), (7, 10)):
                    outputs[index][layer : layer + 1] = short[row : row + 1, :size]
                outputs[11][layer : layer + 1] = wide[0:1, :wide_size]


def call(kernel, outs, ins, scratch, *arrays, flops=0, out_specs=None, limit=58):
    out_specs = tuple(out_specs or (ANY for _ in outs))
    count = sum(math.prod(a.shape) * a.dtype.itemsize for a in list(arrays) + list(outs))
    held = [kept for kept in scratch if kept.memory_space == pltpu.VMEM]
    held += [a for a, spec in zip(list(arrays) + list(outs), list(ins) + list(out_specs)) if spec is VMEM]
    need = sum(math.prod(a.shape) * a.dtype.itemsize for a in held) + (8 << 20)
    return pl.pallas_call(
        kernel,
        out_shape=tuple(outs),
        in_specs=list(ins),
        out_specs=out_specs,
        scratch_shapes=scratch,
        compiler_params=pltpu.CompilerParams(vmem_limit_bytes=max(need, limit << 20)),
        cost_estimate=pl.CostEstimate(flops=flops, bytes_accessed=count, transcendentals=0),
    )(*arrays)


def swap_cores(array):
    return lax.ppermute(array, "tok", [(0, 1), (1, 0)])


def after(array, *others):
    return lax.optimization_barrier((array,) + others)[0]


def step_bit(order, step, core):
    bit = order[step] if step < len(order) else step
    return bit ^ core if bit < 2 else bit


def distance(chips, order, slot, core):
    steps = chips.bit_length() - 1
    bits = [step_bit(order, step, core) for step in range(steps) if slot >> (steps - 1 - step) & 1]
    return sum(1 << bit for bit in bits)


def step_pairs(chips, order, step):
    return [
        (chip * 2 + core, (chip ^ (1 << step_bit(order, step, core))) * 2 + core)
        for chip in range(chips)
        for core in range(2)
    ]


class Halving:
    def __init__(self, kept, sent, chips, order=(0, 1)):
        self.chips = chips
        self.order = order
        self.slots = chips // 2
        self.step = 0
        self.parts = [kept]
        self.move(sent)

    def move(self, sent):
        pairs = step_pairs(self.chips, self.order, self.step)
        self.parts.append(lax.ppermute(sent, ("row", "tok"), pairs))
        self.step += 1

    def next(self, before=None):
        half = self.slots // 2
        sent = sum(part[half : self.slots].astype(f32) for part in self.parts)
        sent = sent.astype(self.parts[0].dtype)
        if before is not None:
            sent = after(sent, before)
        self.slots = half
        self.move(sent)
        return sent

    def rest(self):
        while self.slots > 1:
            self.next()
        return self


def slots_of_chips(chips, me, core):
    sides = [[distance(chips, (0, 1), slot, side) for slot in range(chips)] for side in range(2)]
    return me ^ jnp.asarray(sides, jnp.int32)[core]


def plain_sums(left, left_far, right, right_far, slots, chips, core):
    product = dot_tn(
        jnp.concatenate([left, left_far], axis=0), jnp.concatenate([right, right_far], axis=0)
    ).astype(bf16)
    product = product.reshape(chips, -1, product.shape[1])[slots]
    done = Halving(product[: chips // 2], product[chips // 2 :], chips).rest()
    total = sum(part[0].astype(f32) for part in done.parts)
    total = total.reshape(2, -1, total.shape[1])
    kept = lax.dynamic_index_in_dim(total, core, 0, keepdims=False)
    other = swap_cores(lax.dynamic_index_in_dim(total, 1 - core, 0, keepdims=False))
    return jnp.where(
        core == 0,
        jnp.concatenate([kept, other], axis=1),
        jnp.concatenate([other, kept], axis=1),
    )


def plain_vectors(vectors, slots, chips, core):
    pieces = [vector.reshape(chips, 2, -1) for vector in vectors]
    packed = jnp.concatenate(pieces, axis=2)
    sent = lax.dynamic_index_in_dim(packed, 1 - core, 1, keepdims=False)
    packed = lax.dynamic_index_in_dim(packed, core, 1, keepdims=False) + swap_cores(sent)
    packed = packed[slots]
    done = Halving(packed[: chips // 2], packed[chips // 2 :], chips).rest()
    packed = sum(part[0] for part in done.parts)
    cuts, at = [], 0
    for piece in pieces:
        cuts.append(packed[at : at + piece.shape[2]])
        at += piece.shape[2]
    return cuts


def body(
    tokens,
    cotangent,
    segment_ids,
    valid,
    first_gain,
    first_shift,
    joint_weight,
    joint_bias,
    output_weight,
    output_bias,
    second_gain,
    second_shift,
    up_weight,
    up_bias,
    down_weight,
    down_bias,
    chips,
):
    layers, width = joint_weight.shape[:2]
    inner = up_weight.shape[2]
    heads = width // head_size
    rows = tokens.shape[1]
    columns = width // 2
    wide = 3 * columns
    part = width // chips
    native = part % 48 == 0
    strips_up = inner // 2 // columns
    strips_joint = wide // columns
    core = lax.axis_index("tok").astype(jnp.int32)
    code = segment_ids * 2 + valid
    code_far = swap_cores(code)
    dma = pltpu.SemaphoreType.DMA
    weights = (joint_weight, output_weight, up_weight, down_weight)

    def vm(*sizes, kind=bf16):
        return pltpu.VMEM(sizes, kind)

    def low_shape(*sizes):
        return shape(sizes, bf16)

    def full_shape(*sizes):
        return shape(sizes, f32)

    def places_of(arrays):
        return [HBM if any(array is weight for weight in weights) else ANY for array in arrays]

    def wired(kernel, small, large, outs, scratch, flops, vector_outs=0):
        return call(
            kernel,
            outs,
            [VMEM] * len(small) + places_of(large),
            scratch,
            *small,
            *large,
            flops=flops,
            out_specs=[ANY] * (len(outs) - vector_outs) + [VMEM] * vector_outs,
        )

    tokens = tokens[0]
    cotangent = cotangent[0]
    last = layers - 1
    query, packed, up_kept = wired(
        project_kernel,
        [first_gain, first_shift, joint_bias],
        [tokens, joint_weight, cotangent],
        [low_shape(rows, width), low_shape(rows, 3 * width + columns), low_shape(rows, columns)],
        [
            vm(rows, width),
            vm(width, 3 * width),
            vm(rows, width),
            vm(rows, width),
            vm(rows, width),
            vm(rows, 2 * width),
            dma((12,)),
        ],
        2 * rows * width * 3 * width,
    )
    saved = []
    stream = tokens
    for layer in range(last):
        far = swap_cores(packed)
        gate = [item for kept in saved for item in kept[-2:]]
        acts, hidden, soft, middle, slope, stream_next, query_next, packed_next = wired(
            functools.partial(middle_kernel, layer),
            [after(code, *gate), code_far, output_bias, second_gain, second_shift, up_bias]
            + [down_bias, first_gain, first_shift, joint_bias],
            [stream, query, packed, far, output_weight, up_weight, down_weight, joint_weight],
            [
                low_shape(rows, 2 * width),
                low_shape(rows, inner),
                low_shape(heads, rows, 2 * rows),
                full_shape(rows, width),
                low_shape(rows, inner),
                full_shape(rows, width),
                low_shape(rows, width),
                low_shape(rows, 3 * width),
            ],
            [
                vm(rows, width, kind=stream.dtype),
                vm(rows, width),
                vm(2 * rows, 2 * width),
                vm(rows, 2 * rows, kind=f32),
                vm(rows, 2 * width),
                vm(rows, inner),
                vm(heads, rows, 2 * rows),
                vm(rows, width, kind=f32),
                vm(rows, inner),
                vm(width, width),
                vm(width, inner),
                vm(inner, width),
                vm(width, 3 * width),
                vm(rows, width, kind=f32),
                vm(rows, width),
                vm(rows, width),
                vm(rows, 2 * width),
                dma((24,)),
            ],
            2 * rows * width * (2 * inner + 4 * width + 4 * rows),
        )
        saved.append(
            (stream, query, packed, far, acts, hidden, soft, middle, slope)
            + (swap_cores(acts), swap_cores(hidden))
        )
        stream, query, packed = stream_next, query_next, packed_next

    mixed_columns = inner // 2 + columns
    far = swap_cores(packed)
    gate = [item for kept in saved for item in kept[-2:]] if len(saved) > 1 else []
    got = wired(
        functools.partial(turn_kernel, last),
        [after(code, *gate), code_far, output_bias, second_gain, second_shift, up_bias, down_bias],
        [stream, query, packed, far, cotangent, output_weight, up_weight, down_weight],
        [
            low_shape(rows, 2 * width),
            low_shape(rows, inner),
            low_shape(heads, rows, 2 * rows),
            low_shape(rows, width),
            low_shape(rows, mixed_columns),
            low_shape(rows, mixed_columns),
            low_shape(rows, width),
            full_shape(rows, width),
            full_shape(8, width),
            full_shape(8, inner),
        ],
        [
            vm(rows, width, kind=stream.dtype),
            vm(rows, width),
            vm(2 * rows, 2 * width),
            vm(rows, 2 * rows, kind=f32),
            vm(rows, 2 * width),
            vm(rows, inner),
            vm(heads, rows, 2 * rows),
            vm(rows, width, kind=f32),
            vm(rows, width),
            vm(2, rows, mixed_columns),
            vm(rows, width),
            vm(rows, width, kind=f32),
            vm(rows, width, kind=f32),
            vm(rows, width),
            vm(rows, width, kind=f32),
            vm(width, width),
            vm(width, inner),
            vm(inner, width),
            dma((24,)),
        ],
        2 * rows * width * (4 * inner + width + 4 * rows),
        vector_outs=2,
    )
    acts, hidden, soft, output, preact_kept, preact_sent, low, middle_grad = got[:8]
    vectors_two, up_sum = got[8:]
    saved.append(
        (stream, query, packed, far, acts, hidden, soft, None, None)
        + (swap_cores(acts), swap_cores(hidden))
    )

    def attention_back(layer, low, gate):
        query, packed, far, _, _, soft = saved[layer][1:7]
        return wired(
            functools.partial(attention_back_kernel, layer),
            [],
            [after(low, *gate), query, packed, far, soft, output_weight],
            [
                low_shape(rows, width),
                full_shape(rows, 2 * width),
                low_shape(rows, 2 * width),
                full_shape(8, width),
            ],
            [
                vm(rows, width),
                vm(rows, width),
                vm(2 * rows, 2 * width),
                vm(heads, rows, 2 * rows),
                vm(rows, width),
                vm(width, width),
                vm(rows, width),
                vm(rows, 2 * width, kind=f32),
                vm(rows, 2 * width),
                dma((heads // 2,)),
                dma((8,)),
            ],
            2 * rows * width * (width + 10 * rows),
            vector_outs=1,
        )

    back_scratch = [
        vm(rows, 2 * width, kind=f32),
        vm(rows, 2 * width),
        vm(rows, width, kind=f32),
        vm(rows, width, kind=f32),
        vm(rows, 3 * width),
        vm(rows, width, kind=f32),
    ]

    def project_back(layer, dq, own, received, dq_sum, vectors_two, middle_grad, gate):
        stream = saved[layer][0]
        scratch = list(back_scratch)
        scratch[2] = vm(rows, width, kind=stream.dtype)
        return wired(
            functools.partial(project_back_kernel, layer),
            [after(code, *gate), first_gain, dq_sum, vectors_two],
            [dq, own, received, stream, middle_grad, joint_weight],
            [
                low_shape(rows, wide),
                low_shape(rows, wide),
                full_shape(rows, width),
                full_shape(8, width),
            ],
            scratch + [vm(width, 3 * width), dma((16,))],
            2 * rows * width * 3 * width,
            vector_outs=1,
        )

    def between(above, dq, own, received, dq_sum, vectors_two, middle_grad, gate):
        stream = saved[above][0]
        middle, slope = saved[above - 1][7:9]
        return wired(
            functools.partial(between_kernel, above),
            [after(code, *gate), first_gain, second_gain, dq_sum, vectors_two],
            [dq, own, received, stream, middle_grad, slope, middle]
            + [joint_weight, down_weight, up_weight],
            [
                low_shape(rows, wide),
                low_shape(rows, wide),
                low_shape(rows, columns),
                low_shape(rows, columns),
                low_shape(rows, mixed_columns),
                low_shape(rows, mixed_columns),
                low_shape(rows, width),
                full_shape(rows, width),
                full_shape(8, width),
                full_shape(8, width),
                full_shape(8, inner),
            ],
            back_scratch
            + [
                vm(rows, width),
                vm(rows, inner),
                vm(rows, width, kind=f32),
                vm(2, rows, mixed_columns),
                vm(rows, width),
                vm(rows, width, kind=f32),
                vm(rows, width, kind=f32),
                vm(width, 3 * width),
                vm(inner, width),
                vm(width, inner),
                dma((2, inner // width)),
                dma((24,)),
            ],
            2 * rows * width * (3 * width + 2 * inner),
            vector_outs=3,
        )

    groups = []
    gate = []

    def start(order, items, gate_arrays, vectors=()):
        arrays, plan, pieces, places = [], [], [], []
        row, vector_row = 0, 0

        def number(array):
            for index, known in enumerate(arrays):
                if known is array:
                    return index
            arrays.append(array)
            return len(arrays) - 1

        for left, left_far, at, at_far, size, right, right_far, r_at, r_at_far, strips, kind in items:
            left, left_far, right, right_far = map(number, (left, left_far, right, right_far))
            plan.append(
                (left, left_far, at, at_far, size, right, right_far, r_at, r_at_far, strips, row)
            )
            pieces.append((row, size // chips // 2, strips))
            places.append((size // chips // 2, kind[0], kind[1], strips))
            row += strips * size // chips
        if vectors:
            vector_row = row
            pieces.append((row, 16, 0))
            places.append((16, vectors[2]))
            row += 16
        depth = sum(item[9] * item[4] for item in plan)
        kept, sent = call(
            functools.partial(weight_kernel, chips, order, tuple(plan), vector_row),
            (low_shape(chips // 2, row, columns),) * 2,
            [ANY] + [VMEM] * len(vectors[:2]) + [ANY] * len(arrays),
            [vm(2, rows, item[4]) for item in plan]
            + [vm(2, rows, item[9] * columns) for item in plan]
            + [
                vm(chips, row, columns),
                dma((chips * len(plan),)),
                dma((sum(2 * max(1, item[4] // 768) + 2 for item in plan),)),
            ],
            after(code, *gate_arrays),
            *vectors[:2],
            *arrays,
            flops=4 * rows * columns * depth,
        )
        groups.append((Halving(kept, sent, chips, order), row, pieces, places))
        return kept

    def step(*which):
        return [
            groups[index][0].next() if index >= 0 else groups[~index][0].parts[-1]
            for index in which
            if max(index, ~index) < len(groups) and (index < 0 or groups[index][0].slots > 1)
        ]

    orders = [{"z": (0, 2, 1), "r": (0, 1, 2)}[letter] for letter in plan["orders"]]

    def down_item(layer, up_kept, up_far, at_far):
        hidden, hidden_far = saved[layer][5], saved[layer][10]
        return (hidden, hidden_far, 0, 0, inner, up_kept, up_far, 0, at_far, 1, (3, layer))

    def up_items(layer, kept, far):
        acts, acts_far = saved[layer][4], saved[layer][9]
        return [
            (acts, acts_far, width, width, width, kept, far, 0, 0, strips_up, (2, layer)),
            (acts, acts_far, 0, 0, width, kept, far, inner // 2, inner // 2, 1, (1, layer)),
        ]

    def joint_item(layer, kept, far):
        packed, packed_far = saved[layer][2], saved[layer][3]
        at = 2 * width
        return (packed, packed_far, at, at, width, kept, far, 0, 0, strips_joint, (0, layer))

    preact_far = swap_cores(preact_sent)
    dq, own, sent, dq_sum = attention_back(last, low, [])
    received = swap_cores(sent)
    joints = []
    loose = []
    if native:
        items = [down_item(last, up_kept, saved[0][3], 3 * width)]
        if plan["first"]:
            gate = [start(orders[0], items + up_items(last, preact_kept, preact_far), [dq])]
        else:
            gate = [start(orders[0], items, [dq])]
            gate = [start(orders[1], up_items(last, preact_kept, preact_far), gate)]
        gate += step(*plan["F2"])
    else:
        up_far = saved[0][3][:, 3 * width :]
        loose.append((last, up_kept, up_far, preact_kept, preact_far))
    for above in reversed(range(1, layers)):
        layer = above - 1
        got = between(above, dq, own, received, dq_sum, vectors_two, middle_grad, gate)
        mix_kept, mix_sent, up_kept, up_sent, preact_kept, preact_sent, low, middle_grad = got[:8]
        vectors_one, vectors_two, up_sum_next = got[8:]
        mix_far, up_far = swap_cores(mix_sent), swap_cores(up_sent)
        preact_far = swap_cores(preact_sent)
        gate = [low]
        if native:
            items = [joint_item(above, mix_kept, mix_far), down_item(layer, up_kept, up_far, 0)]
            gate += step(*plan["jd"])
            gate = [start(orders[-3], items, gate, (vectors_one, up_sum, above))]
            gate += step(*plan["u0"])
            gate = [start(orders[-2], up_items(layer, preact_kept, preact_far), gate)]
            gate += step(*plan["B1b"])
        else:
            joints.append((above, mix_kept, mix_far, vectors_one, up_sum))
            loose.append((layer, up_kept, up_far, preact_kept, preact_far))
        up_sum = up_sum_next
        dq, own, sent, dq_sum = attention_back(layer, low, gate)
        received = swap_cores(sent)
        gate = [dq] + step(*plan["B2"])
    got = project_back(0, dq, own, received, dq_sum, vectors_two, middle_grad, gate)
    mix_kept, mix_sent, input_gradient, vectors_one = got
    mix_far = swap_cores(mix_sent)
    if native:
        gate = [input_gradient] + step(*plan["j0"])
        kept = start(
            orders[-1], [joint_item(0, mix_kept, mix_far)], gate, (vectors_one, up_sum, 0)
        )
        tail = kept
        for index in plan["tail"]:
            if index < 0:
                tail = after(groups[~index][0].parts[-1], tail)
            elif groups[index][0].slots > 1:
                tail = groups[index][0].next(tail)
    else:
        joints.append((0, mix_kept, mix_far, vectors_one, up_sum))
        return plain_outputs(
            output, input_gradient, saved, loose, joints, chips, core, layers, width, inner
        )

    half = part // 2
    outs = [
        full_shape(layers, half, 3 * width),
        full_shape(layers, half, width),
        full_shape(layers, half, inner),
        full_shape(layers, inner // chips // 2, width),
        full_shape(layers, half),
        full_shape(layers, half),
        full_shape(layers, 2, half),
        full_shape(layers, half),
        full_shape(layers, half),
        full_shape(layers, half),
        full_shape(layers, half),
        full_shape(layers, inner // chips // 2),
    ]

    def finish(some, gate_arrays):
        parts, pieces, places, group_rows, base = [], [], [], [], 0
        for halving, count, group_pieces, group_places in some:
            parts += halving.rest().parts
            pieces.append(tuple(group_pieces))
            group_rows.append(count)
            for place in group_places:
                if len(place) == 4:
                    size, index, layer, strips = place
                    places.append((base, size, index, layer, strips))
                    base += size * strips
                else:
                    places.append((base, 8, place[1]))
                    base += 16
        steps = len(parts) // len(some)
        if gate_arrays:
            parts[0] = after(parts[0], *gate_arrays)
        kept, sent = call(
            functools.partial(sum_kernel, pieces),
            (full_shape(base, columns),) * 2,
            [ANY] * len(parts),
            [vm(steps, count, columns) for count in group_rows]
            + [
                vm(max(group_rows), columns, kind=f32),
                vm(base, columns, kind=f32),
                vm(base, columns, kind=f32),
                dma((len(parts) + 2,)),
            ],
            *parts,
        )
        return kept, swap_cores(sent), places

    split = plan["done"]
    done = [
        finish(some, (tail,) if plan["tail"] else ())
        for some in (groups[:split], groups[split:])
        if some
    ]
    final = call(
        functools.partial(place_kernel, [places for _, _, places in done]),
        outs,
        [ANY] * (2 * len(done)),
        [vm(*array.shape, kind=f32) for kept, far, _ in done for array in (kept, far)]
        + [dma((2 * len(done),))],
        *[array for kept, far, _ in done for array in (kept, far)],
        out_specs=(VMEM,) * len(outs),
    )
    joints, outputs, ups, downs, gain_one, shift_one, biases = final[:7]
    bias_out, gain_two, shift_two, bias_down, bias_up = final[7:]
    return (
        output[None],
        input_gradient[None],
        gain_one,
        shift_one,
        joints,
        biases,
        outputs,
        bias_out,
        gain_two,
        shift_two,
        ups,
        bias_up,
        downs,
        bias_down,
    )


def plain_outputs(
    output, input_gradient, saved, loose, joints, chips, core, layers, width, inner
):
    slots = slots_of_chips(chips, lax.axis_index("row").astype(jnp.int32), core)
    split = functools.partial(plain_sums, slots=slots, chips=chips, core=core)
    mats, vecs = [[None] * 4 for _ in range(layers)], [None] * layers
    for layer, up_kept, up_far, preact_kept, preact_far in loose:
        acts, hidden, acts_far, hidden_far = (saved[layer][index] for index in (4, 5, 9, 10))
        cut = inner // 2
        mats[layer][1] = split(
            acts[:, :width], acts_far[:, :width], preact_kept[:, cut:], preact_far[:, cut:]
        )
        mats[layer][2] = split(
            acts[:, width:], acts_far[:, width:], preact_kept[:, :cut], preact_far[:, :cut]
        )
        mats[layer][3] = split(hidden, hidden_far, up_kept, up_far)
    for layer, mix_kept, mix_far, vectors, up_sum in joints:
        packed, packed_far = saved[layer][2:4]
        window = slice(2 * width, 3 * width)
        mats[layer][0] = split(packed[:, window], packed_far[:, window], mix_kept, mix_far)
        vecs[layer] = [vectors[row] for row in range(8)] + [up_sum[0]]
    cuts = plain_vectors(
        [vector for layer in range(layers) for vector in vecs[layer]], slots, chips, core
    )

    def stacked(position):
        return jnp.stack([cuts[layer * 9 + position] for layer in range(layers)])

    def matrix(position):
        return jnp.stack([mats[layer][position] for layer in range(layers)])

    return (
        output[None],
        input_gradient[None],
        stacked(0),
        stacked(1),
        matrix(0),
        jnp.stack([stacked(2), stacked(3)], axis=1),
        matrix(1),
        stacked(4),
        stacked(5),
        stacked(6),
        matrix(2),
        stacked(8),
        matrix(3),
        stacked(7),
    )


def solution(mesh):
    chips = mesh.shape["row"]
    split = P("row", "tok", None)
    in_specs = (split, split, P("row", "tok"), P("row", "tok")) + (P(),) * 12
    vector = P(None, ("row", "tok"))
    table = P(None, ("row", "tok"), None)
    out_specs = (
        split,
        split,
        vector,
        vector,
        table,
        P(None, None, ("row", "tok")),
        table,
        vector,
        vector,
        vector,
        table,
        vector,
        table,
        vector,
    )

    def run(*arrays):
        return body(*arrays, chips=chips)

    return jax.shard_map(run, mesh=mesh, in_specs=in_specs, out_specs=out_specs, check_vma=False)
```

```python
import functools
import math

import jax
import jax.numpy as jnp
from jax import lax
from jax.experimental import pallas as pl
from jax.experimental.pallas import tpu as pltpu
from jax.sharding import PartitionSpec as P

epsilon = 1e-05
score_scale = 0.125
masked_score = -1e30
head_size = 64
lanes = 128
plan = {"F2": (), "jd": (0,), "u0": (1,), "B1b": (0,), "B2": (0, 1), "j0": (2, 3, 1), "tail": (), "first": 0, "orders": "zzzrr", "done": 3}
forward_unroll = 3
backward_unroll = 1
mlp_unroll = 2
f32 = jnp.float32
bf16 = jnp.bfloat16
VMEM = pl.BlockSpec(memory_space=pltpu.VMEM)
SMEM = pl.BlockSpec(memory_space=pltpu.SMEM)
HBM = pl.BlockSpec(memory_space=pltpu.HBM)
ANY = pl.BlockSpec(memory_space=pl.ANY)


def shape(dims, kind):
    return jax.ShapeDtypeStruct(dims, kind)


def dot(left, right):
    return jnp.dot(left, right, preferred_element_type=f32)


def dot_nt(left, right):
    return lax.dot_general(left, right, (((1,), (1,)), ((), ())), preferred_element_type=f32)


def dot_tn(left, right):
    return lax.dot_general(left, right, (((0,), (0,)), ((), ())), preferred_element_type=f32)


def normalize(stream):
    centre = stream - jnp.mean(stream, axis=-1, keepdims=True)
    inverse = lax.rsqrt(jnp.mean(centre * centre, axis=-1, keepdims=True) + epsilon)
    return centre * inverse, inverse


def norm_back(upstream, unit, inverse, gain):
    scaled = upstream * gain
    return inverse * (
        scaled
        - jnp.mean(scaled, axis=-1, keepdims=True)
        - unit * jnp.mean(scaled * unit, axis=-1, keepdims=True)
    )


def column_sum(array):
    return jnp.sum(array, axis=0, keepdims=True)


def gelu_and_slope(x):
    size = jnp.abs(x)
    t = 1.0 / (1.0 + (0.3275911 * 0.7071067811865476) * size)
    bell = jnp.exp(-0.5 * (x * x))
    series = t * (
        0.5 * 0.254829592
        + t
        * (
            0.5 * -0.284496736
            + t * (0.5 * 1.421413741 + t * (0.5 * -1.453152027 + t * (0.5 * 1.061405429)))
        )
    )
    tail = series * bell
    share = jnp.where(x >= 0, 1.0 - tail, tail)
    return x * share, share + x * (bell * 0.3989422804014327)


class Copies:
    def __init__(self, sems):
        self.sems = sems
        self.used = 0
        self.out = []

    def bring(self, source, target):
        copy = pltpu.make_async_copy(source, target, self.sems.at[self.used])
        self.used += 1
        copy.start()
        return copy

    def send(self, source, target):
        self.out.append(self.bring(source, target))

    def thirds(self, source, target, order):
        third = target.shape[1] // 3
        windows = [pl.ds(index * third, third) for index in order]
        return [self.bring(source.at[:, window], target.at[:, window]) for window in windows]

    def finish(self):
        for copy in self.out:
            copy.wait()


def emit_project(stream, layer, gain, shift, bias, weight, waits, normed_ref, query_ref, kv_ref):
    width = stream.shape[1]
    unit, _ = normalize(stream)
    normed_ref[...] = (unit * gain[layer : layer + 1] + shift[layer : layer + 1]).astype(bf16)
    normed = normed_ref[...]
    waits[0].wait()
    kv_ref[:, :width] = dot(normed, weight[:, width : 2 * width]).astype(bf16)
    waits[1].wait()
    kv_ref[:, width:] = (
        dot(normed, weight[:, 2 * width :]) + bias[layer, 1:2]
    ).astype(bf16)
    waits[2].wait()
    queries = (dot(normed, weight[:, :width]) + bias[layer, 0:1]).astype(bf16)
    query_ref[...] = queries * jnp.asarray(score_scale, bf16)


def head_masks():
    lane = lax.broadcasted_iota(jnp.int32, (1, lanes), 1)
    return (lane < head_size, lane >= head_size)


def emit_mask(rows, code_ref, far_ref, mask_ref):
    own = code_ref[...].astype(f32)
    diagonal = lax.broadcasted_iota(jnp.int32, (rows, rows), 0) == lax.broadcasted_iota(
        jnp.int32, (rows, rows), 1
    )
    column = jnp.sum(jnp.where(diagonal, own, 0.0), axis=1, keepdims=True)
    mask_ref[:, :rows] = jnp.where(column == own, 0.0, masked_score)
    mask_ref[:, rows:] = jnp.where(column == far_ref[...].astype(f32), 0.0, masked_score)


def emit_attention(width, query_ref, kv_ref, mask_ref, attended_ref, soft_ref):
    rows = query_ref.shape[0]
    masks = head_masks()
    zero = jnp.zeros((), bf16)

    def one_pair(pair, carry):
        columns = pl.ds(pl.multiple_of(pair * lanes, lanes), lanes)
        value_columns = pl.ds(pl.multiple_of(width + pair * lanes, lanes), lanes)
        queries = query_ref[:, columns]
        both = jnp.concatenate([jnp.where(mask, queries, zero) for mask in masks], axis=0)
        scores = dot_nt(both, kv_ref[:, columns])
        softs = []
        for side in range(2):
            own = scores[side * rows : (side + 1) * rows] + mask_ref[...]
            exponent = jnp.exp(own - jnp.max(own, axis=-1, keepdims=True))
            soft = exponent * (1.0 / jnp.sum(exponent, axis=-1, keepdims=True))
            softs.append(soft.astype(bf16))
            soft_ref[pair * 2 + side] = softs[-1]
        total = dot(jnp.concatenate(softs, axis=0), kv_ref[:, value_columns])
        attended_ref[:, columns] = jnp.where(masks[0], total[:rows], total[rows:]).astype(bf16)
        return carry

    lax.fori_loop(0, width // lanes, one_pair, 0, unroll=forward_unroll)


def emit_attention_back(
    width, query_ref, kv_ref, soft_ref, wait_soft, grad_ref, dq_ref, dq_sum, own_ref, sent_ref
):
    rows = query_ref.shape[0]
    masks = head_masks()
    zero = jnp.zeros((), bf16)
    def one_pair(pair, carry):
        wait_soft(pair)
        columns = pl.ds(pl.multiple_of(pair * lanes, lanes), lanes)
        value_columns = pl.ds(pl.multiple_of(width + pair * lanes, lanes), lanes)
        queries = query_ref[:, columns]
        grads = grad_ref[:, columns]
        keys = kv_ref[:, columns]
        own_grads = [jnp.where(mask, grads, zero) for mask in masks]
        soft_grads = dot_nt(jnp.concatenate(own_grads, axis=0), kv_ref[:, value_columns])
        dq = jnp.zeros((rows, lanes), f32)
        dk = jnp.zeros((2 * rows, lanes), f32)
        dv = jnp.zeros((2 * rows, lanes), f32)
        for side in range(2):
            soft_low = soft_ref[pair * 2 + side]
            soft = soft_low.astype(f32)
            soft_grad = soft_grads[side * rows : (side + 1) * rows]
            delta = jnp.sum(soft_grad * soft, axis=-1, keepdims=True)
            score_grad = (soft * (soft_grad - delta)).astype(bf16)
            dq += dot(score_grad, jnp.where(masks[side], keys, zero))
            dk += dot_tn(score_grad, jnp.where(masks[side], queries, zero))
            dv += dot_tn(soft_low, own_grads[side])
        dq = dq * score_scale
        dq_ref[:, columns] = dq.astype(bf16)
        dq_sum[0:1, columns] = column_sum(dq)
        own_ref[:, columns] = dk[:rows]
        own_ref[:, value_columns] = dv[:rows]
        sent_ref[:, columns] = dk[rows:].astype(bf16)
        sent_ref[:, value_columns] = dv[rows:].astype(bf16)
        return carry

    lax.fori_loop(0, width // lanes, one_pair, 0, unroll=backward_unroll)


def project_kernel(
    gain, shift, bias, tokens_hbm, weight_hbm, grad_hbm,
    query_hbm, packed_hbm, kept_hbm,
    tokens, weight, grad, normed, query, kv, sems,
):
    copies = Copies(sems)
    width = tokens.shape[1]
    half = width // 2
    first = copies.bring(tokens_hbm, tokens)
    third = copies.bring(grad_hbm, grad)
    thirds = copies.thirds(weight_hbm.at[0], weight, (1, 2, 0))
    core = lax.axis_index("tok")
    first.wait()
    third.wait()
    copies.send(
        grad.at[:, pl.ds(pl.multiple_of((1 - core) * half, half), half)],
        packed_hbm.at[:, pl.ds(3 * width, half)],
    )
    copies.send(grad.at[:, pl.ds(pl.multiple_of(core * half, half), half)], kept_hbm)
    emit_project(tokens[...].astype(f32), 0, gain, shift, bias, weight, thirds, normed, query, kv)
    copies.send(kv, packed_hbm.at[:, pl.ds(0, 2 * width)])
    copies.send(normed, packed_hbm.at[:, pl.ds(2 * width, width)])
    copies.send(query, query_hbm)
    copies.finish()


def emit_upper_half(layer, stream, output_weight, bias, gain, shift, acts, middle_ref):
    width = stream.shape[1]
    middle = stream + dot(acts[:, :width], output_weight[...]) + bias[layer : layer + 1]
    middle_ref[...] = middle
    unit, _ = normalize(middle)
    acts[:, width:] = (unit * gain[layer : layer + 1] + shift[layer : layer + 1]).astype(bf16)


def middle_kernel(
    layer, code, code_far, output_bias, gain, shift, up_bias,
    down_bias, next_gain, next_shift, joint_bias,
    stream_hbm, query_hbm, packed_hbm, far_hbm, output_hbm, up_hbm, down_hbm, joint_hbm,
    acts_hbm, hidden_hbm, soft_hbm, middle_hbm, slope_hbm,
    stream_next_hbm, query_next_hbm, packed_next_hbm,
    stream_ref, query, kv, mask, acts, hidden_ref, soft, middle_ref, slope,
    output_weight, up_weight, down_weight, joint_weight, total, normed, query_next, kv_next, sems,
):
    copies = Copies(sems)
    rows, width = query.shape
    inner = up_weight.shape[1]
    kv_window = pl.ds(0, 2 * width)
    wait = [
        copies.bring(query_hbm, query),
        copies.bring(packed_hbm.at[:, kv_window], kv.at[pl.ds(0, rows)]),
        copies.bring(far_hbm.at[:, kv_window], kv.at[pl.ds(rows, rows)]),
        copies.bring(stream_hbm, stream_ref),
    ]
    emit_mask(rows, code, code_far, mask)
    for copy in wait[:3]:
        copy.wait()
    output_copy = copies.bring(output_hbm.at[layer], output_weight)
    up_copy = copies.bring(up_hbm.at[layer], up_weight)
    down_copy = copies.bring(down_hbm.at[layer], down_weight)
    thirds = copies.thirds(joint_hbm.at[layer + 1], joint_weight, (1, 2, 0))
    emit_attention(width, query, kv, mask, acts, soft)
    copies.send(soft, soft_hbm)
    wait[3].wait()
    output_copy.wait()
    emit_upper_half(
        layer,
        stream_ref[...].astype(f32),
        output_weight,
        output_bias,
        gain,
        shift,
        acts,
        middle_ref,
    )
    copies.send(acts, acts_hbm)
    copies.send(middle_ref, middle_hbm)
    up_copy.wait()
    down_copy.wait()
    total[...] = middle_ref[...] + down_bias[layer : layer + 1]
    chunk = width

    def one_chunk(index, carry):
        columns = pl.ds(pl.multiple_of(index * chunk, chunk), chunk)
        preact = dot(acts[:, width:], up_weight[:, columns])
        hidden, rate = gelu_and_slope(preact + up_bias[layer : layer + 1, columns])
        hidden_ref[:, columns] = hidden.astype(bf16)
        slope[:, columns] = rate.astype(bf16)
        total[...] += dot(hidden_ref[:, columns], down_weight[columns, :])
        return carry

    lax.fori_loop(0, inner // chunk, one_chunk, 0, unroll=mlp_unroll)
    copies.send(hidden_ref, hidden_hbm)
    copies.send(slope, slope_hbm)
    copies.send(total, stream_next_hbm)
    emit_project(
        total[...],
        layer + 1,
        next_gain,
        next_shift,
        joint_bias,
        joint_weight,
        thirds,
        normed,
        query_next,
        kv_next,
    )
    copies.send(kv_next, packed_next_hbm.at[:, kv_window])
    copies.send(normed, packed_next_hbm.at[:, pl.ds(2 * width, width)])
    copies.send(query_next, query_next_hbm)
    copies.finish()


def emit_middle_grad(layer, core, upstream, middle, total, gain, vectors, low, grad_ref, grads):
    width = middle.shape[1]
    columns = width // 2
    unit, inverse = normalize(middle)
    normed_grad = total[...]
    vectors[5:6] = column_sum(normed_grad * unit)
    vectors[6:7] = column_sum(normed_grad)
    middle_grad = upstream + norm_back(normed_grad, unit, inverse, gain[layer : layer + 1])
    vectors[4:5] = column_sum(middle_grad)
    grad_ref[...] = middle_grad
    low[...] = middle_grad.astype(bf16)
    behind = grads.shape[2] - columns
    for turn, side in enumerate((1 - core, core)):
        grads[turn, :, behind:] = low[:, pl.ds(pl.multiple_of(side * columns, lanes), columns)]


def turn_kernel(
    layer, code, code_far, output_bias, gain, shift, up_bias, down_bias,
    stream_hbm, query_hbm, packed_hbm, far_hbm, upstream_hbm, output_hbm, up_hbm, down_hbm,
    acts_hbm, hidden_hbm, soft_hbm, result_hbm, kept_hbm, sent_hbm, low_hbm, grad_hbm,
    vectors, up_sum,
    stream_ref, query, kv, mask, acts, hidden_ref, soft, middle_ref, upstream_ref,
    grads, low, grad_ref, result, result_low, total,
    output_weight, up_weight, down_weight, sems,
):
    copies = Copies(sems)
    rows, width = query.shape
    inner = up_weight.shape[1]
    core = lax.axis_index("tok")
    kv_window = pl.ds(0, 2 * width)
    wait = [
        copies.bring(query_hbm, query),
        copies.bring(packed_hbm.at[:, kv_window], kv.at[pl.ds(0, rows)]),
        copies.bring(far_hbm.at[:, kv_window], kv.at[pl.ds(rows, rows)]),
        copies.bring(stream_hbm, stream_ref),
    ]
    emit_mask(rows, code, code_far, mask)
    for copy in wait[:3]:
        copy.wait()
    output_copy = copies.bring(output_hbm.at[layer], output_weight)
    upstream_copy = copies.bring(upstream_hbm, upstream_ref)
    up_copy = copies.bring(up_hbm.at[layer], up_weight)
    down_copy = copies.bring(down_hbm.at[layer], down_weight)
    emit_attention(width, query, kv, mask, acts, soft)
    copies.send(soft, soft_hbm)
    wait[3].wait()
    output_copy.wait()
    emit_upper_half(
        layer,
        stream_ref[...].astype(f32),
        output_weight,
        output_bias,
        gain,
        shift,
        acts,
        middle_ref,
    )
    copies.send(acts, acts_hbm)
    upstream_copy.wait()
    upstream = upstream_ref[...].astype(f32)
    low[...] = upstream.astype(bf16)
    vectors[0:4] = jnp.zeros_like(vectors[0:4])
    vectors[7:8] = column_sum(upstream)
    up_sum[...] = jnp.zeros_like(up_sum)
    result[...] = middle_ref[...] + down_bias[layer : layer + 1]
    total[...] = jnp.zeros_like(total)
    up_copy.wait()
    down_copy.wait()
    chunk = width
    half = inner // 2

    def one_chunk(index, carry):
        turn = index // (half // chunk)
        at = pl.multiple_of(index % (half // chunk) * chunk, chunk)
        side = jnp.where(turn == 0, 1 - core, core)
        columns = pl.ds(pl.multiple_of(side * half + at, chunk), chunk)
        preact = dot(acts[:, width:], up_weight[:, columns])
        hidden, rate = gelu_and_slope(preact + up_bias[layer : layer + 1, columns])
        hidden_ref[:, columns] = hidden.astype(bf16)
        result[...] += dot(hidden_ref[:, columns], down_weight[columns, :])
        preact_grad = dot_nt(low[...], down_weight[columns, :]) * rate
        up_sum[0:1, columns] = column_sum(preact_grad)
        grads[turn, :, pl.ds(at, chunk)] = preact_grad.astype(bf16)
        total[...] += dot_nt(preact_grad.astype(bf16), up_weight[:, columns])
        return carry

    lax.fori_loop(0, inner // chunk, one_chunk, 0, unroll=mlp_unroll)
    copies.send(hidden_ref, hidden_hbm)
    result_low[...] = result[...].astype(bf16)
    copies.send(result_low, result_hbm)
    emit_middle_grad(
        layer,
        core,
        upstream_ref[...].astype(f32),
        middle_ref[...],
        total,
        gain,
        vectors,
        low,
        grad_ref,
        grads,
    )
    copies.send(low, low_hbm)
    copies.send(grads.at[0], sent_hbm)
    copies.send(grads.at[1], kept_hbm)
    copies.send(grad_ref, grad_hbm)
    copies.finish()


def attention_back_kernel(
    layer, low_hbm, query_hbm, packed_hbm, far_hbm, soft_hbm, output_hbm,
    dq_hbm, own_hbm, sent_hbm, dq_sum,
    low, query, kv, soft, attended_grad, output_weight, dq, own, sent, soft_sems, sems,
):
    copies = Copies(sems)
    rows, width = low.shape
    kv_window = pl.ds(0, 2 * width)
    wait = [
        copies.bring(low_hbm, low),
        copies.bring(output_hbm.at[layer], output_weight),
        copies.bring(query_hbm, query),
        copies.bring(packed_hbm.at[:, kv_window], kv.at[pl.ds(0, rows)]),
        copies.bring(far_hbm.at[:, kv_window], kv.at[pl.ds(rows, rows)]),
    ]

    def soft_copy(pair):
        two = pl.ds(pair * 2, 2)
        return pltpu.make_async_copy(soft_hbm.at[two], soft.at[two], soft_sems.at[pair])

    for pair in range(width // lanes):
        soft_copy(pair).start()
    dq_sum[...] = jnp.zeros_like(dq_sum)
    wait[0].wait()
    wait[1].wait()
    attended_grad[...] = dot_nt(low[...], output_weight[...]).astype(bf16)
    for copy in wait[2:]:
        copy.wait()
    emit_attention_back(
        width,
        query,
        kv,
        soft,
        lambda pair: soft_copy(pair).wait(),
        attended_grad,
        dq,
        dq_sum,
        own,
        sent,
    )
    copies.send(sent, sent_hbm)
    copies.send(dq, dq_hbm)
    copies.send(own, own_hbm)
    copies.finish()


def emit_project_back(
    layer, copies, core, wait, thirds, dq_sum, vectors_two, gain, mixed, own, received,
    stream_ref, grad_ref, joint_weight, kept_hbm, sent_hbm, vectors,
):
    rows, width = stream_ref.shape
    wide = 3 * width // 2
    vectors[4:8] = vectors_two[4:8]
    vectors[2:3] = dq_sum[0:1]
    for copy in wait[:3]:
        copy.wait()
    kv_grad = own[...] + received[...].astype(f32)
    mixed[:, width:] = kv_grad.astype(bf16)
    vectors[3:4] = column_sum(kv_grad[:, width:])
    for side, target in ((1 - core, sent_hbm), (core, kept_hbm)):
        copies.send(mixed.at[:, pl.ds(pl.multiple_of(side * wide, lanes), wide)], target)
    normed_grad = jnp.zeros((rows, width), f32)
    for index, copy in enumerate(thirds):
        copy.wait()
        window = slice(index * width, (index + 1) * width)
        normed_grad += dot_nt(mixed[:, window], joint_weight[:, window])
    wait[3].wait()
    unit, inverse = normalize(stream_ref[...].astype(f32))
    vectors[0:1] = column_sum(normed_grad * unit)
    vectors[1:2] = column_sum(normed_grad)
    wait[4].wait()
    return grad_ref[...] + norm_back(normed_grad, unit, inverse, gain[layer : layer + 1])


def project_back_kernel(
    layer, gate, gain, dq_sum, vectors_two,
    dq_hbm, own_hbm, received_hbm, stream_hbm, grad_hbm, joint_hbm,
    kept_hbm, sent_hbm, upstream_hbm, vectors,
    own, received, stream_ref, grad_ref, mixed, upstream, joint_weight, sems,
):
    copies = Copies(sems)
    width = stream_ref.shape[1]
    wait = [
        copies.bring(dq_hbm, mixed.at[:, pl.ds(0, width)]),
        copies.bring(own_hbm, own),
        copies.bring(received_hbm, received),
        copies.bring(stream_hbm, stream_ref),
        copies.bring(grad_hbm, grad_ref),
    ]
    thirds = copies.thirds(joint_hbm.at[layer], joint_weight, (0, 1, 2))
    upstream[...] = emit_project_back(
        layer, copies, lax.axis_index("tok"), wait, thirds, dq_sum, vectors_two, gain, mixed,
        own, received, stream_ref, grad_ref, joint_weight, kept_hbm, sent_hbm, vectors,
    )
    copies.send(upstream, upstream_hbm)
    copies.finish()


def between_kernel(
    above, gate, gain, second_gain, dq_sum, vectors_two,
    dq_hbm, own_hbm, received_hbm, stream_hbm, grad_hbm, slope_hbm, middle_hbm,
    joint_hbm, down_hbm, up_hbm,
    mix_kept_hbm, mix_sent_hbm, up_kept_hbm, up_sent_hbm, kept_hbm, sent_hbm, low_hbm,
    grad_next_hbm, vectors, vectors_next, up_sum,
    own, received, stream_ref, grad_ref, mixed, upstream, low, slope, middle_ref,
    grads, low_next, grad_next, total, joint_weight, down_weight, up_weight, weight_sems, sems,
):
    copies = Copies(sems)
    rows, width = stream_ref.shape
    inner = up_weight.shape[1]
    layer = above - 1
    core = lax.axis_index("tok")
    wait = [
        copies.bring(dq_hbm, mixed.at[:, pl.ds(0, width)]),
        copies.bring(own_hbm, own),
        copies.bring(received_hbm, received),
        copies.bring(stream_hbm, stream_ref),
        copies.bring(grad_hbm, grad_ref),
    ]
    thirds = copies.thirds(joint_hbm.at[above], joint_weight, (0, 1, 2))
    chunk = width
    half = inner // 2

    def window_of(index):
        turn = index // (half // chunk)
        at = pl.multiple_of(index % (half // chunk) * chunk, chunk)
        side = jnp.where(turn == 0, 1 - core, core)
        return turn, at, pl.ds(pl.multiple_of(side * half + at, chunk), chunk)

    def weight_copies(index):
        window = window_of(index)[2]
        return (
            pltpu.make_async_copy(
                down_hbm.at[layer, window], down_weight.at[window], weight_sems.at[0, index]
            ),
            pltpu.make_async_copy(
                up_hbm.at[layer, :, window], up_weight.at[:, window], weight_sems.at[1, index]
            ),
        )

    slope_copy = copies.bring(slope_hbm, slope)
    for index in range(inner // chunk):
        for copy in weight_copies(index):
            copy.start()
    middle_copy = copies.bring(middle_hbm, middle_ref)
    below = emit_project_back(
        above, copies, core, wait, thirds, dq_sum, vectors_two, gain, mixed,
        own, received, stream_ref, grad_ref, joint_weight, mix_kept_hbm, mix_sent_hbm, vectors,
    )
    upstream[...] = below
    low[...] = below.astype(bf16)
    columns = width // 2
    for side, target in ((1 - core, up_sent_hbm), (core, up_kept_hbm)):
        copies.send(low.at[:, pl.ds(pl.multiple_of(side * columns, lanes), columns)], target)
    vectors_next[0:4] = jnp.zeros_like(vectors_next[0:4])
    vectors_next[7:8] = column_sum(below)
    up_sum[...] = jnp.zeros_like(up_sum)
    total[...] = jnp.zeros_like(total)
    slope_copy.wait()

    def one_chunk(index, carry):
        turn, at, window = window_of(index)
        for copy in weight_copies(index):
            copy.wait()
        preact_grad = dot_nt(low[...], down_weight[window, :]) * slope[:, window].astype(f32)
        up_sum[0:1, window] = column_sum(preact_grad)
        grads[turn, :, pl.ds(at, chunk)] = preact_grad.astype(bf16)
        total[...] += dot_nt(preact_grad.astype(bf16), up_weight[:, window])
        return carry

    lax.fori_loop(0, inner // chunk, one_chunk, 0, unroll=mlp_unroll)
    middle_copy.wait()
    emit_middle_grad(
        layer,
        core,
        upstream[...],
        middle_ref[...],
        total,
        second_gain,
        vectors_next,
        low_next,
        grad_next,
        grads,
    )
    copies.send(low_next, low_hbm)
    copies.send(grads.at[0], sent_hbm)
    copies.send(grads.at[1], kept_hbm)
    copies.send(grad_next, grad_next_hbm)
    copies.finish()


def weight_kernel(chips, order, plan, vector_row, *refs):
    core, me = lax.axis_index("tok"), lax.axis_index("row")
    refs = refs[1:]
    if vector_row:
        vectors, up_sum = refs[:2]
        refs = refs[2:]
    count = 1 + max(max(item[0], item[1], item[5], item[6]) for item in plan)
    arrays = refs[:count]
    kept_hbm, sent_hbm = refs[count : count + 2]
    refs = refs[count + 2 :]
    lefts, rights = refs[: len(plan)], refs[len(plan) : 2 * len(plan)]
    turned, block, slot_sems, left_sems, sems = refs[2 * len(plan) :]
    columns = block.shape[2]
    half = chips // 2
    steps = chips.bit_length() - 1
    bits = [
        jnp.where(core == 0, step_bit(order, step, 0), step_bit(order, step, 1))
        for step in range(steps)
    ]

    def slot_of(chip):
        apart = chip ^ me
        slot = 0
        for bit in bits:
            slot = slot * 2 + ((apart >> bit) & 1)
        return slot

    def left_copy(number, index, side):
        own, far, at, at_far, size = plan[number][:5]
        first = pl.multiple_of(index * 768, 768)
        return pltpu.make_async_copy(
            arrays[(own, far)[side]].at[:, pl.ds((at, at_far)[side] + first, 768)],
            lefts[number].at[side, :, pl.ds(first, 768)],
            left_sems.at[number, side, index],
        )

    def right_copy(number, side):
        own, far, at, at_far, strips = plan[number][5:10]
        window = pl.ds((at, at_far)[side], strips * columns)
        return pltpu.make_async_copy(
            arrays[(own, far)[side]].at[:, window], rights[number].at[side], sems.at[number, side]
        )

    for number, item in enumerate(plan):
        for index in range(item[4] // 768):
            for side in range(2):
                left_copy(number, index, side).start()
            if not index:
                for side in range(2):
                    right_copy(number, side).start()

    def row_copy(number, chip, row, count):
        slot = slot_of(chip)
        window = pl.ds(row, count)
        sem = slot_sems.at[number, chip]

        @pl.when(slot >= half)
        def _():
            target = sent_hbm.at[slot - half, window]
            pltpu.make_async_copy(block.at[slot, window], target, sem).start()

        @pl.when(slot < half)
        def _():
            pltpu.make_async_copy(block.at[slot, window], kept_hbm.at[slot, window], sem).start()

    depth = 16
    if vector_row:
        width, inner = vectors.shape[1], up_sum.shape[1]

        def one_chip(chip, carry):
            short = pltpu.roll(vectors[...], width - chip * (width // chips), axis=1)
            wide = pltpu.roll(up_sum[...], inner - chip * (inner // chips), axis=1)
            block[slot_of(chip), vector_row : vector_row + depth, :] = jnp.concatenate(
                [short[:, :columns], wide[:, :columns]], axis=0
            ).astype(bf16)
            return carry

        lax.fori_loop(0, chips, one_chip, 0)
    counts = []
    for number, item in enumerate(plan):
        size, strips, row = item[4], item[9], item[10]
        left, right = lefts[number], rights[number]
        rows = left.shape[1]
        part = size // chips
        some = 768 // part
        count = strips * part + (depth if vector_row == row + strips * part else 0)
        counts.append((row, count))

        def one_piece(index, carry, number=number, left=left, right=right, strips=strips, row=row):
            for side in range(2):
                left_copy(number, index, side).wait()
                first = pl.multiple_of(index * 768, 768)
                turned[:, side * rows : (side + 1) * rows] = left[side, :, pl.ds(first, 768)].T

            @pl.when(index == 0)
            def _():
                for side in range(2):
                    right_copy(number, side).wait()

            def one_strip(strip, carry):
                window = pl.ds(pl.multiple_of(strip * columns, columns), columns)
                product = dot(turned[:, :rows], right[0, :, window])
                product += dot(turned[:, rows:], right[1, :, window])
                at = pl.multiple_of(row + strip * part, 16)
                for one in range(some):
                    block[slot_of(index * some + one), pl.ds(at, part), :] = product[
                        one * part : (one + 1) * part
                    ].astype(bf16)
                return carry

            lax.fori_loop(0, strips, one_strip, 0)

            def one_send(one, carry):
                row_copy(number, index * some + one, row, count)
                return carry

            lax.fori_loop(0, some, one_send, 0)
            return carry

        lax.fori_loop(0, size // 768, one_piece, 0)
    for number, (row, count) in enumerate(counts):

        def one_wait(chip, carry, number=number, window=pl.ds(row, count)):
            pltpu.make_async_copy(
                block.at[0, window], kept_hbm.at[0, window], slot_sems.at[number, chip]
            ).wait()
            return carry

        lax.fori_loop(0, chips, one_wait, 0)


def sum_kernel(groups, *refs):
    count = len(groups)
    steps = (len(refs) - 2 - count - 4) // count
    inputs = refs[: count * steps]
    kept_hbm, sent_hbm = refs[count * steps : 2 + count * steps]
    buffers = refs[2 + count * steps : 2 + count * steps + count]
    total, kept, sent, sems = refs[2 + count * steps + count :]
    copies = Copies(sems)
    core = lax.axis_index("tok")
    waits = [
        [
            copies.bring(inputs[g * steps + step].at[0], buffers[g].at[step])
            for step in range(steps)
        ]
        for g in range(count)
    ]
    out = 0
    for g, pieces in enumerate(groups):
        for copy in waits[g]:
            copy.wait()
        rows = buffers[g].shape[1]
        value = buffers[g][0].astype(f32)
        for step in range(1, steps):
            value += buffers[g][step].astype(f32)
        total[:rows] = value
        for row, part, repeats in pieces:
            if not repeats:
                kept[out : out + part] = total[row : row + part]
                sent[out : out + part] = total[row : row + part]
                out += part
            for repeat in range(repeats):
                first = row + repeat * 2 * part
                kept[out : out + part] = total[pl.ds(pl.multiple_of(first + core * part, 8), part)]
                sent[out : out + part] = total[
                    pl.ds(pl.multiple_of(first + (1 - core) * part, 8), part)
                ]
                out += part
    copies.send(sent, sent_hbm)
    copies.send(kept, kept_hbm)
    copies.finish()


def place_kernel(places, *refs):
    count = len(places)
    inputs, outputs = refs[: 2 * count], refs[2 * count : -2 * count - 1]
    buffers, sems = refs[-2 * count - 1 : -1], refs[-1]
    copies = Copies(sems)
    wait = [copies.bring(source, target) for source, target in zip(inputs, buffers)]
    core = lax.axis_index("tok")
    for number, group in enumerate(places):
        kept, far = buffers[2 * number : 2 * number + 2]
        columns = kept.shape[1]
        for copy in wait[2 * number : 2 * number + 2]:
            copy.wait()
        for place in group:
            if len(place) == 5:
                first, part, index, layer, strips = place
                for strip in range(strips):
                    rows = slice(first + strip * part, first + (strip + 1) * part)
                    for side, source in ((core, kept), (1 - core, far)):
                        at = pl.multiple_of(side * (strips * columns) + strip * columns, lanes)
                        outputs[index][layer, :, pl.ds(at, columns)] = source[rows, :]
            else:
                first, half, layer = place
                short = kept[first : first + half] + far[first : first + half]
                wide = kept[first + half : first + 2 * half] + far[first + half : first + 2 * half]
                size, wide_size = outputs[4].shape[1], outputs[11].shape[1]
                short = pltpu.roll(short, columns - core * size, axis=1)
                wide = pltpu.roll(wide, columns - core * wide_size, axis=1)
                outputs[4][layer : layer + 1] = short[0:1, :size]
                outputs[5][layer : layer + 1] = short[1:2, :size]
                outputs[6][layer] = short[2:4, :size]
                for row, index in ((4, 7), (5, 8), (6, 9), (7, 10)):
                    outputs[index][layer : layer + 1] = short[row : row + 1, :size]
                outputs[11][layer : layer + 1] = wide[0:1, :wide_size]


def call(kernel, outs, ins, scratch, *arrays, flops=0, out_specs=None, limit=63):
    out_specs = tuple(out_specs or (ANY for _ in outs))
    count = sum(math.prod(a.shape) * a.dtype.itemsize for a in list(arrays) + list(outs))
    held = [kept for kept in scratch if kept.memory_space == pltpu.VMEM]
    held += [a for a, spec in zip(list(arrays) + list(outs), list(ins) + list(out_specs)) if spec is VMEM]
    need = sum(math.prod(a.shape) * a.dtype.itemsize for a in held) + (8 << 20)
    return pl.pallas_call(
        kernel,
        out_shape=tuple(outs),
        in_specs=list(ins),
        out_specs=out_specs,
        scratch_shapes=scratch,
        compiler_params=pltpu.CompilerParams(vmem_limit_bytes=max(need, limit << 20)),
        cost_estimate=pl.CostEstimate(flops=flops, bytes_accessed=count, transcendentals=0),
    )(*arrays)


def swap_cores(array):
    return lax.ppermute(array, "tok", [(0, 1), (1, 0)])


def after(array, *others):
    return lax.optimization_barrier((array,) + others)[0]


def step_bit(order, step, core):
    bit = order[step] if step < len(order) else step
    return bit ^ core if bit < 2 else bit


def distance(chips, order, slot, core):
    steps = chips.bit_length() - 1
    bits = [step_bit(order, step, core) for step in range(steps) if slot >> (steps - 1 - step) & 1]
    return sum(1 << bit for bit in bits)


def step_pairs(chips, order, step):
    return [
        (chip * 2 + core, (chip ^ (1 << step_bit(order, step, core))) * 2 + core)
        for chip in range(chips)
        for core in range(2)
    ]


class Halving:
    def __init__(self, kept, sent, chips, order=(0, 1)):
        self.chips = chips
        self.order = order
        self.slots = chips // 2
        self.step = 0
        self.parts = [kept]
        self.move(sent)

    def move(self, sent):
        pairs = step_pairs(self.chips, self.order, self.step)
        self.parts.append(lax.ppermute(sent, ("row", "tok"), pairs))
        self.step += 1

    def next(self, before=None):
        half = self.slots // 2
        sent = sum(part[half : self.slots].astype(f32) for part in self.parts)
        sent = sent.astype(self.parts[0].dtype)
        if before is not None:
            sent = after(sent, before)
        self.slots = half
        self.move(sent)
        return sent

    def rest(self):
        while self.slots > 1:
            self.next()
        return self


def slots_of_chips(chips, me, core):
    sides = [[distance(chips, (0, 1), slot, side) for slot in range(chips)] for side in range(2)]
    return me ^ jnp.asarray(sides, jnp.int32)[core]


def plain_sums(left, left_far, right, right_far, slots, chips, core):
    product = dot_tn(
        jnp.concatenate([left, left_far], axis=0), jnp.concatenate([right, right_far], axis=0)
    ).astype(bf16)
    product = product.reshape(chips, -1, product.shape[1])[slots]
    done = Halving(product[: chips // 2], product[chips // 2 :], chips).rest()
    total = sum(part[0].astype(f32) for part in done.parts)
    total = total.reshape(2, -1, total.shape[1])
    kept = lax.dynamic_index_in_dim(total, core, 0, keepdims=False)
    other = swap_cores(lax.dynamic_index_in_dim(total, 1 - core, 0, keepdims=False))
    return jnp.where(
        core == 0,
        jnp.concatenate([kept, other], axis=1),
        jnp.concatenate([other, kept], axis=1),
    )


def plain_vectors(vectors, slots, chips, core):
    pieces = [vector.reshape(chips, 2, -1) for vector in vectors]
    packed = jnp.concatenate(pieces, axis=2)
    sent = lax.dynamic_index_in_dim(packed, 1 - core, 1, keepdims=False)
    packed = lax.dynamic_index_in_dim(packed, core, 1, keepdims=False) + swap_cores(sent)
    packed = packed[slots]
    done = Halving(packed[: chips // 2], packed[chips // 2 :], chips).rest()
    packed = sum(part[0] for part in done.parts)
    cuts, at = [], 0
    for piece in pieces:
        cuts.append(packed[at : at + piece.shape[2]])
        at += piece.shape[2]
    return cuts


def body(
    tokens,
    cotangent,
    segment_ids,
    valid,
    first_gain,
    first_shift,
    joint_weight,
    joint_bias,
    output_weight,
    output_bias,
    second_gain,
    second_shift,
    up_weight,
    up_bias,
    down_weight,
    down_bias,
    chips,
):
    layers, width = joint_weight.shape[:2]
    inner = up_weight.shape[2]
    heads = width // head_size
    rows = tokens.shape[1]
    columns = width // 2
    wide = 3 * columns
    part = width // chips
    native = part % 48 == 0
    strips_up = inner // 2 // columns
    strips_joint = wide // columns
    core = lax.axis_index("tok").astype(jnp.int32)
    code = segment_ids * 2 + valid
    code_far = swap_cores(code)
    dma = pltpu.SemaphoreType.DMA
    weights = (joint_weight, output_weight, up_weight, down_weight)

    def vm(*sizes, kind=bf16):
        return pltpu.VMEM(sizes, kind)

    def low_shape(*sizes):
        return shape(sizes, bf16)

    def full_shape(*sizes):
        return shape(sizes, f32)

    def places_of(arrays):
        return [HBM if any(array is weight for weight in weights) else ANY for array in arrays]

    def wired(kernel, small, large, outs, scratch, flops, vector_outs=0):
        return call(
            kernel,
            outs,
            [VMEM] * len(small) + places_of(large),
            scratch,
            *small,
            *large,
            flops=flops,
            out_specs=[ANY] * (len(outs) - vector_outs) + [VMEM] * vector_outs,
        )

    tokens = tokens[0]
    cotangent = cotangent[0]
    last = layers - 1
    query, packed, up_kept = wired(
        project_kernel,
        [first_gain, first_shift, joint_bias],
        [tokens, joint_weight, cotangent],
        [low_shape(rows, width), low_shape(rows, 3 * width + columns), low_shape(rows, columns)],
        [
            vm(rows, width),
            vm(width, 3 * width),
            vm(rows, width),
            vm(rows, width),
            vm(rows, width),
            vm(rows, 2 * width),
            dma((12,)),
        ],
        2 * rows * width * 3 * width,
    )
    saved = []
    stream = tokens
    for layer in range(last):
        far = swap_cores(packed)
        gate = [item for kept in saved for item in kept[-2:]]
        acts, hidden, soft, middle, slope, stream_next, query_next, packed_next = wired(
            functools.partial(middle_kernel, layer),
            [after(code, *gate), code_far, output_bias, second_gain, second_shift, up_bias]
            + [down_bias, first_gain, first_shift, joint_bias],
            [stream, query, packed, far, output_weight, up_weight, down_weight, joint_weight],
            [
                low_shape(rows, 2 * width),
                low_shape(rows, inner),
                low_shape(heads, rows, 2 * rows),
                full_shape(rows, width),
                low_shape(rows, inner),
                full_shape(rows, width),
                low_shape(rows, width),
                low_shape(rows, 3 * width),
            ],
            [
                vm(rows, width, kind=stream.dtype),
                vm(rows, width),
                vm(2 * rows, 2 * width),
                vm(rows, 2 * rows, kind=f32),
                vm(rows, 2 * width),
                vm(rows, inner),
                vm(heads, rows, 2 * rows),
                vm(rows, width, kind=f32),
                vm(rows, inner),
                vm(width, width),
                vm(width, inner),
                vm(inner, width),
                vm(width, 3 * width),
                vm(rows, width, kind=f32),
                vm(rows, width),
                vm(rows, width),
                vm(rows, 2 * width),
                dma((24,)),
            ],
            2 * rows * width * (2 * inner + 4 * width + 4 * rows),
        )
        saved.append(
            (stream, query, packed, far, acts, hidden, soft, middle, slope)
            + (swap_cores(acts), swap_cores(hidden))
        )
        stream, query, packed = stream_next, query_next, packed_next

    mixed_columns = inner // 2 + columns
    far = swap_cores(packed)
    gate = [item for kept in saved for item in kept[-2:]] if len(saved) > 1 else []
    got = wired(
        functools.partial(turn_kernel, last),
        [after(code, *gate), code_far, output_bias, second_gain, second_shift, up_bias, down_bias],
        [stream, query, packed, far, cotangent, output_weight, up_weight, down_weight],
        [
            low_shape(rows, 2 * width),
            low_shape(rows, inner),
            low_shape(heads, rows, 2 * rows),
            low_shape(rows, width),
            low_shape(rows, mixed_columns),
            low_shape(rows, mixed_columns),
            low_shape(rows, width),
            full_shape(rows, width),
            full_shape(8, width),
            full_shape(8, inner),
        ],
        [
            vm(rows, width, kind=stream.dtype),
            vm(rows, width),
            vm(2 * rows, 2 * width),
            vm(rows, 2 * rows, kind=f32),
            vm(rows, 2 * width),
            vm(rows, inner),
            vm(heads, rows, 2 * rows),
            vm(rows, width, kind=f32),
            vm(rows, width),
            vm(2, rows, mixed_columns),
            vm(rows, width),
            vm(rows, width, kind=f32),
            vm(rows, width, kind=f32),
            vm(rows, width),
            vm(rows, width, kind=f32),
            vm(width, width),
            vm(width, inner),
            vm(inner, width),
            dma((24,)),
        ],
        2 * rows * width * (4 * inner + width + 4 * rows),
        vector_outs=2,
    )
    acts, hidden, soft, output, preact_kept, preact_sent, low, middle_grad = got[:8]
    vectors_two, up_sum = got[8:]
    saved.append(
        (stream, query, packed, far, acts, hidden, soft, None, None)
        + (swap_cores(acts), swap_cores(hidden))
    )

    def attention_back(layer, low, gate):
        query, packed, far, _, _, soft = saved[layer][1:7]
        return wired(
            functools.partial(attention_back_kernel, layer),
            [],
            [after(low, *gate), query, packed, far, soft, output_weight],
            [
                low_shape(rows, width),
                full_shape(rows, 2 * width),
                low_shape(rows, 2 * width),
                full_shape(8, width),
            ],
            [
                vm(rows, width),
                vm(rows, width),
                vm(2 * rows, 2 * width),
                vm(heads, rows, 2 * rows),
                vm(rows, width),
                vm(width, width),
                vm(rows, width),
                vm(rows, 2 * width, kind=f32),
                vm(rows, 2 * width),
                dma((heads // 2,)),
                dma((8,)),
            ],
            2 * rows * width * (width + 10 * rows),
            vector_outs=1,
        )

    back_scratch = [
        vm(rows, 2 * width, kind=f32),
        vm(rows, 2 * width),
        vm(rows, width, kind=f32),
        vm(rows, width, kind=f32),
        vm(rows, 3 * width),
        vm(rows, width, kind=f32),
    ]

    def project_back(layer, dq, own, received, dq_sum, vectors_two, middle_grad, gate):
        stream = saved[layer][0]
        scratch = list(back_scratch)
        scratch[2] = vm(rows, width, kind=stream.dtype)
        return wired(
            functools.partial(project_back_kernel, layer),
            [after(code, *gate), first_gain, dq_sum, vectors_two],
            [dq, own, received, stream, middle_grad, joint_weight],
            [
                low_shape(rows, wide),
                low_shape(rows, wide),
                full_shape(rows, width),
                full_shape(8, width),
            ],
            scratch + [vm(width, 3 * width), dma((16,))],
            2 * rows * width * 3 * width,
            vector_outs=1,
        )

    def between(above, dq, own, received, dq_sum, vectors_two, middle_grad, gate):
        stream = saved[above][0]
        middle, slope = saved[above - 1][7:9]
        return wired(
            functools.partial(between_kernel, above),
            [after(code, *gate), first_gain, second_gain, dq_sum, vectors_two],
            [dq, own, received, stream, middle_grad, slope, middle]
            + [joint_weight, down_weight, up_weight],
            [
                low_shape(rows, wide),
                low_shape(rows, wide),
                low_shape(rows, columns),
                low_shape(rows, columns),
                low_shape(rows, mixed_columns),
                low_shape(rows, mixed_columns),
                low_shape(rows, width),
                full_shape(rows, width),
                full_shape(8, width),
                full_shape(8, width),
                full_shape(8, inner),
            ],
            back_scratch
            + [
                vm(rows, width),
                vm(rows, inner),
                vm(rows, width, kind=f32),
                vm(2, rows, mixed_columns),
                vm(rows, width),
                vm(rows, width, kind=f32),
                vm(rows, width, kind=f32),
                vm(width, 3 * width),
                vm(inner, width),
                vm(width, inner),
                dma((2, inner // width)),
                dma((24,)),
            ],
            2 * rows * width * (3 * width + 2 * inner),
            vector_outs=3,
        )

    groups = []
    gate = []

    def start(order, items, gate_arrays, vectors=()):
        arrays, plan, pieces, places = [], [], [], []
        row, vector_row = 0, 0

        def number(array):
            for index, known in enumerate(arrays):
                if known is array:
                    return index
            arrays.append(array)
            return len(arrays) - 1

        for left, left_far, at, at_far, size, right, right_far, r_at, r_at_far, strips, kind in items:
            left, left_far, right, right_far = map(number, (left, left_far, right, right_far))
            plan.append(
                (left, left_far, at, at_far, size, right, right_far, r_at, r_at_far, strips, row)
            )
            pieces.append((row, size // chips // 2, strips))
            places.append((size // chips // 2, kind[0], kind[1], strips))
            row += strips * size // chips
        if vectors:
            vector_row = row
            pieces.append((row, 16, 0))
            places.append((16, vectors[2]))
            row += 16
        depth = sum(item[9] * item[4] for item in plan)
        kept, sent = call(
            functools.partial(weight_kernel, chips, order, tuple(plan), vector_row),
            (low_shape(chips // 2, row, columns),) * 2,
            [ANY] + [VMEM] * len(vectors[:2]) + [ANY] * len(arrays),
            [vm(2, rows, item[4]) for item in plan]
            + [vm(2, rows, item[9] * columns) for item in plan]
            + [
                vm(768, 2 * rows),
                vm(chips, row, columns),
                dma((len(plan), chips)),
                dma((len(plan), 2, max(item[4] for item in plan) // 768)),
                dma((len(plan), 2)),
            ],
            after(code, *gate_arrays),
            *vectors[:2],
            *arrays,
            flops=4 * rows * columns * depth,
        )
        groups.append((Halving(kept, sent, chips, order), row, pieces, places))
        return kept

    def step(*which):
        return [
            groups[index][0].next() if index >= 0 else groups[~index][0].parts[-1]
            for index in which
            if max(index, ~index) < len(groups) and (index < 0 or groups[index][0].slots > 1)
        ]

    orders = [{"z": (0, 2, 1), "r": (0, 1, 2)}[letter] for letter in plan["orders"]]

    def down_item(layer, up_kept, up_far, at_far):
        hidden, hidden_far = saved[layer][5], saved[layer][10]
        return (hidden, hidden_far, 0, 0, inner, up_kept, up_far, 0, at_far, 1, (3, layer))

    def up_items(layer, kept, far):
        acts, acts_far = saved[layer][4], saved[layer][9]
        return [
            (acts, acts_far, width, width, width, kept, far, 0, 0, strips_up, (2, layer)),
            (acts, acts_far, 0, 0, width, kept, far, inner // 2, inner // 2, 1, (1, layer)),
        ]

    def joint_item(layer, kept, far):
        packed, packed_far = saved[layer][2], saved[layer][3]
        at = 2 * width
        return (packed, packed_far, at, at, width, kept, far, 0, 0, strips_joint, (0, layer))

    preact_far = swap_cores(preact_sent)
    dq, own, sent, dq_sum = attention_back(last, low, [])
    received = swap_cores(sent)
    joints = []
    loose = []
    if native:
        items = [down_item(last, up_kept, saved[0][3], 3 * width)]
        if plan["first"]:
            gate = [start(orders[0], items + up_items(last, preact_kept, preact_far), [dq])]
        else:
            gate = [start(orders[0], items, [dq])]
            gate = [start(orders[1], up_items(last, preact_kept, preact_far), gate)]
        gate += step(*plan["F2"])
    else:
        up_far = saved[0][3][:, 3 * width :]
        loose.append((last, up_kept, up_far, preact_kept, preact_far))
    for above in reversed(range(1, layers)):
        layer = above - 1
        got = between(above, dq, own, received, dq_sum, vectors_two, middle_grad, gate)
        mix_kept, mix_sent, up_kept, up_sent, preact_kept, preact_sent, low, middle_grad = got[:8]
        vectors_one, vectors_two, up_sum_next = got[8:]
        mix_far, up_far = swap_cores(mix_sent), swap_cores(up_sent)
        preact_far = swap_cores(preact_sent)
        gate = [low]
        if native:
            items = [joint_item(above, mix_kept, mix_far), down_item(layer, up_kept, up_far, 0)]
            gate += step(*plan["jd"])
            gate = [start(orders[-3], items, gate, (vectors_one, up_sum, above))]
            gate += step(*plan["u0"])
            gate = [start(orders[-2], up_items(layer, preact_kept, preact_far), gate)]
            gate += step(*plan["B1b"])
        else:
            joints.append((above, mix_kept, mix_far, vectors_one, up_sum))
            loose.append((layer, up_kept, up_far, preact_kept, preact_far))
        up_sum = up_sum_next
        dq, own, sent, dq_sum = attention_back(layer, low, gate)
        received = swap_cores(sent)
        gate = [dq] + step(*plan["B2"])
    got = project_back(0, dq, own, received, dq_sum, vectors_two, middle_grad, gate)
    mix_kept, mix_sent, input_gradient, vectors_one = got
    mix_far = swap_cores(mix_sent)
    if native:
        gate = [input_gradient] + step(*plan["j0"])
        kept = start(
            orders[-1], [joint_item(0, mix_kept, mix_far)], gate, (vectors_one, up_sum, 0)
        )
        tail = kept
        for index in plan["tail"]:
            if index < 0:
                tail = after(groups[~index][0].parts[-1], tail)
            elif groups[index][0].slots > 1:
                tail = groups[index][0].next(tail)
    else:
        joints.append((0, mix_kept, mix_far, vectors_one, up_sum))
        return plain_outputs(
            output, input_gradient, saved, loose, joints, chips, core, layers, width, inner
        )

    half = part // 2
    outs = [
        full_shape(layers, half, 3 * width),
        full_shape(layers, half, width),
        full_shape(layers, half, inner),
        full_shape(layers, inner // chips // 2, width),
        full_shape(layers, half),
        full_shape(layers, half),
        full_shape(layers, 2, half),
        full_shape(layers, half),
        full_shape(layers, half),
        full_shape(layers, half),
        full_shape(layers, half),
        full_shape(layers, inner // chips // 2),
    ]

    def finish(some, gate_arrays):
        parts, pieces, places, group_rows, base = [], [], [], [], 0
        for halving, count, group_pieces, group_places in some:
            parts += halving.rest().parts
            pieces.append(tuple(group_pieces))
            group_rows.append(count)
            for place in group_places:
                if len(place) == 4:
                    size, index, layer, strips = place
                    places.append((base, size, index, layer, strips))
                    base += size * strips
                else:
                    places.append((base, 8, place[1]))
                    base += 16
        steps = len(parts) // len(some)
        if gate_arrays:
            parts[0] = after(parts[0], *gate_arrays)
        kept, sent = call(
            functools.partial(sum_kernel, pieces),
            (full_shape(base, columns),) * 2,
            [ANY] * len(parts),
            [vm(steps, count, columns) for count in group_rows]
            + [
                vm(max(group_rows), columns, kind=f32),
                vm(base, columns, kind=f32),
                vm(base, columns, kind=f32),
                dma((len(parts) + 2,)),
            ],
            *parts,
        )
        return kept, swap_cores(sent), places

    split = plan["done"]
    done = [
        finish(some, (tail,) if plan["tail"] else ())
        for some in (groups[:split], groups[split:])
        if some
    ]
    final = call(
        functools.partial(place_kernel, [places for _, _, places in done]),
        outs,
        [ANY] * (2 * len(done)),
        [vm(*array.shape, kind=f32) for kept, far, _ in done for array in (kept, far)]
        + [dma((2 * len(done),))],
        *[array for kept, far, _ in done for array in (kept, far)],
        out_specs=(VMEM,) * len(outs),
    )
    joints, outputs, ups, downs, gain_one, shift_one, biases = final[:7]
    bias_out, gain_two, shift_two, bias_down, bias_up = final[7:]
    return (
        output[None],
        input_gradient[None],
        gain_one,
        shift_one,
        joints,
        biases,
        outputs,
        bias_out,
        gain_two,
        shift_two,
        ups,
        bias_up,
        downs,
        bias_down,
    )


def plain_outputs(
    output, input_gradient, saved, loose, joints, chips, core, layers, width, inner
):
    slots = slots_of_chips(chips, lax.axis_index("row").astype(jnp.int32), core)
    split = functools.partial(plain_sums, slots=slots, chips=chips, core=core)
    mats, vecs = [[None] * 4 for _ in range(layers)], [None] * layers
    for layer, up_kept, up_far, preact_kept, preact_far in loose:
        acts, hidden, acts_far, hidden_far = (saved[layer][index] for index in (4, 5, 9, 10))
        cut = inner // 2
        mats[layer][1] = split(
            acts[:, :width], acts_far[:, :width], preact_kept[:, cut:], preact_far[:, cut:]
        )
        mats[layer][2] = split(
            acts[:, width:], acts_far[:, width:], preact_kept[:, :cut], preact_far[:, :cut]
        )
        mats[layer][3] = split(hidden, hidden_far, up_kept, up_far)
    for layer, mix_kept, mix_far, vectors, up_sum in joints:
        packed, packed_far = saved[layer][2:4]
        window = slice(2 * width, 3 * width)
        mats[layer][0] = split(packed[:, window], packed_far[:, window], mix_kept, mix_far)
        vecs[layer] = [vectors[row] for row in range(8)] + [up_sum[0]]
    cuts = plain_vectors(
        [vector for layer in range(layers) for vector in vecs[layer]], slots, chips, core
    )

    def stacked(position):
        return jnp.stack([cuts[layer * 9 + position] for layer in range(layers)])

    def matrix(position):
        return jnp.stack([mats[layer][position] for layer in range(layers)])

    return (
        output[None],
        input_gradient[None],
        stacked(0),
        stacked(1),
        matrix(0),
        jnp.stack([stacked(2), stacked(3)], axis=1),
        matrix(1),
        stacked(4),
        stacked(5),
        stacked(6),
        matrix(2),
        stacked(8),
        matrix(3),
        stacked(7),
    )


def solution(mesh):
    chips = mesh.shape["row"]
    split = P("row", "tok", None)
    in_specs = (split, split, P("row", "tok"), P("row", "tok")) + (P(),) * 12
    vector = P(None, ("row", "tok"))
    table = P(None, ("row", "tok"), None)
    out_specs = (
        split,
        split,
        vector,
        vector,
        table,
        P(None, None, ("row", "tok")),
        table,
        vector,
        vector,
        vector,
        table,
        vector,
        table,
        vector,
    )

    def run(*arrays):
        return body(*arrays, chips=chips)

    return jax.shard_map(run, mesh=mesh, in_specs=in_specs, out_specs=out_specs, check_vma=False)
```

```python
import functools
import math

import jax
import jax.numpy as jnp
from jax import lax
from jax.experimental import pallas as pl
from jax.experimental.pallas import tpu as pltpu
from jax.sharding import PartitionSpec as P

epsilon = 1e-05
score_scale = 0.125
masked_score = -1e30
head_size = 64
lanes = 128
plan = {"F2": (), "jd": (0,), "u0": (1,), "B1b": (0,), "B2": (0, 1), "j0": (2, 3, 1), "tail": (), "first": 0, "orders": "zzzrr", "done": 3}
forward_unroll = 3
backward_unroll = 1
mlp_unroll = 2
f32 = jnp.float32
bf16 = jnp.bfloat16
VMEM = pl.BlockSpec(memory_space=pltpu.VMEM)
SMEM = pl.BlockSpec(memory_space=pltpu.SMEM)
HBM = pl.BlockSpec(memory_space=pltpu.HBM)
ANY = pl.BlockSpec(memory_space=pl.ANY)


def shape(dims, kind):
    return jax.ShapeDtypeStruct(dims, kind)


def dot(left, right):
    return jnp.dot(left, right, preferred_element_type=f32)


def dot_nt(left, right):
    return lax.dot_general(left, right, (((1,), (1,)), ((), ())), preferred_element_type=f32)


def dot_tn(left, right):
    return lax.dot_general(left, right, (((0,), (0,)), ((), ())), preferred_element_type=f32)


def normalize(stream):
    centre = stream - jnp.mean(stream, axis=-1, keepdims=True)
    inverse = lax.rsqrt(jnp.mean(centre * centre, axis=-1, keepdims=True) + epsilon)
    return centre * inverse, inverse


def norm_back(upstream, unit, inverse, gain):
    scaled = upstream * gain
    return inverse * (
        scaled
        - jnp.mean(scaled, axis=-1, keepdims=True)
        - unit * jnp.mean(scaled * unit, axis=-1, keepdims=True)
    )


def column_sum(array):
    return jnp.sum(array, axis=0, keepdims=True)


def gelu_and_slope(x):
    size = jnp.abs(x)
    t = 1.0 / (1.0 + (0.3275911 * 0.7071067811865476) * size)
    bell = jnp.exp(-0.5 * (x * x))
    series = t * (
        0.5 * 0.254829592
        + t
        * (
            0.5 * -0.284496736
            + t * (0.5 * 1.421413741 + t * (0.5 * -1.453152027 + t * (0.5 * 1.061405429)))
        )
    )
    tail = series * bell
    share = jnp.where(x >= 0, 1.0 - tail, tail)
    return x * share, share + x * (bell * 0.3989422804014327)


class Copies:
    def __init__(self, sems):
        self.sems = sems
        self.used = 0
        self.out = []

    def bring(self, source, target):
        copy = pltpu.make_async_copy(source, target, self.sems.at[self.used])
        self.used += 1
        copy.start()
        return copy

    def send(self, source, target):
        self.out.append(self.bring(source, target))

    def thirds(self, source, target, order):
        third = target.shape[1] // 3
        windows = [pl.ds(index * third, third) for index in order]
        return [self.bring(source.at[:, window], target.at[:, window]) for window in windows]

    def finish(self):
        for copy in self.out:
            copy.wait()


def emit_project(stream, layer, gain, shift, bias, weight, waits, normed_ref, query_ref, kv_ref):
    width = stream.shape[1]
    unit, _ = normalize(stream)
    normed_ref[...] = (unit * gain[layer : layer + 1] + shift[layer : layer + 1]).astype(bf16)
    normed = normed_ref[...]
    waits[0].wait()
    kv_ref[:, :width] = dot(normed, weight[:, width : 2 * width]).astype(bf16)
    waits[1].wait()
    kv_ref[:, width:] = (
        dot(normed, weight[:, 2 * width :]) + bias[layer, 1:2]
    ).astype(bf16)
    waits[2].wait()
    queries = (dot(normed, weight[:, :width]) + bias[layer, 0:1]).astype(bf16)
    query_ref[...] = queries * jnp.asarray(score_scale, bf16)


def head_masks():
    lane = lax.broadcasted_iota(jnp.int32, (1, lanes), 1)
    return (lane < head_size, lane >= head_size)


def emit_mask(rows, code_ref, far_ref, mask_ref):
    own = code_ref[...].astype(f32)
    diagonal = lax.broadcasted_iota(jnp.int32, (rows, rows), 0) == lax.broadcasted_iota(
        jnp.int32, (rows, rows), 1
    )
    column = jnp.sum(jnp.where(diagonal, own, 0.0), axis=1, keepdims=True)
    mask_ref[:, :rows] = jnp.where(column == own, 0.0, masked_score)
    mask_ref[:, rows:] = jnp.where(column == far_ref[...].astype(f32), 0.0, masked_score)


def emit_attention(width, query_ref, kv_ref, mask_ref, attended_ref, soft_ref):
    rows = query_ref.shape[0]
    masks = head_masks()
    zero = jnp.zeros((), bf16)

    def one_pair(pair, carry):
        columns = pl.ds(pl.multiple_of(pair * lanes, lanes), lanes)
        value_columns = pl.ds(pl.multiple_of(width + pair * lanes, lanes), lanes)
        queries = query_ref[:, columns]
        both = jnp.concatenate([jnp.where(mask, queries, zero) for mask in masks], axis=0)
        scores = dot_nt(both, kv_ref[:, columns])
        softs = []
        for side in range(2):
            own = scores[side * rows : (side + 1) * rows] + mask_ref[...]
            exponent = jnp.exp(own - jnp.max(own, axis=-1, keepdims=True))
            soft = exponent * (1.0 / jnp.sum(exponent, axis=-1, keepdims=True))
            softs.append(soft.astype(bf16))
            soft_ref[pair * 2 + side] = softs[-1]
        total = dot(jnp.concatenate(softs, axis=0), kv_ref[:, value_columns])
        attended_ref[:, columns] = jnp.where(masks[0], total[:rows], total[rows:]).astype(bf16)
        return carry

    lax.fori_loop(0, width // lanes, one_pair, 0, unroll=forward_unroll)


def emit_attention_back(
    width, query_ref, kv_ref, soft_ref, wait_soft, grad_ref, dq_ref, dq_sum, own_ref, sent_ref
):
    rows = query_ref.shape[0]
    masks = head_masks()
    zero = jnp.zeros((), bf16)
    def one_pair(pair, carry):
        wait_soft(pair)
        columns = pl.ds(pl.multiple_of(pair * lanes, lanes), lanes)
        value_columns = pl.ds(pl.multiple_of(width + pair * lanes, lanes), lanes)
        queries = query_ref[:, columns]
        grads = grad_ref[:, columns]
        keys = kv_ref[:, columns]
        own_grads = [jnp.where(mask, grads, zero) for mask in masks]
        soft_grads = dot_nt(jnp.concatenate(own_grads, axis=0), kv_ref[:, value_columns])
        dq = jnp.zeros((rows, lanes), f32)
        dk = jnp.zeros((2 * rows, lanes), f32)
        dv = jnp.zeros((2 * rows, lanes), f32)
        for side in range(2):
            soft_low = soft_ref[pair * 2 + side]
            soft = soft_low.astype(f32)
            soft_grad = soft_grads[side * rows : (side + 1) * rows]
            delta = jnp.sum(soft_grad * soft, axis=-1, keepdims=True)
            score_grad = (soft * (soft_grad - delta)).astype(bf16)
            dq += dot(score_grad, jnp.where(masks[side], keys, zero))
            dk += dot_tn(score_grad, jnp.where(masks[side], queries, zero))
            dv += dot_tn(soft_low, own_grads[side])
        dq = dq * score_scale
        dq_ref[:, columns] = dq.astype(bf16)
        dq_sum[0:1, columns] = column_sum(dq)
        own_ref[:, columns] = dk[:rows]
        own_ref[:, value_columns] = dv[:rows]
        sent_ref[:, columns] = dk[rows:].astype(bf16)
        sent_ref[:, value_columns] = dv[rows:].astype(bf16)
        return carry

    lax.fori_loop(0, width // lanes, one_pair, 0, unroll=backward_unroll)


def project_kernel(
    gain, shift, bias, tokens_hbm, weight_hbm, grad_hbm,
    query_hbm, packed_hbm, kept_hbm,
    tokens, weight, grad, normed, query, kv, sems,
):
    copies = Copies(sems)
    width = tokens.shape[1]
    half = width // 2
    first = copies.bring(tokens_hbm, tokens)
    thirds = copies.thirds(weight_hbm.at[0], weight, (1, 2, 0))
    third = copies.bring(grad_hbm, grad)
    core = lax.axis_index("tok")
    first.wait()
    emit_project(tokens[...].astype(f32), 0, gain, shift, bias, weight, thirds, normed, query, kv)
    copies.send(kv, packed_hbm.at[:, pl.ds(0, 2 * width)])
    third.wait()
    copies.send(
        grad.at[:, pl.ds(pl.multiple_of((1 - core) * half, half), half)],
        packed_hbm.at[:, pl.ds(3 * width, half)],
    )
    copies.send(grad.at[:, pl.ds(pl.multiple_of(core * half, half), half)], kept_hbm)
    copies.send(normed, packed_hbm.at[:, pl.ds(2 * width, width)])
    copies.send(query, query_hbm)
    copies.finish()


def emit_upper_half(layer, stream, output_weight, bias, gain, shift, acts, middle_ref):
    width = stream.shape[1]
    middle = stream + dot(acts[:, :width], output_weight[...]) + bias[layer : layer + 1]
    middle_ref[...] = middle
    unit, _ = normalize(middle)
    acts[:, width:] = (unit * gain[layer : layer + 1] + shift[layer : layer + 1]).astype(bf16)


def middle_kernel(
    layer, code, code_far, output_bias, gain, shift, up_bias,
    down_bias, next_gain, next_shift, joint_bias,
    stream_hbm, query_hbm, packed_hbm, far_hbm, output_hbm, up_hbm, down_hbm, joint_hbm,
    acts_hbm, hidden_hbm, soft_hbm, middle_hbm, slope_hbm,
    stream_next_hbm, query_next_hbm, packed_next_hbm,
    stream_ref, query, kv, mask, acts, hidden_ref, soft, middle_ref, slope,
    output_weight, up_weight, down_weight, joint_weight, total, normed, query_next, kv_next, sems,
):
    copies = Copies(sems)
    rows, width = query.shape
    inner = up_weight.shape[1]
    kv_window = pl.ds(0, 2 * width)
    wait = [
        copies.bring(query_hbm, query),
        copies.bring(packed_hbm.at[:, kv_window], kv.at[pl.ds(0, rows)]),
        copies.bring(far_hbm.at[:, kv_window], kv.at[pl.ds(rows, rows)]),
        copies.bring(stream_hbm, stream_ref),
    ]
    emit_mask(rows, code, code_far, mask)
    for copy in wait[:3]:
        copy.wait()
    output_copy = copies.bring(output_hbm.at[layer], output_weight)
    up_copy = copies.bring(up_hbm.at[layer], up_weight)
    down_copy = copies.bring(down_hbm.at[layer], down_weight)
    thirds = copies.thirds(joint_hbm.at[layer + 1], joint_weight, (1, 2, 0))
    emit_attention(width, query, kv, mask, acts, soft)
    copies.send(soft, soft_hbm)
    wait[3].wait()
    output_copy.wait()
    emit_upper_half(
        layer,
        stream_ref[...].astype(f32),
        output_weight,
        output_bias,
        gain,
        shift,
        acts,
        middle_ref,
    )
    copies.send(acts, acts_hbm)
    copies.send(middle_ref, middle_hbm)
    up_copy.wait()
    down_copy.wait()
    total[...] = middle_ref[...] + down_bias[layer : layer + 1]
    chunk = width

    def one_chunk(index, carry):
        columns = pl.ds(pl.multiple_of(index * chunk, chunk), chunk)
        preact = dot(acts[:, width:], up_weight[:, columns])
        hidden, rate = gelu_and_slope(preact + up_bias[layer : layer + 1, columns])
        hidden_ref[:, columns] = hidden.astype(bf16)
        slope[:, columns] = rate.astype(bf16)
        total[...] += dot(hidden_ref[:, columns], down_weight[columns, :])
        return carry

    lax.fori_loop(0, inner // chunk, one_chunk, 0, unroll=mlp_unroll)
    copies.send(hidden_ref, hidden_hbm)
    copies.send(slope, slope_hbm)
    copies.send(total, stream_next_hbm)
    emit_project(
        total[...],
        layer + 1,
        next_gain,
        next_shift,
        joint_bias,
        joint_weight,
        thirds,
        normed,
        query_next,
        kv_next,
    )
    copies.send(kv_next, packed_next_hbm.at[:, kv_window])
    copies.send(normed, packed_next_hbm.at[:, pl.ds(2 * width, width)])
    copies.send(query_next, query_next_hbm)
    copies.finish()


def emit_middle_grad(layer, core, upstream, middle, total, gain, vectors, low, grad_ref, grads):
    width = middle.shape[1]
    columns = width // 2
    unit, inverse = normalize(middle)
    normed_grad = total[...]
    vectors[5:6] = column_sum(normed_grad * unit)
    vectors[6:7] = column_sum(normed_grad)
    middle_grad = upstream + norm_back(normed_grad, unit, inverse, gain[layer : layer + 1])
    vectors[4:5] = column_sum(middle_grad)
    grad_ref[...] = middle_grad
    low[...] = middle_grad.astype(bf16)
    behind = grads.shape[2] - columns
    for turn, side in enumerate((1 - core, core)):
        grads[turn, :, behind:] = low[:, pl.ds(pl.multiple_of(side * columns, lanes), columns)]


def turn_kernel(
    layer, code, code_far, output_bias, gain, shift, up_bias, down_bias,
    stream_hbm, query_hbm, packed_hbm, far_hbm, upstream_hbm, output_hbm, up_hbm, down_hbm,
    acts_hbm, hidden_hbm, soft_hbm, result_hbm, kept_hbm, sent_hbm, low_hbm, grad_hbm,
    vectors, up_sum,
    stream_ref, query, kv, mask, acts, hidden_ref, soft, middle_ref, upstream_ref,
    grads, low, grad_ref, result, result_low, total,
    output_weight, up_weight, down_weight, sems,
):
    copies = Copies(sems)
    rows, width = query.shape
    inner = up_weight.shape[1]
    core = lax.axis_index("tok")
    kv_window = pl.ds(0, 2 * width)
    wait = [
        copies.bring(query_hbm, query),
        copies.bring(packed_hbm.at[:, kv_window], kv.at[pl.ds(0, rows)]),
        copies.bring(far_hbm.at[:, kv_window], kv.at[pl.ds(rows, rows)]),
        copies.bring(stream_hbm, stream_ref),
    ]
    emit_mask(rows, code, code_far, mask)
    for copy in wait[:3]:
        copy.wait()
    output_copy = copies.bring(output_hbm.at[layer], output_weight)
    upstream_copy = copies.bring(upstream_hbm, upstream_ref)
    up_copy = copies.bring(up_hbm.at[layer], up_weight)
    down_copy = copies.bring(down_hbm.at[layer], down_weight)
    emit_attention(width, query, kv, mask, acts, soft)
    copies.send(soft, soft_hbm)
    wait[3].wait()
    output_copy.wait()
    emit_upper_half(
        layer,
        stream_ref[...].astype(f32),
        output_weight,
        output_bias,
        gain,
        shift,
        acts,
        middle_ref,
    )
    copies.send(acts, acts_hbm)
    upstream_copy.wait()
    upstream = upstream_ref[...].astype(f32)
    low[...] = upstream.astype(bf16)
    vectors[0:4] = jnp.zeros_like(vectors[0:4])
    vectors[7:8] = column_sum(upstream)
    up_sum[...] = jnp.zeros_like(up_sum)
    result[...] = middle_ref[...] + down_bias[layer : layer + 1]
    total[...] = jnp.zeros_like(total)
    up_copy.wait()
    down_copy.wait()
    chunk = width
    half = inner // 2

    def one_chunk(index, carry):
        turn = index // (half // chunk)
        at = pl.multiple_of(index % (half // chunk) * chunk, chunk)
        side = jnp.where(turn == 0, 1 - core, core)
        columns = pl.ds(pl.multiple_of(side * half + at, chunk), chunk)
        preact = dot(acts[:, width:], up_weight[:, columns])
        hidden, rate = gelu_and_slope(preact + up_bias[layer : layer + 1, columns])
        hidden_ref[:, columns] = hidden.astype(bf16)
        result[...] += dot(hidden_ref[:, columns], down_weight[columns, :])
        preact_grad = dot_nt(low[...], down_weight[columns, :]) * rate
        up_sum[0:1, columns] = column_sum(preact_grad)
        grads[turn, :, pl.ds(at, chunk)] = preact_grad.astype(bf16)
        total[...] += dot_nt(preact_grad.astype(bf16), up_weight[:, columns])
        return carry

    lax.fori_loop(0, inner // chunk, one_chunk, 0, unroll=mlp_unroll)
    copies.send(hidden_ref, hidden_hbm)
    result_low[...] = result[...].astype(bf16)
    copies.send(result_low, result_hbm)
    emit_middle_grad(
        layer,
        core,
        upstream_ref[...].astype(f32),
        middle_ref[...],
        total,
        gain,
        vectors,
        low,
        grad_ref,
        grads,
    )
    copies.send(low, low_hbm)
    copies.send(grads.at[0], sent_hbm)
    copies.send(grads.at[1], kept_hbm)
    copies.send(grad_ref, grad_hbm)
    copies.finish()


def attention_back_kernel(
    layer, low_hbm, query_hbm, packed_hbm, far_hbm, soft_hbm, output_hbm,
    dq_hbm, own_hbm, sent_hbm, dq_sum,
    low, query, kv, soft, attended_grad, output_weight, dq, own, sent, soft_sems, sems,
):
    copies = Copies(sems)
    rows, width = low.shape
    kv_window = pl.ds(0, 2 * width)
    wait = [
        copies.bring(low_hbm, low),
        copies.bring(output_hbm.at[layer], output_weight),
        copies.bring(query_hbm, query),
        copies.bring(packed_hbm.at[:, kv_window], kv.at[pl.ds(0, rows)]),
        copies.bring(far_hbm.at[:, kv_window], kv.at[pl.ds(rows, rows)]),
    ]

    def soft_copy(pair):
        two = pl.ds(pair * 2, 2)
        return pltpu.make_async_copy(soft_hbm.at[two], soft.at[two], soft_sems.at[pair])

    for pair in range(width // lanes):
        soft_copy(pair).start()
    dq_sum[...] = jnp.zeros_like(dq_sum)
    wait[0].wait()
    wait[1].wait()
    attended_grad[...] = dot_nt(low[...], output_weight[...]).astype(bf16)
    for copy in wait[2:]:
        copy.wait()
    emit_attention_back(
        width,
        query,
        kv,
        soft,
        lambda pair: soft_copy(pair).wait(),
        attended_grad,
        dq,
        dq_sum,
        own,
        sent,
    )
    copies.send(sent, sent_hbm)
    copies.send(dq, dq_hbm)
    copies.send(own, own_hbm)
    copies.finish()


def emit_project_back(
    layer, copies, core, wait, thirds, dq_sum, vectors_two, gain, mixed, own, received,
    stream_ref, grad_ref, joint_weight, kept_hbm, sent_hbm, vectors,
):
    rows, width = stream_ref.shape
    wide = 3 * width // 2
    vectors[4:8] = vectors_two[4:8]
    vectors[2:3] = dq_sum[0:1]
    for copy in wait[:3]:
        copy.wait()
    kv_grad = own[...] + received[...].astype(f32)
    mixed[:, width:] = kv_grad.astype(bf16)
    vectors[3:4] = column_sum(kv_grad[:, width:])
    for side, target in ((1 - core, sent_hbm), (core, kept_hbm)):
        copies.send(mixed.at[:, pl.ds(pl.multiple_of(side * wide, lanes), wide)], target)
    normed_grad = jnp.zeros((rows, width), f32)
    for index, copy in enumerate(thirds):
        copy.wait()
        window = slice(index * width, (index + 1) * width)
        normed_grad += dot_nt(mixed[:, window], joint_weight[:, window])
    wait[3].wait()
    unit, inverse = normalize(stream_ref[...].astype(f32))
    vectors[0:1] = column_sum(normed_grad * unit)
    vectors[1:2] = column_sum(normed_grad)
    wait[4].wait()
    return grad_ref[...] + norm_back(normed_grad, unit, inverse, gain[layer : layer + 1])


def project_back_kernel(
    layer, gate, gain, dq_sum, vectors_two,
    dq_hbm, own_hbm, received_hbm, stream_hbm, grad_hbm, joint_hbm,
    kept_hbm, sent_hbm, upstream_hbm, vectors,
    own, received, stream_ref, grad_ref, mixed, upstream, joint_weight, sems,
):
    copies = Copies(sems)
    width = stream_ref.shape[1]
    wait = [
        copies.bring(dq_hbm, mixed.at[:, pl.ds(0, width)]),
        copies.bring(own_hbm, own),
        copies.bring(received_hbm, received),
        copies.bring(stream_hbm, stream_ref),
        copies.bring(grad_hbm, grad_ref),
    ]
    thirds = copies.thirds(joint_hbm.at[layer], joint_weight, (0, 1, 2))
    upstream[...] = emit_project_back(
        layer, copies, lax.axis_index("tok"), wait, thirds, dq_sum, vectors_two, gain, mixed,
        own, received, stream_ref, grad_ref, joint_weight, kept_hbm, sent_hbm, vectors,
    )
    copies.send(upstream, upstream_hbm)
    copies.finish()


def between_kernel(
    above, gate, gain, second_gain, dq_sum, vectors_two,
    dq_hbm, own_hbm, received_hbm, stream_hbm, grad_hbm, slope_hbm, middle_hbm,
    joint_hbm, down_hbm, up_hbm,
    mix_kept_hbm, mix_sent_hbm, up_kept_hbm, up_sent_hbm, kept_hbm, sent_hbm, low_hbm,
    grad_next_hbm, vectors, vectors_next, up_sum,
    own, received, stream_ref, grad_ref, mixed, upstream, low, slope, middle_ref,
    grads, low_next, grad_next, total, joint_weight, down_weight, up_weight, weight_sems, sems,
):
    copies = Copies(sems)
    rows, width = stream_ref.shape
    inner = up_weight.shape[1]
    layer = above - 1
    core = lax.axis_index("tok")
    wait = [
        copies.bring(dq_hbm, mixed.at[:, pl.ds(0, width)]),
        copies.bring(own_hbm, own),
        copies.bring(received_hbm, received),
        copies.bring(stream_hbm, stream_ref),
        copies.bring(grad_hbm, grad_ref),
    ]
    thirds = copies.thirds(joint_hbm.at[above], joint_weight, (0, 1, 2))
    chunk = width
    half = inner // 2

    def window_of(index):
        turn = index // (half // chunk)
        at = pl.multiple_of(index % (half // chunk) * chunk, chunk)
        side = jnp.where(turn == 0, 1 - core, core)
        return turn, at, pl.ds(pl.multiple_of(side * half + at, chunk), chunk)

    def weight_copies(index):
        window = window_of(index)[2]
        return (
            pltpu.make_async_copy(
                down_hbm.at[layer, window], down_weight.at[window], weight_sems.at[0, index]
            ),
            pltpu.make_async_copy(
                up_hbm.at[layer, :, window], up_weight.at[:, window], weight_sems.at[1, index]
            ),
        )

    slope_copy = copies.bring(slope_hbm, slope)
    for index in range(inner // chunk):
        for copy in weight_copies(index):
            copy.start()
    middle_copy = copies.bring(middle_hbm, middle_ref)
    below = emit_project_back(
        above, copies, core, wait, thirds, dq_sum, vectors_two, gain, mixed,
        own, received, stream_ref, grad_ref, joint_weight, mix_kept_hbm, mix_sent_hbm, vectors,
    )
    upstream[...] = below
    low[...] = below.astype(bf16)
    columns = width // 2
    for side, target in ((1 - core, up_sent_hbm), (core, up_kept_hbm)):
        copies.send(low.at[:, pl.ds(pl.multiple_of(side * columns, lanes), columns)], target)
    vectors_next[0:4] = jnp.zeros_like(vectors_next[0:4])
    vectors_next[7:8] = column_sum(below)
    up_sum[...] = jnp.zeros_like(up_sum)
    total[...] = jnp.zeros_like(total)
    slope_copy.wait()

    def one_chunk(index, carry):
        turn, at, window = window_of(index)
        for copy in weight_copies(index):
            copy.wait()
        preact_grad = dot_nt(low[...], down_weight[window, :]) * slope[:, window].astype(f32)
        up_sum[0:1, window] = column_sum(preact_grad)
        grads[turn, :, pl.ds(at, chunk)] = preact_grad.astype(bf16)
        total[...] += dot_nt(preact_grad.astype(bf16), up_weight[:, window])
        return carry

    lax.fori_loop(0, inner // chunk, one_chunk, 0, unroll=mlp_unroll)
    middle_copy.wait()
    emit_middle_grad(
        layer,
        core,
        upstream[...],
        middle_ref[...],
        total,
        second_gain,
        vectors_next,
        low_next,
        grad_next,
        grads,
    )
    copies.send(low_next, low_hbm)
    copies.send(grads.at[0], sent_hbm)
    copies.send(grads.at[1], kept_hbm)
    copies.send(grad_next, grad_next_hbm)
    copies.finish()


def weight_kernel(chips, order, plan, vector_row, *refs):
    core, me = lax.axis_index("tok"), lax.axis_index("row")
    refs = refs[1:]
    if vector_row:
        vectors, up_sum = refs[:2]
        refs = refs[2:]
    count = 1 + max(max(item[0], item[1], item[5], item[6]) for item in plan)
    arrays = refs[:count]
    kept_hbm, sent_hbm = refs[count : count + 2]
    refs = refs[count + 2 :]
    lefts, rights = refs[: len(plan)], refs[len(plan) : 2 * len(plan)]
    turned, block, slot_sems, left_sems, sems = refs[2 * len(plan) :]
    columns = block.shape[2]
    half = chips // 2
    steps = chips.bit_length() - 1
    bits = [
        jnp.where(core == 0, step_bit(order, step, 0), step_bit(order, step, 1))
        for step in range(steps)
    ]

    def slot_of(chip):
        apart = chip ^ me
        slot = 0
        for bit in bits:
            slot = slot * 2 + ((apart >> bit) & 1)
        return slot

    def left_copy(number, index, side):
        own, far, at, at_far, size = plan[number][:5]
        first = pl.multiple_of(index * 768, 768)
        return pltpu.make_async_copy(
            arrays[(own, far)[side]].at[:, pl.ds((at, at_far)[side] + first, 768)],
            lefts[number].at[side, :, pl.ds(first, 768)],
            left_sems.at[number, side, index],
        )

    def right_copy(number, side):
        own, far, at, at_far, strips = plan[number][5:10]
        window = pl.ds((at, at_far)[side], strips * columns)
        return pltpu.make_async_copy(
            arrays[(own, far)[side]].at[:, window], rights[number].at[side], sems.at[number, side]
        )

    for number, item in enumerate(plan):
        for index in range(item[4] // 768):
            for side in range(2):
                left_copy(number, index, side).start()
            if not index:
                for side in range(2):
                    right_copy(number, side).start()

    def row_copy(number, chip, row, count):
        slot = slot_of(chip)
        window = pl.ds(row, count)
        sem = slot_sems.at[number, chip]

        @pl.when(slot >= half)
        def _():
            target = sent_hbm.at[slot - half, window]
            pltpu.make_async_copy(block.at[slot, window], target, sem).start()

        @pl.when(slot < half)
        def _():
            pltpu.make_async_copy(block.at[slot, window], kept_hbm.at[slot, window], sem).start()

    depth = 16
    if vector_row:
        width, inner = vectors.shape[1], up_sum.shape[1]

        def one_chip(chip, carry):
            short = pltpu.roll(vectors[...], width - chip * (width // chips), axis=1)
            wide = pltpu.roll(up_sum[...], inner - chip * (inner // chips), axis=1)
            block[slot_of(chip), vector_row : vector_row + depth, :] = jnp.concatenate(
                [short[:, :columns], wide[:, :columns]], axis=0
            ).astype(bf16)
            return carry

        lax.fori_loop(0, chips, one_chip, 0)
    counts = []
    for number, item in enumerate(plan):
        size, strips, row = item[4], item[9], item[10]
        left, right = lefts[number], rights[number]
        rows = left.shape[1]
        part = size // chips
        some = 768 // part
        count = strips * part + (depth if vector_row == row + strips * part else 0)
        counts.append((row, count))

        def one_piece(index, carry, number=number, left=left, right=right, strips=strips, row=row):
            for side in range(2):
                left_copy(number, index, side).wait()
                first = pl.multiple_of(index * 768, 768)
                turned[:, side * rows : (side + 1) * rows] = left[side, :, pl.ds(first, 768)].T

            @pl.when(index == 0)
            def _():
                for side in range(2):
                    right_copy(number, side).wait()

            def one_strip(strip, carry):
                window = pl.ds(pl.multiple_of(strip * columns, columns), columns)
                product = dot(turned[:, :rows], right[0, :, window])
                product += dot(turned[:, rows:], right[1, :, window])
                at = pl.multiple_of(row + strip * part, 16)
                for one in range(some):
                    block[slot_of(index * some + one), pl.ds(at, part), :] = product[
                        one * part : (one + 1) * part
                    ].astype(bf16)
                return carry

            lax.fori_loop(0, strips, one_strip, 0)

            def one_send(one, carry):
                row_copy(number, index * some + one, row, count)
                return carry

            lax.fori_loop(0, some, one_send, 0)
            return carry

        lax.fori_loop(0, size // 768, one_piece, 0)
    for number, (row, count) in enumerate(counts):

        def one_wait(chip, carry, number=number, window=pl.ds(row, count)):
            pltpu.make_async_copy(
                block.at[0, window], kept_hbm.at[0, window], slot_sems.at[number, chip]
            ).wait()
            return carry

        lax.fori_loop(0, chips, one_wait, 0)


def sum_kernel(groups, *refs):
    count = len(groups)
    steps = (len(refs) - 2 - count - 4) // count
    inputs = refs[: count * steps]
    kept_hbm, sent_hbm = refs[count * steps : 2 + count * steps]
    buffers = refs[2 + count * steps : 2 + count * steps + count]
    total, kept, sent, sems = refs[2 + count * steps + count :]
    copies = Copies(sems)
    core = lax.axis_index("tok")
    waits = [
        [
            copies.bring(inputs[g * steps + step].at[0], buffers[g].at[step])
            for step in range(steps)
        ]
        for g in range(count)
    ]
    out = 0
    for g, pieces in enumerate(groups):
        for copy in waits[g]:
            copy.wait()
        rows = buffers[g].shape[1]
        value = buffers[g][0].astype(f32)
        for step in range(1, steps):
            value += buffers[g][step].astype(f32)
        total[:rows] = value
        for row, part, repeats in pieces:
            if not repeats:
                kept[out : out + part] = total[row : row + part]
                sent[out : out + part] = total[row : row + part]
                out += part
            for repeat in range(repeats):
                first = row + repeat * 2 * part
                kept[out : out + part] = total[pl.ds(pl.multiple_of(first + core * part, 8), part)]
                sent[out : out + part] = total[
                    pl.ds(pl.multiple_of(first + (1 - core) * part, 8), part)
                ]
                out += part
    copies.send(sent, sent_hbm)
    copies.send(kept, kept_hbm)
    copies.finish()


def place_kernel(places, *refs):
    count = len(places)
    inputs, outputs = refs[: 2 * count], refs[2 * count : -2 * count - 1]
    buffers, sems = refs[-2 * count - 1 : -1], refs[-1]
    copies = Copies(sems)
    wait = [copies.bring(source, target) for source, target in zip(inputs, buffers)]
    core = lax.axis_index("tok")
    for number, group in enumerate(places):
        kept, far = buffers[2 * number : 2 * number + 2]
        columns = kept.shape[1]
        for copy in wait[2 * number : 2 * number + 2]:
            copy.wait()
        for place in group:
            if len(place) == 5:
                first, part, index, layer, strips = place
                for strip in range(strips):
                    rows = slice(first + strip * part, first + (strip + 1) * part)
                    for side, source in ((core, kept), (1 - core, far)):
                        at = pl.multiple_of(side * (strips * columns) + strip * columns, lanes)
                        outputs[index][layer, :, pl.ds(at, columns)] = source[rows, :]
            else:
                first, half, layer = place
                short = kept[first : first + half] + far[first : first + half]
                wide = kept[first + half : first + 2 * half] + far[first + half : first + 2 * half]
                size, wide_size = outputs[4].shape[1], outputs[11].shape[1]
                short = pltpu.roll(short, columns - core * size, axis=1)
                wide = pltpu.roll(wide, columns - core * wide_size, axis=1)
                outputs[4][layer : layer + 1] = short[0:1, :size]
                outputs[5][layer : layer + 1] = short[1:2, :size]
                outputs[6][layer] = short[2:4, :size]
                for row, index in ((4, 7), (5, 8), (6, 9), (7, 10)):
                    outputs[index][layer : layer + 1] = short[row : row + 1, :size]
                outputs[11][layer : layer + 1] = wide[0:1, :wide_size]


def call(kernel, outs, ins, scratch, *arrays, flops=0, out_specs=None, limit=63):
    out_specs = tuple(out_specs or (ANY for _ in outs))
    count = sum(math.prod(a.shape) * a.dtype.itemsize for a in list(arrays) + list(outs))
    held = [kept for kept in scratch if kept.memory_space == pltpu.VMEM]
    held += [a for a, spec in zip(list(arrays) + list(outs), list(ins) + list(out_specs)) if spec is VMEM]
    need = sum(math.prod(a.shape) * a.dtype.itemsize for a in held) + (8 << 20)
    return pl.pallas_call(
        kernel,
        out_shape=tuple(outs),
        in_specs=list(ins),
        out_specs=out_specs,
        scratch_shapes=scratch,
        compiler_params=pltpu.CompilerParams(vmem_limit_bytes=max(need, limit << 20)),
        cost_estimate=pl.CostEstimate(flops=flops, bytes_accessed=count, transcendentals=0),
    )(*arrays)


def swap_cores(array):
    return lax.ppermute(array, "tok", [(0, 1), (1, 0)])


def after(array, *others):
    return lax.optimization_barrier((array,) + others)[0]


def step_bit(order, step, core):
    bit = order[step] if step < len(order) else step
    return bit ^ core if bit < 2 else bit


def distance(chips, order, slot, core):
    steps = chips.bit_length() - 1
    bits = [step_bit(order, step, core) for step in range(steps) if slot >> (steps - 1 - step) & 1]
    return sum(1 << bit for bit in bits)


def step_pairs(chips, order, step):
    return [
        (chip * 2 + core, (chip ^ (1 << step_bit(order, step, core))) * 2 + core)
        for chip in range(chips)
        for core in range(2)
    ]


class Halving:
    def __init__(self, kept, sent, chips, order=(0, 1)):
        self.chips = chips
        self.order = order
        self.slots = chips // 2
        self.step = 0
        self.parts = [kept]
        self.move(sent)

    def move(self, sent):
        pairs = step_pairs(self.chips, self.order, self.step)
        self.parts.append(lax.ppermute(sent, ("row", "tok"), pairs))
        self.step += 1

    def next(self, before=None):
        half = self.slots // 2
        sent = sum(part[half : self.slots].astype(f32) for part in self.parts)
        sent = sent.astype(self.parts[0].dtype)
        if before is not None:
            sent = after(sent, before)
        self.slots = half
        self.move(sent)
        return sent

    def rest(self):
        while self.slots > 1:
            self.next()
        return self


def slots_of_chips(chips, me, core):
    sides = [[distance(chips, (0, 1), slot, side) for slot in range(chips)] for side in range(2)]
    return me ^ jnp.asarray(sides, jnp.int32)[core]


def plain_sums(left, left_far, right, right_far, slots, chips, core):
    product = dot_tn(
        jnp.concatenate([left, left_far], axis=0), jnp.concatenate([right, right_far], axis=0)
    ).astype(bf16)
    product = product.reshape(chips, -1, product.shape[1])[slots]
    done = Halving(product[: chips // 2], product[chips // 2 :], chips).rest()
    total = sum(part[0].astype(f32) for part in done.parts)
    total = total.reshape(2, -1, total.shape[1])
    kept = lax.dynamic_index_in_dim(total, core, 0, keepdims=False)
    other = swap_cores(lax.dynamic_index_in_dim(total, 1 - core, 0, keepdims=False))
    return jnp.where(
        core == 0,
        jnp.concatenate([kept, other], axis=1),
        jnp.concatenate([other, kept], axis=1),
    )


def plain_vectors(vectors, slots, chips, core):
    pieces = [vector.reshape(chips, 2, -1) for vector in vectors]
    packed = jnp.concatenate(pieces, axis=2)
    sent = lax.dynamic_index_in_dim(packed, 1 - core, 1, keepdims=False)
    packed = lax.dynamic_index_in_dim(packed, core, 1, keepdims=False) + swap_cores(sent)
    packed = packed[slots]
    done = Halving(packed[: chips // 2], packed[chips // 2 :], chips).rest()
    packed = sum(part[0] for part in done.parts)
    cuts, at = [], 0
    for piece in pieces:
        cuts.append(packed[at : at + piece.shape[2]])
        at += piece.shape[2]
    return cuts


def body(
    tokens,
    cotangent,
    segment_ids,
    valid,
    first_gain,
    first_shift,
    joint_weight,
    joint_bias,
    output_weight,
    output_bias,
    second_gain,
    second_shift,
    up_weight,
    up_bias,
    down_weight,
    down_bias,
    chips,
):
    layers, width = joint_weight.shape[:2]
    inner = up_weight.shape[2]
    heads = width // head_size
    rows = tokens.shape[1]
    columns = width // 2
    wide = 3 * columns
    part = width // chips
    native = part % 48 == 0
    strips_up = inner // 2 // columns
    strips_joint = wide // columns
    core = lax.axis_index("tok").astype(jnp.int32)
    code = segment_ids * 2 + valid
    code_far = swap_cores(code)
    dma = pltpu.SemaphoreType.DMA
    weights = (joint_weight, output_weight, up_weight, down_weight)

    def vm(*sizes, kind=bf16):
        return pltpu.VMEM(sizes, kind)

    def low_shape(*sizes):
        return shape(sizes, bf16)

    def full_shape(*sizes):
        return shape(sizes, f32)

    def places_of(arrays):
        return [HBM if any(array is weight for weight in weights) else ANY for array in arrays]

    def wired(kernel, small, large, outs, scratch, flops, vector_outs=0):
        return call(
            kernel,
            outs,
            [VMEM] * len(small) + places_of(large),
            scratch,
            *small,
            *large,
            flops=flops,
            out_specs=[ANY] * (len(outs) - vector_outs) + [VMEM] * vector_outs,
        )

    tokens = tokens[0]
    cotangent = cotangent[0]
    last = layers - 1
    query, packed, up_kept = wired(
        project_kernel,
        [first_gain, first_shift, joint_bias],
        [tokens, joint_weight, cotangent],
        [low_shape(rows, width), low_shape(rows, 3 * width + columns), low_shape(rows, columns)],
        [
            vm(rows, width),
            vm(width, 3 * width),
            vm(rows, width),
            vm(rows, width),
            vm(rows, width),
            vm(rows, 2 * width),
            dma((12,)),
        ],
        2 * rows * width * 3 * width,
    )
    saved = []
    stream = tokens
    for layer in range(last):
        far = swap_cores(packed)
        gate = [item for kept in saved for item in kept[-2:]]
        acts, hidden, soft, middle, slope, stream_next, query_next, packed_next = wired(
            functools.partial(middle_kernel, layer),
            [after(code, *gate), code_far, output_bias, second_gain, second_shift, up_bias]
            + [down_bias, first_gain, first_shift, joint_bias],
            [stream, query, packed, far, output_weight, up_weight, down_weight, joint_weight],
            [
                low_shape(rows, 2 * width),
                low_shape(rows, inner),
                low_shape(heads, rows, 2 * rows),
                full_shape(rows, width),
                low_shape(rows, inner),
                full_shape(rows, width),
                low_shape(rows, width),
                low_shape(rows, 3 * width),
            ],
            [
                vm(rows, width, kind=stream.dtype),
                vm(rows, width),
                vm(2 * rows, 2 * width),
                vm(rows, 2 * rows, kind=f32),
                vm(rows, 2 * width),
                vm(rows, inner),
                vm(heads, rows, 2 * rows),
                vm(rows, width, kind=f32),
                vm(rows, inner),
                vm(width, width),
                vm(width, inner),
                vm(inner, width),
                vm(width, 3 * width),
                vm(rows, width, kind=f32),
                vm(rows, width),
                vm(rows, width),
                vm(rows, 2 * width),
                dma((24,)),
            ],
            2 * rows * width * (2 * inner + 4 * width + 4 * rows),
        )
        saved.append(
            (stream, query, packed, far, acts, hidden, soft, middle, slope)
            + (swap_cores(acts), swap_cores(hidden))
        )
        stream, query, packed = stream_next, query_next, packed_next

    mixed_columns = inner // 2 + columns
    far = swap_cores(packed)
    gate = [item for kept in saved for item in kept[-2:]] if len(saved) > 1 else []
    got = wired(
        functools.partial(turn_kernel, last),
        [after(code, *gate), code_far, output_bias, second_gain, second_shift, up_bias, down_bias],
        [stream, query, packed, far, cotangent, output_weight, up_weight, down_weight],
        [
            low_shape(rows, 2 * width),
            low_shape(rows, inner),
            low_shape(heads, rows, 2 * rows),
            low_shape(rows, width),
            low_shape(rows, mixed_columns),
            low_shape(rows, mixed_columns),
            low_shape(rows, width),
            full_shape(rows, width),
            full_shape(8, width),
            full_shape(8, inner),
        ],
        [
            vm(rows, width, kind=stream.dtype),
            vm(rows, width),
            vm(2 * rows, 2 * width),
            vm(rows, 2 * rows, kind=f32),
            vm(rows, 2 * width),
            vm(rows, inner),
            vm(heads, rows, 2 * rows),
            vm(rows, width, kind=f32),
            vm(rows, width),
            vm(2, rows, mixed_columns),
            vm(rows, width),
            vm(rows, width, kind=f32),
            vm(rows, width, kind=f32),
            vm(rows, width),
            vm(rows, width, kind=f32),
            vm(width, width),
            vm(width, inner),
            vm(inner, width),
            dma((24,)),
        ],
        2 * rows * width * (4 * inner + width + 4 * rows),
        vector_outs=2,
    )
    acts, hidden, soft, output, preact_kept, preact_sent, low, middle_grad = got[:8]
    vectors_two, up_sum = got[8:]
    saved.append(
        (stream, query, packed, far, acts, hidden, soft, None, None)
        + (swap_cores(acts), swap_cores(hidden))
    )

    def attention_back(layer, low, gate):
        query, packed, far, _, _, soft = saved[layer][1:7]
        return wired(
            functools.partial(attention_back_kernel, layer),
            [],
            [after(low, *gate), query, packed, far, soft, output_weight],
            [
                low_shape(rows, width),
                full_shape(rows, 2 * width),
                low_shape(rows, 2 * width),
                full_shape(8, width),
            ],
            [
                vm(rows, width),
                vm(rows, width),
                vm(2 * rows, 2 * width),
                vm(heads, rows, 2 * rows),
                vm(rows, width),
                vm(width, width),
                vm(rows, width),
                vm(rows, 2 * width, kind=f32),
                vm(rows, 2 * width),
                dma((heads // 2,)),
                dma((8,)),
            ],
            2 * rows * width * (width + 10 * rows),
            vector_outs=1,
        )

    back_scratch = [
        vm(rows, 2 * width, kind=f32),
        vm(rows, 2 * width),
        vm(rows, width, kind=f32),
        vm(rows, width, kind=f32),
        vm(rows, 3 * width),
        vm(rows, width, kind=f32),
    ]

    def project_back(layer, dq, own, received, dq_sum, vectors_two, middle_grad, gate):
        stream = saved[layer][0]
        scratch = list(back_scratch)
        scratch[2] = vm(rows, width, kind=stream.dtype)
        return wired(
            functools.partial(project_back_kernel, layer),
            [after(code, *gate), first_gain, dq_sum, vectors_two],
            [dq, own, received, stream, middle_grad, joint_weight],
            [
                low_shape(rows, wide),
                low_shape(rows, wide),
                full_shape(rows, width),
                full_shape(8, width),
            ],
            scratch + [vm(width, 3 * width), dma((16,))],
            2 * rows * width * 3 * width,
            vector_outs=1,
        )

    def between(above, dq, own, received, dq_sum, vectors_two, middle_grad, gate):
        stream = saved[above][0]
        middle, slope = saved[above - 1][7:9]
        return wired(
            functools.partial(between_kernel, above),
            [after(code, *gate), first_gain, second_gain, dq_sum, vectors_two],
            [dq, own, received, stream, middle_grad, slope, middle]
            + [joint_weight, down_weight, up_weight],
            [
                low_shape(rows, wide),
                low_shape(rows, wide),
                low_shape(rows, columns),
                low_shape(rows, columns),
                low_shape(rows, mixed_columns),
                low_shape(rows, mixed_columns),
                low_shape(rows, width),
                full_shape(rows, width),
                full_shape(8, width),
                full_shape(8, width),
                full_shape(8, inner),
            ],
            back_scratch
            + [
                vm(rows, width),
                vm(rows, inner),
                vm(rows, width, kind=f32),
                vm(2, rows, mixed_columns),
                vm(rows, width),
                vm(rows, width, kind=f32),
                vm(rows, width, kind=f32),
                vm(width, 3 * width),
                vm(inner, width),
                vm(width, inner),
                dma((2, inner // width)),
                dma((24,)),
            ],
            2 * rows * width * (3 * width + 2 * inner),
            vector_outs=3,
        )

    groups = []
    gate = []

    def start(order, items, gate_arrays, vectors=()):
        arrays, plan, pieces, places = [], [], [], []
        row, vector_row = 0, 0

        def number(array):
            for index, known in enumerate(arrays):
                if known is array:
                    return index
            arrays.append(array)
            return len(arrays) - 1

        for left, left_far, at, at_far, size, right, right_far, r_at, r_at_far, strips, kind in items:
            left, left_far, right, right_far = map(number, (left, left_far, right, right_far))
            plan.append(
                (left, left_far, at, at_far, size, right, right_far, r_at, r_at_far, strips, row)
            )
            pieces.append((row, size // chips // 2, strips))
            places.append((size // chips // 2, kind[0], kind[1], strips))
            row += strips * size // chips
        if vectors:
            vector_row = row
            pieces.append((row, 16, 0))
            places.append((16, vectors[2]))
            row += 16
        depth = sum(item[9] * item[4] for item in plan)
        kept, sent = call(
            functools.partial(weight_kernel, chips, order, tuple(plan), vector_row),
            (low_shape(chips // 2, row, columns),) * 2,
            [ANY] + [VMEM] * len(vectors[:2]) + [ANY] * len(arrays),
            [vm(2, rows, item[4]) for item in plan]
            + [vm(2, rows, item[9] * columns) for item in plan]
            + [
                vm(768, 2 * rows),
                vm(chips, row, columns),
                dma((len(plan), chips)),
                dma((len(plan), 2, max(item[4] for item in plan) // 768)),
                dma((len(plan), 2)),
            ],
            after(code, *gate_arrays),
            *vectors[:2],
            *arrays,
            flops=4 * rows * columns * depth,
        )
        groups.append((Halving(kept, sent, chips, order), row, pieces, places))
        return kept

    def step(*which):
        return [
            groups[index][0].next() if index >= 0 else groups[~index][0].parts[-1]
            for index in which
            if max(index, ~index) < len(groups) and (index < 0 or groups[index][0].slots > 1)
        ]

    orders = [{"z": (0, 2, 1), "r": (0, 1, 2)}[letter] for letter in plan["orders"]]

    def down_item(layer, up_kept, up_far, at_far):
        hidden, hidden_far = saved[layer][5], saved[layer][10]
        return (hidden, hidden_far, 0, 0, inner, up_kept, up_far, 0, at_far, 1, (3, layer))

    def up_items(layer, kept, far):
        acts, acts_far = saved[layer][4], saved[layer][9]
        return [
            (acts, acts_far, width, width, width, kept, far, 0, 0, strips_up, (2, layer)),
            (acts, acts_far, 0, 0, width, kept, far, inner // 2, inner // 2, 1, (1, layer)),
        ]

    def joint_item(layer, kept, far):
        packed, packed_far = saved[layer][2], saved[layer][3]
        at = 2 * width
        return (packed, packed_far, at, at, width, kept, far, 0, 0, strips_joint, (0, layer))

    preact_far = swap_cores(preact_sent)
    dq, own, sent, dq_sum = attention_back(last, low, [])
    received = swap_cores(sent)
    joints = []
    loose = []
    if native:
        items = [down_item(last, up_kept, saved[0][3], 3 * width)]
        if plan["first"]:
            gate = [start(orders[0], items + up_items(last, preact_kept, preact_far), [dq])]
        else:
            gate = [start(orders[0], items, [dq])]
            gate = [start(orders[1], up_items(last, preact_kept, preact_far), gate)]
        gate += step(*plan["F2"])
    else:
        up_far = saved[0][3][:, 3 * width :]
        loose.append((last, up_kept, up_far, preact_kept, preact_far))
    for above in reversed(range(1, layers)):
        layer = above - 1
        got = between(above, dq, own, received, dq_sum, vectors_two, middle_grad, gate)
        mix_kept, mix_sent, up_kept, up_sent, preact_kept, preact_sent, low, middle_grad = got[:8]
        vectors_one, vectors_two, up_sum_next = got[8:]
        mix_far, up_far = swap_cores(mix_sent), swap_cores(up_sent)
        preact_far = swap_cores(preact_sent)
        gate = [low]
        if native:
            items = [joint_item(above, mix_kept, mix_far), down_item(layer, up_kept, up_far, 0)]
            gate += step(*plan["jd"])
            gate = [start(orders[-3], items, gate, (vectors_one, up_sum, above))]
            gate += step(*plan["u0"])
            gate = [start(orders[-2], up_items(layer, preact_kept, preact_far), gate)]
            gate += step(*plan["B1b"])
        else:
            joints.append((above, mix_kept, mix_far, vectors_one, up_sum))
            loose.append((layer, up_kept, up_far, preact_kept, preact_far))
        up_sum = up_sum_next
        dq, own, sent, dq_sum = attention_back(layer, low, gate)
        received = swap_cores(sent)
        gate = [dq] + step(*plan["B2"])
    got = project_back(0, dq, own, received, dq_sum, vectors_two, middle_grad, gate)
    mix_kept, mix_sent, input_gradient, vectors_one = got
    mix_far = swap_cores(mix_sent)
    if native:
        gate = [input_gradient] + step(*plan["j0"])
        kept = start(
            orders[-1], [joint_item(0, mix_kept, mix_far)], gate, (vectors_one, up_sum, 0)
        )
        tail = kept
        for index in plan["tail"]:
            if index < 0:
                tail = after(groups[~index][0].parts[-1], tail)
            elif groups[index][0].slots > 1:
                tail = groups[index][0].next(tail)
    else:
        joints.append((0, mix_kept, mix_far, vectors_one, up_sum))
        return plain_outputs(
            output, input_gradient, saved, loose, joints, chips, core, layers, width, inner
        )

    half = part // 2
    outs = [
        full_shape(layers, half, 3 * width),
        full_shape(layers, half, width),
        full_shape(layers, half, inner),
        full_shape(layers, inner // chips // 2, width),
        full_shape(layers, half),
        full_shape(layers, half),
        full_shape(layers, 2, half),
        full_shape(layers, half),
        full_shape(layers, half),
        full_shape(layers, half),
        full_shape(layers, half),
        full_shape(layers, inner // chips // 2),
    ]

    def finish(some, gate_arrays):
        parts, pieces, places, group_rows, base = [], [], [], [], 0
        for halving, count, group_pieces, group_places in some:
            parts += halving.rest().parts
            pieces.append(tuple(group_pieces))
            group_rows.append(count)
            for place in group_places:
                if len(place) == 4:
                    size, index, layer, strips = place
                    places.append((base, size, index, layer, strips))
                    base += size * strips
                else:
                    places.append((base, 8, place[1]))
                    base += 16
        steps = len(parts) // len(some)
        if gate_arrays:
            parts[0] = after(parts[0], *gate_arrays)
        kept, sent = call(
            functools.partial(sum_kernel, pieces),
            (full_shape(base, columns),) * 2,
            [ANY] * len(parts),
            [vm(steps, count, columns) for count in group_rows]
            + [
                vm(max(group_rows), columns, kind=f32),
                vm(base, columns, kind=f32),
                vm(base, columns, kind=f32),
                dma((len(parts) + 2,)),
            ],
            *parts,
        )
        return kept, swap_cores(sent), places

    split = plan["done"]
    done = [
        finish(some, (tail,) if plan["tail"] else ())
        for some in (groups[:split], groups[split:])
        if some
    ]
    final = call(
        functools.partial(place_kernel, [places for _, _, places in done]),
        outs,
        [ANY] * (2 * len(done)),
        [vm(*array.shape, kind=f32) for kept, far, _ in done for array in (kept, far)]
        + [dma((2 * len(done),))],
        *[array for kept, far, _ in done for array in (kept, far)],
        out_specs=(VMEM,) * len(outs),
    )
    joints, outputs, ups, downs, gain_one, shift_one, biases = final[:7]
    bias_out, gain_two, shift_two, bias_down, bias_up = final[7:]
    return (
        output[None],
        input_gradient[None],
        gain_one,
        shift_one,
        joints,
        biases,
        outputs,
        bias_out,
        gain_two,
        shift_two,
        ups,
        bias_up,
        downs,
        bias_down,
    )


def plain_outputs(
    output, input_gradient, saved, loose, joints, chips, core, layers, width, inner
):
    slots = slots_of_chips(chips, lax.axis_index("row").astype(jnp.int32), core)
    split = functools.partial(plain_sums, slots=slots, chips=chips, core=core)
    mats, vecs = [[None] * 4 for _ in range(layers)], [None] * layers
    for layer, up_kept, up_far, preact_kept, preact_far in loose:
        acts, hidden, acts_far, hidden_far = (saved[layer][index] for index in (4, 5, 9, 10))
        cut = inner // 2
        mats[layer][1] = split(
            acts[:, :width], acts_far[:, :width], preact_kept[:, cut:], preact_far[:, cut:]
        )
        mats[layer][2] = split(
            acts[:, width:], acts_far[:, width:], preact_kept[:, :cut], preact_far[:, :cut]
        )
        mats[layer][3] = split(hidden, hidden_far, up_kept, up_far)
    for layer, mix_kept, mix_far, vectors, up_sum in joints:
        packed, packed_far = saved[layer][2:4]
        window = slice(2 * width, 3 * width)
        mats[layer][0] = split(packed[:, window], packed_far[:, window], mix_kept, mix_far)
        vecs[layer] = [vectors[row] for row in range(8)] + [up_sum[0]]
    cuts = plain_vectors(
        [vector for layer in range(layers) for vector in vecs[layer]], slots, chips, core
    )

    def stacked(position):
        return jnp.stack([cuts[layer * 9 + position] for layer in range(layers)])

    def matrix(position):
        return jnp.stack([mats[layer][position] for layer in range(layers)])

    return (
        output[None],
        input_gradient[None],
        stacked(0),
        stacked(1),
        matrix(0),
        jnp.stack([stacked(2), stacked(3)], axis=1),
        matrix(1),
        stacked(4),
        stacked(5),
        stacked(6),
        matrix(2),
        stacked(8),
        matrix(3),
        stacked(7),
    )


def solution(mesh):
    chips = mesh.shape["row"]
    split = P("row", "tok", None)
    in_specs = (split, split, P("row", "tok"), P("row", "tok")) + (P(),) * 12
    vector = P(None, ("row", "tok"))
    table = P(None, ("row", "tok"), None)
    out_specs = (
        split,
        split,
        vector,
        vector,
        table,
        P(None, None, ("row", "tok")),
        table,
        vector,
        vector,
        vector,
        table,
        vector,
        table,
        vector,
    )

    def run(*arrays):
        return body(*arrays, chips=chips)

    return jax.shard_map(run, mesh=mesh, in_specs=in_specs, out_specs=out_specs, check_vma=False)
```
